256 devices in a mesh: dom: 64 (over z, y, x_hi), rep: 4 (over x_lo, core).
Axes of the slice: x: 4 (x_hi: 2, x_lo: 2; x = x_hi * 2 + x_lo), y: 4, z: 8, core: 2. Of those that a mesh axis runs over, the one named last changes fastest.
Arguments:
- features: bfloat16 [4, 16384, 1024], P('rep', 'dom'), may hold values from -60 to 60
- block_mask: int32 [4, 64, 2, 2], P('rep', 'dom'), may hold values 0 or 1
- expander_perm: int32 [4, 64, 4, 256], P('rep', 'dom'), may hold values from 0 to 255, each once within a row
- cotangent: bfloat16 [4, 16384, 1024], P('rep', 'dom'), may hold values from -6 to 6
- w_query: bfloat16 [1024, 512], replicated, may hold values from -0.1875 to 0.1875
- w_key: bfloat16 [1024, 512], replicated, may hold values from -0.1875 to 0.1875
- w_value: bfloat16 [1024, 512], replicated, may hold values from -0.1875 to 0.1875
- w_out: bfloat16 [512, 1024], replicated, may hold values from -0.25 to 0.25
Outputs:
- feature_grad: bfloat16 [4, 16384, 1024], P('rep', 'dom')
- proj_grads: bfloat16 [3, 1024, 512], P(None, 'dom')
- out_grad: bfloat16 [512, 1024], P('dom')
The draws below stay inside these ranges and needn't reach their ends.
All inputs are finite; a program needn't handle non-finite values. No bound on the sum of `block_mask` on one device may be relied on, other than what follows from the above.
Results may differ from the reference program's by a relative error of at most 0.0095.
The reference program's roundings to bfloat16 on the way count: a program that leaves them out, or rounds other values in their place, can miss the bound.
Values may be sent and summed in bfloat16 or wider, within the bound.
No kernel may reach another device: no remote copies, remote signals or barrier semaphores. Data moves between devices by JAX's collectives and lax.ppermute only.
A program may use at most 128 MiB of HBM per device.

```python
import jax
import jax.numpy as jnp
from jax import lax

D = 1024
HEADS = 8
HEAD_DIM = 64
EXPANDERS = 4
BLK_DEV = 2
HD = 512
NODES_DEV = 256
DOMAINS = 64
NODES = 16384
GRAPHS = 4


def draw_features(key, part):
    base = jax.random.normal(key, (GRAPHS, NODES, D), jnp.float32)
    parts_count = NODES // NODES_DEV
    owner = jnp.arange(NODES) // NODES_DEV
    column = jnp.arange(D) // (D // parts_count)
    paired = (owner * 37 + 5) % parts_count
    spike = jnp.where(column[None, :] == paired[:, None], 3.0, 1.0)
    values = base * spike[None]
    return jnp.clip(values, -60.0, 60.0).astype(jnp.bfloat16)


def place_ends(array, stream_key, least, top_value):
    longest = array.shape.index(max(array.shape))
    spots = []
    for shift in (0, 1):
        where = [jax.random.randint(jax.random.fold_in(stream_key, axis), (), 0, length) for axis, length in enumerate(array.shape)]
        where[longest] = (where[longest] + shift) % array.shape[longest]
        spots.append(tuple(where))
    return array.at[spots[0]].set(least).at[spots[1]].set(top_value)


def steps_of(stream_key, shape, cuts, low, high):
    gain = 1.0
    for position, parts in cuts:
        draws = jax.random.uniform(jax.random.fold_in(jax.random.fold_in(stream_key, 6), position), (parts,), jnp.float32, low / len(cuts), high / len(cuts))
        gain = gain * jnp.repeat(jnp.exp(draws), shape[position] // parts).reshape((-1,) + (1,) * (len(shape) - 1 - position))
    return gain


def centred(stream_key, dims, scale, reach, split=(), kind=jnp.bfloat16):
    entries = jax.random.normal(stream_key, dims, jnp.float32) * scale
    if len(split) > 0:
        entries = steps_of(stream_key, dims, split, -0.22, 0.18) * entries
    return jnp.clip(entries, min=-reach, max=reach).astype(kind)


def setup_inputs(seed: int = 0) -> dict:
    key_of = jax.random.split(jax.random.key(seed), 9)
    return {
        "features": draw_features(jax.random.fold_in(key_of[8], 71), 0),
        "block_mask": place_ends((jax.random.randint(key_of[1], (GRAPHS, DOMAINS, BLK_DEV, BLK_DEV), 0, 5) < 2).astype(jnp.int32), jax.random.fold_in(key_of[1], 1), 0, 1),
        "expander_perm": jax.vmap(lambda own: jax.random.permutation(own, NODES_DEV))(jax.random.split(key_of[2], GRAPHS * DOMAINS * EXPANDERS)).reshape((GRAPHS, DOMAINS, EXPANDERS, NODES_DEV)).astype(jnp.int32),
        "cotangent": centred(key_of[3], (GRAPHS, NODES, D), 1.0, 6.0, ((0, 4), (1, 64))),
        "w_query": centred(key_of[4], (D, HD), D ** -0.5, 0.1875),
        "w_key": centred(key_of[5], (D, HD), D ** -0.5, 0.1875),
        "w_value": centred(key_of[6], (D, HD), D ** -0.5, 0.1875),
        "w_out": centred(key_of[7], (HD, D), HD ** -0.5, 0.25),
    }


def attend_grad(query, key, value, far_key, far_value, mask, grad):
    rows = query.shape[0]
    blocks = mask.shape[0]
    size = rows // blocks
    f32 = jnp.float32
    query_h = query.reshape(rows, HEADS, HEAD_DIM)
    key_h = key.reshape(rows, HEADS, HEAD_DIM)
    value_h = value.reshape(rows, HEADS, HEAD_DIM)
    far_kh = far_key.reshape(EXPANDERS, rows, HEADS, HEAD_DIM).astype(f32)
    far_vh = far_value.reshape(EXPANDERS, rows, HEADS, HEAD_DIM).astype(f32)
    grad_h = grad.reshape(rows, HEADS, HEAD_DIM)
    grad_f = grad_h.astype(f32)
    query_f = query_h.astype(f32)
    factor = HEAD_DIM ** (-0.5)
    full = jnp.broadcast_to(mask[:, None, :, None] > 0, (blocks, size, blocks, size)).reshape(rows, rows)
    scores = jnp.einsum('ihd,jhd->hij', query_h, key_h, preferred_element_type=f32) * factor
    scores = jnp.where(full[None], scores, -1e+30)
    far_scores = lax.optimization_barrier(jnp.sum(query_f[None] * far_kh, axis=3)) * factor
    top = jnp.maximum(lax.optimization_barrier(jnp.max(scores, axis=2)), jnp.transpose(lax.optimization_barrier(jnp.max(far_scores, axis=0))))
    weights = jnp.exp(scores - top[:, :, None])
    far_weights = jnp.exp(far_scores - jnp.transpose(top)[None])
    total = lax.optimization_barrier(jnp.sum(weights, axis=2)) + jnp.transpose(lax.optimization_barrier(jnp.sum(far_weights, axis=0)))
    probs = weights / total[:, :, None]
    far_probs = far_weights / jnp.transpose(total)[None]
    probs_b = probs.astype(jnp.bfloat16)
    out = jnp.einsum('hij,jhd->ihd', probs_b, value_h, preferred_element_type=f32)
    out = out + lax.optimization_barrier(jnp.sum(far_probs[..., None] * far_vh, axis=0))
    delta = lax.optimization_barrier(jnp.sum(grad_f * out, axis=2))
    dprob = jnp.einsum('ihd,jhd->hij', grad_h, value_h, preferred_element_type=f32)
    dscore = probs * (dprob - jnp.transpose(delta)[:, :, None])
    dscore_b = dscore.astype(jnp.bfloat16)
    far_dprob = lax.optimization_barrier(jnp.sum(grad_f[None] * far_vh, axis=3))
    far_dscore = far_probs * (far_dprob - delta[None])
    query_g = jnp.einsum('hij,jhd->ihd', dscore_b, key_h, preferred_element_type=f32)
    query_g = (query_g + lax.optimization_barrier(jnp.sum(far_dscore[..., None] * far_kh, axis=0))) * factor
    key_g = jnp.einsum('hij,ihd->jhd', dscore_b, query_h, preferred_element_type=f32) * factor
    value_g = jnp.einsum('hij,ihd->jhd', probs_b, grad_h, preferred_element_type=f32)
    far_key_g = far_dscore[..., None] * query_f[None] * factor
    far_value_g = far_probs[..., None] * grad_f[None]
    width = HEADS * HEAD_DIM
    return (out.astype(jnp.bfloat16).reshape(rows, width), query_g.reshape(rows, width), key_g.reshape(rows, width), value_g.reshape(rows, width), far_key_g.reshape(EXPANDERS, rows, width), far_value_g.reshape(EXPANDERS, rows, width))

def reference(features, block_mask, expander_perm, cotangent, w_query, w_key, w_value, w_out):
    rows = features.reshape(GRAPHS * NODES, D)
    cot = cotangent.reshape(GRAPHS * NODES, D)

    def project(weight):
        return jnp.dot(rows, weight, preferred_element_type=jnp.float32).astype(jnp.bfloat16).reshape(GRAPHS, DOMAINS, NODES_DEV, HD)
    query = project(w_query)
    key = project(w_key)
    value = project(w_value)
    levels = DOMAINS.bit_length() - 1
    index = jnp.arange(DOMAINS, dtype=jnp.int32)
    partners = [jnp.bitwise_xor(index, 1 << m * levels // EXPANDERS) for m in range(EXPANDERS)]
    far_key = jnp.stack([jnp.take_along_axis(key[:, partners[m]], expander_perm[:, :, m, :, None], axis=2) for m in range(EXPANDERS)], axis=2)
    far_value = jnp.stack([jnp.take_along_axis(value[:, partners[m]], expander_perm[:, :, m, :, None], axis=2) for m in range(EXPANDERS)], axis=2)
    attn_grad = jnp.dot(cot, jnp.transpose(w_out), preferred_element_type=jnp.float32).astype(jnp.bfloat16)
    flat = GRAPHS * DOMAINS

    def local(items):
        q_d, k_d, v_d, fk_d, fv_d, mask_d, grad_d, perm_d = items
        out, q_g, k_g, v_g, fk_g, fv_g = attend_grad(q_d, k_d, v_d, fk_d, fv_d, mask_d, grad_d)
        empty = jnp.zeros((NODES_DEV, HD), jnp.float32)
        sent_k = jnp.stack([empty.at[perm_d[m]].set(fk_g[m]) for m in range(EXPANDERS)]).astype(jnp.bfloat16)
        sent_v = jnp.stack([empty.at[perm_d[m]].set(fv_g[m]) for m in range(EXPANDERS)]).astype(jnp.bfloat16)
        return (out, q_g, k_g, v_g, sent_k, sent_v)
    items = (query.reshape(flat, NODES_DEV, HD), key.reshape(flat, NODES_DEV, HD), value.reshape(flat, NODES_DEV, HD), far_key.reshape(flat, EXPANDERS, NODES_DEV, HD), far_value.reshape(flat, EXPANDERS, NODES_DEV, HD), block_mask.reshape(flat, BLK_DEV, BLK_DEV), attn_grad.reshape(flat, NODES_DEV, HD), expander_perm.reshape(flat, EXPANDERS, NODES_DEV))
    attn, q_g, k_g, v_g, sent_k, sent_v = lax.map(local, items)
    sent_k = sent_k.reshape(GRAPHS, DOMAINS, EXPANDERS, NODES_DEV, HD)
    sent_v = sent_v.reshape(GRAPHS, DOMAINS, EXPANDERS, NODES_DEV, HD)
    k_sum = k_g.reshape(GRAPHS, DOMAINS, NODES_DEV, HD)
    v_sum = v_g.reshape(GRAPHS, DOMAINS, NODES_DEV, HD)
    for m in range(EXPANDERS):
        k_sum = k_sum + sent_k[:, partners[m], m].astype(jnp.float32)
        v_sum = v_sum + sent_v[:, partners[m], m].astype(jnp.float32)
    query_d = q_g.astype(jnp.bfloat16).reshape(GRAPHS * NODES, HD)
    key_d = k_sum.astype(jnp.bfloat16).reshape(GRAPHS * NODES, HD)
    value_d = v_sum.astype(jnp.bfloat16).reshape(GRAPHS * NODES, HD)
    feature_grad = jnp.dot(query_d, jnp.transpose(w_query), preferred_element_type=jnp.float32)
    feature_grad = feature_grad + jnp.dot(key_d, jnp.transpose(w_key), preferred_element_type=jnp.float32)
    feature_grad = feature_grad + jnp.dot(value_d, jnp.transpose(w_value), preferred_element_type=jnp.float32)
    feature_grad = feature_grad.astype(jnp.bfloat16).reshape(GRAPHS, NODES, D)
    factor = (GRAPHS * NODES) ** (-0.5)
    rows_t = jnp.transpose(rows)
    grad_q = jnp.dot(rows_t, query_d, preferred_element_type=jnp.float32) * factor
    grad_k = jnp.dot(rows_t, key_d, preferred_element_type=jnp.float32) * factor
    grad_v = jnp.dot(rows_t, value_d, preferred_element_type=jnp.float32) * factor
    attn_rows = jnp.transpose(attn.reshape(GRAPHS * NODES, HD))
    grad_o = jnp.dot(attn_rows, cot, preferred_element_type=jnp.float32) * factor
    return (feature_grad, jnp.stack([grad_q, grad_k, grad_v]).astype(jnp.bfloat16), grad_o.astype(jnp.bfloat16))
```

```python
import functools

import jax
import jax.numpy as jnp
from jax import lax
from jax.experimental import pallas as pl
from jax.experimental.pallas import tpu as pltpu
from jax.sharding import Mesh, PartitionSpec as P

HEADS = 8
HEAD_DIM = 64
EXPANDERS = 4
DOM = ("z", "y", "xh")
REP = ("xl", "core")
PLANE = ("y", "xh", "xl")
F32 = jnp.float32
BF16 = jnp.bfloat16


def swap(value, axes, bit):
    count = 1
    for axis in axes:
        count *= lax.axis_size(axis)
    return lax.ppermute(value, axes, [(i, i ^ 1 << bit) for i in range(count)])


def attend_grad(query, key, value, far_key, far_value, mask, grad):
    rows = query.shape[0]
    blocks = mask.shape[0]
    size = rows // blocks
    f32 = jnp.float32
    query_h = query.reshape(rows, HEADS, HEAD_DIM)
    key_h = key.reshape(rows, HEADS, HEAD_DIM)
    value_h = value.reshape(rows, HEADS, HEAD_DIM)
    far_kh = far_key.reshape(EXPANDERS, rows, HEADS, HEAD_DIM).astype(f32)
    far_vh = far_value.reshape(EXPANDERS, rows, HEADS, HEAD_DIM).astype(f32)
    grad_h = grad.reshape(rows, HEADS, HEAD_DIM)
    grad_f = grad_h.astype(f32)
    query_f = query_h.astype(f32)
    factor = HEAD_DIM ** (-0.5)
    full = jnp.broadcast_to(mask[:, None, :, None] > 0, (blocks, size, blocks, size)).reshape(
        rows, rows
    )
    scores = jnp.einsum("ihd,jhd->hij", query_h, key_h, preferred_element_type=f32) * factor
    scores = jnp.where(full[None], scores, -1e30)
    far_scores = jnp.sum(query_f[None] * far_kh, axis=3) * factor
    top = jnp.maximum(jnp.max(scores, axis=2), jnp.transpose(jnp.max(far_scores, axis=0)))
    weights = jnp.exp(scores - top[:, :, None])
    far_weights = jnp.exp(far_scores - jnp.transpose(top)[None])
    total = jnp.sum(weights, axis=2) + jnp.transpose(jnp.sum(far_weights, axis=0))
    probs = weights / total[:, :, None]
    far_probs = far_weights / jnp.transpose(total)[None]
    probs_b = probs.astype(jnp.bfloat16)
    out = jnp.einsum("hij,jhd->ihd", probs_b, value_h, preferred_element_type=f32)
    out = out + jnp.sum(far_probs[..., None] * far_vh, axis=0)
    delta = jnp.sum(grad_f * out, axis=2)
    dprob = jnp.einsum("ihd,jhd->hij", grad_h, value_h, preferred_element_type=f32)
    dscore = probs * (dprob - jnp.transpose(delta)[:, :, None])
    dscore_b = dscore.astype(jnp.bfloat16)
    far_dprob = jnp.sum(grad_f[None] * far_vh, axis=3)
    far_dscore = far_probs * (far_dprob - delta[None])
    query_g = jnp.einsum("hij,jhd->ihd", dscore_b, key_h, preferred_element_type=f32)
    query_g = (query_g + jnp.sum(far_dscore[..., None] * far_kh, axis=0)) * factor
    key_g = jnp.einsum("hij,ihd->jhd", dscore_b, query_h, preferred_element_type=f32) * factor
    value_g = jnp.einsum("hij,ihd->jhd", probs_b, grad_h, preferred_element_type=f32)
    far_key_g = far_dscore[..., None] * query_f[None] * factor
    far_value_g = far_probs[..., None] * grad_f[None]
    width = HEADS * HEAD_DIM
    return (
        out.astype(jnp.bfloat16).reshape(rows, width),
        query_g.reshape(rows, width),
        key_g.reshape(rows, width),
        value_g.reshape(rows, width),
        far_key_g.reshape(EXPANDERS, rows, width),
        far_value_g.reshape(EXPANDERS, rows, width),
    )


def terms_kernel(sizes, feat, feat2, qkv, qkv2, attn, attn2, cot, cot2, out):
    nz, ny, nx, nl = sizes
    tn = (((0,), (0,)), ((), ()))
    wide = functools.partial(lax.dot_general, dimension_numbers=tn, preferred_element_type=F32)
    for part in range(3):
        cols = pl.ds(part * 256, 256)
        prod = wide(feat[...], qkv[:, cols]) + wide(feat2[...], qkv2[:, cols])
        for y in range(ny):
            for x in range(nx):
                for z in range(nz):
                    row = ((z * ny + y) * nx + x) * 16
                    for low in range(nl):
                        out[(y * nx + x) * nl + low, pl.ds(z * 64 + part * 16, 16), :] = prod[
                            row : row + 16, low * 128 : low * 128 + 128
                        ].astype(BF16)
    prod = wide(attn[...], cot[...]) + wide(attn2[...], cot2[...])
    for y in range(ny):
        for x in range(nx):
            for z in range(nz):
                row = ((z * ny + y) * nx + x) * 8
                for low in range(nl):
                    piece = prod[row : row + 8, low * 256 : low * 256 + 256]
                    both = jnp.concatenate([piece[:, :128], piece[:, 128:]], axis=0)
                    out[(y * nx + x) * nl + low, pl.ds(z * 64 + 48, 16), :] = both.astype(BF16)


def weight_terms(feat, feat2, qkv, qkv2, attn, attn2, cot, cot2):
    sizes = tuple(lax.axis_size(a) for a in ("z", "y", "xh", "xl"))
    nz, ny, nx, nl = sizes
    return pl.pallas_call(
        functools.partial(terms_kernel, sizes),
        out_shape=jax.ShapeDtypeStruct((ny * nx * nl, nz * 64, 128), BF16),
        in_specs=[pl.BlockSpec(memory_space=pltpu.VMEM)] * 8,
        out_specs=pl.BlockSpec(memory_space=pltpu.VMEM),
        compiler_params=pltpu.CompilerParams(vmem_limit_bytes=48 << 20),
        cost_estimate=pl.CostEstimate(
            flops=4 * 2 * 512 * 1024 * 256, bytes_accessed=6 << 20, transcendentals=0
        ),
        name="weight_terms",
    )(feat, feat2, qkv, qkv2, attn, attn2, cot, cot2)


def half(value, index):
    size = value.shape[1] // 2
    return lax.dynamic_slice_in_dim(value, index * size, size, axis=1)


def shards(features, block_mask, expander_perm, cotangent, w_query, w_key, w_value, w_out):
    rows = features[0]
    cot = cotangent[0]
    mask = block_mask[0, 0]
    perms = expander_perm[0, 0]
    count = rows.shape[0]
    width = w_query.shape[1]
    core = lax.axis_index("core")
    query = jnp.dot(rows, w_query, preferred_element_type=jnp.float32).astype(jnp.bfloat16)
    key = jnp.dot(rows, w_key, preferred_element_type=jnp.float32).astype(jnp.bfloat16)
    value = jnp.dot(rows, w_value, preferred_element_type=jnp.float32).astype(jnp.bfloat16)
    domains = 1
    for axis in DOM:
        domains *= lax.axis_size(axis)
    levels = domains.bit_length() - 1
    bits = [m * levels // EXPANDERS for m in range(EXPANDERS)]
    both = jnp.concatenate([key, value], axis=1)
    far = [swap(both, DOM, bits[m]) for m in range(EXPANDERS)]
    rows2 = swap(rows, ("core",), 0)
    cot2 = swap(half(cot, 1 - core), ("core",), 0)
    far = [jnp.take(far[m], perms[m], axis=0) for m in range(EXPANDERS)]
    far_key = jnp.stack([f[:, :width] for f in far])
    far_value = jnp.stack([f[:, width:] for f in far])
    attn_grad = jnp.dot(cot, jnp.transpose(w_out), preferred_element_type=jnp.float32).astype(
        jnp.bfloat16
    )
    attn, q_g, k_sum, v_sum, fk_g, fv_g = attend_grad(
        query, key, value, far_key, far_value, mask, attn_grad
    )
    spots = jnp.arange(count, dtype=perms.dtype)
    for m in range(EXPANDERS):
        place = (perms[m][None, :] == spots[:, None]).astype(BF16)
        sent = jnp.concatenate([fk_g[m], fv_g[m]], axis=1).astype(BF16)
        sent = jnp.dot(place, sent, preferred_element_type=F32).astype(BF16)
        back = swap(sent, DOM, bits[m])
        k_sum = k_sum + back[:, :width].astype(jnp.float32)
        v_sum = v_sum + back[:, width:].astype(jnp.float32)
    query_d = q_g.astype(jnp.bfloat16)
    key_d = k_sum.astype(jnp.bfloat16)
    value_d = v_sum.astype(jnp.bfloat16)
    feature_grad = jnp.dot(query_d, jnp.transpose(w_query), preferred_element_type=jnp.float32)
    feature_grad = feature_grad + jnp.dot(
        key_d, jnp.transpose(w_key), preferred_element_type=jnp.float32
    )
    feature_grad = feature_grad + jnp.dot(
        value_d, jnp.transpose(w_value), preferred_element_type=jnp.float32
    )
    feature_grad = feature_grad.astype(jnp.bfloat16)
    mine = jnp.concatenate([half(x, core) for x in (query_d, key_d, value_d)], axis=1)
    theirs = jnp.concatenate([half(x, 1 - core) for x in (query_d, key_d, value_d)], axis=1)
    mate = swap(theirs, ("core",), 0)
    attn2 = swap(attn, ("core",), 0)
    terms = weight_terms(rows, rows2, mine, mate, attn, attn2, half(cot, core), cot2)
    got = lax.all_to_all(terms, PLANE, 0, 0, tiled=True)
    planes = lax.axis_size("z")
    part = jnp.sum(got.astype(F32), axis=0).astype(BF16).reshape(planes, 64, 128)
    got = lax.all_to_all(part, "z", 0, 0, tiled=True)
    graphs = lax.axis_size("xl") * lax.axis_size("core")
    factor = (graphs * domains * count) ** (-0.5)
    share = (jnp.sum(got.astype(F32), axis=0) * factor).astype(BF16)
    whole = lax.all_gather(share, REP, axis=0, tiled=False)
    whole = whole.reshape(lax.axis_size("xl"), lax.axis_size("core"), 64, 128)
    proj = whole[:, :, :48].reshape(2, 2, 3, 16, 128)
    proj_grads = jnp.transpose(proj, (2, 3, 1, 0, 4)).reshape(3, 16, width)
    outs = whole[:, :, 48:].reshape(2, 2, 2, 8, 128)
    out_grad = jnp.transpose(outs, (3, 1, 0, 2, 4)).reshape(8, 2 * width)
    return (feature_grad[None], proj_grads, out_grad)


def solution(mesh):
    fine = Mesh(mesh.devices.reshape(8, 4, 2, 2, 2), DOM + REP)
    placed = (
        P(REP, DOM, None),
        P(REP, DOM, None, None),
        P(REP, DOM, None, None),
        P(REP, DOM, None),
        P(),
        P(),
        P(),
        P(),
    )
    return jax.shard_map(
        shards,
        mesh=fine,
        in_specs=placed,
        out_specs=(P(REP, DOM, None), P(None, DOM, None), P(DOM, None)),
        check_vma=False,
    )
```

```python
import functools

import jax
import jax.numpy as jnp
from jax import lax
from jax.experimental import pallas as pl
from jax.experimental.pallas import tpu as pltpu
from jax.sharding import Mesh, PartitionSpec as P

HEADS = 8
HEAD_DIM = 64
EXPANDERS = 4
NODES = 256
WIDTH = 512
MODEL = 1024
DOM = ("z", "y", "xh")
REP = ("xl", "core")
PLANE = ("y", "xh", "xl")
LINE = ("z", "xl", "core")
SIZES = (8, 4, 2, 2, 2)
F32 = jnp.float32
BF16 = jnp.bfloat16
SCALE = HEAD_DIM ** (-0.5)
VMEM = pl.BlockSpec(memory_space=pltpu.VMEM)
SMEM = pl.BlockSpec(memory_space=pltpu.SMEM)


def dot(a, b):
    return jnp.dot(a, b, preferred_element_type=F32)


def dot_nt(a, b):
    return lax.dot_general(a, b, (((1,), (1,)), ((), ())), preferred_element_type=F32)


def call(body, name, outs, specs, args, flops, scratch=(), moved=2 << 20):
    return pl.pallas_call(
        body,
        out_shape=outs,
        in_specs=specs,
        out_specs=jax.tree.map(lambda _: VMEM, outs),
        scratch_shapes=scratch,
        compiler_params=pltpu.CompilerParams(vmem_limit_bytes=40 << 20),
        cost_estimate=pl.CostEstimate(flops=flops, bytes_accessed=moved, transcendentals=0),
        name=name,
    )(*args)


def shape(*dims, dtype=BF16):
    return jax.ShapeDtypeStruct(dims, dtype)


def swap(value, axes, bit):
    count = 1
    for axis in axes:
        count *= lax.axis_size(axis)
    return lax.ppermute(value, axes, [(i, i ^ 1 << bit) for i in range(count)])


def key_value_kernel(feat, wk, wv, kv, kv_t):
    for part, weight in enumerate((wk, wv)):
        span = pl.ds(part * WIDTH, WIDTH)
        got = dot(feat[...], weight[...]).astype(BF16)
        kv[:, span] = got
        kv_t[span, :] = got.T


def query_grad_kernel(feat, wq, cot, wo, qa_t, feat_t):
    qa_t[pl.ds(0, WIDTH), :] = dot(feat[...], wq[...]).astype(BF16).T
    qa_t[pl.ds(WIDTH, WIDTH), :] = dot_nt(cot[...], wo[...]).astype(BF16).T
    feat_t[...] = feat[...].T


def one_hot(row):
    spots = lax.broadcasted_iota(jnp.int32, (NODES, NODES), 0)
    return jnp.where(spots == row, 1.0, 0.0).astype(BF16)


def attend_kernel(
    core, mask, perms, kv, kv_t, qa_t, r0, r1, r2, r3,
    attn_t, query_t, mate, local_t, d0, d1, d2, d3, far,
):
    far_in = (r0, r1, r2, r3)
    far_out = (d0, d1, d2, d3)
    for m in range(EXPANDERS):
        far[m] = dot(far_in[m][...], one_hot(perms[m : m + 1, :])).astype(BF16)
        far_out[m][pl.ds(16, 8), :] = jnp.broadcast_to(perms[m : m + 1, :].astype(F32), (8, NODES))
    half = NODES // 2
    row_head = lax.broadcasted_iota(jnp.int32, (2 * HEAD_DIM, NODES), 0) // HEAD_DIM
    for head in range(HEADS):
        pair = pl.ds(head // 2 * 128, 128)
        pair_v = pl.ds(WIDTH + head // 2 * 128, 128)
        here = pl.ds(head * HEAD_DIM, HEAD_DIM)
        here_v = pl.ds(WIDTH + head * HEAD_DIM, HEAD_DIM)
        mine = row_head == head % 2
        zero = jnp.zeros((), BF16)
        query_h = qa_t[here, :]
        grad_h = qa_t[here_v, :]
        query_f = query_h.astype(F32)
        grad_f = grad_h.astype(F32)
        scores = dot(kv[:, pair], jnp.where(mine, qa_t[pair, :], zero)) * SCALE
        parts = []
        for source in range(2):
            row = scores[source * half : (source + 1) * half]
            keep = [
                jnp.where(mask[to, source] > 0, row[:, to * half : (to + 1) * half], -1e30)
                for to in range(2)
            ]
            parts.append(jnp.concatenate(keep, axis=1))
        scores = jnp.concatenate(parts, axis=0)
        far_s, far_dp = [], []
        for m in range(EXPANDERS):
            far_k = far[m, here, :].astype(F32)
            far_v = far[m, here_v, :].astype(F32)
            far_s.append(jnp.sum(query_f * far_k, axis=0, keepdims=True) * SCALE)
            far_dp.append(jnp.sum(grad_f * far_v, axis=0, keepdims=True))
        top = jnp.max(scores, axis=0, keepdims=True)
        for s in far_s:
            top = jnp.maximum(top, s)
        weights = jnp.exp(scores - top)
        far_w = [jnp.exp(s - top) for s in far_s]
        total = jnp.sum(weights, axis=0, keepdims=True) + (far_w[0] + far_w[1] + far_w[2] + far_w[3])
        inverse = 1.0 / total
        probs = weights * inverse
        far_p = [w * inverse for w in far_w]
        probs_b = probs.astype(BF16)
        out = dot(kv_t[here_v, :], probs_b)
        for m in range(EXPANDERS):
            out = out + far_p[m] * far[m, here_v, :].astype(F32)
        delta = jnp.sum(grad_f * out, axis=0, keepdims=True)
        out_b = out.astype(BF16)
        attn_t[here, :] = out_b
        dprob = dot(kv[:, pair_v], jnp.where(mine, qa_t[pair_v, :], zero))
        dscore_b = (probs * (dprob - delta)).astype(BF16)
        query_g = dot(kv_t[here, :], dscore_b)
        for m in range(EXPANDERS):
            dfar = far_p[m] * (far_dp[m] - delta)
            query_g = query_g + dfar * far[m, here, :].astype(F32)
            far_out[m][head : head + 1, :] = dfar * SCALE
            far_out[m][8 + head : 9 + head, :] = far_p[m]
        query_t[here, :] = (query_g * SCALE).astype(BF16)
        local_t[here, :] = dot_nt(query_h, dscore_b) * SCALE
        local_t[here_v, :] = dot_nt(grad_h, probs_b)
    mate[pl.ds(0, 256), :] = query_t[pl.ds(pl.multiple_of((1 - core[0]) * 256, 256), 256), :]
    mate[pl.ds(256, WIDTH), :] = attn_t[...]


def owner_kernel(core, local_t, d0, d1, d2, d3, q0, q1, q2, q3, grads_t, mate):
    numbers = (d0, d1, d2, d3)
    sent = (q0, q1, q2, q3)
    total = local_t[...]
    for m in range(EXPANDERS):
        place = one_hot(numbers[m][16:17, :].astype(jnp.int32))
        rows = []
        for part in range(2 * HEADS):
            rows.append(
                (
                    sent[m][pl.ds(part * HEAD_DIM, HEAD_DIM), :].astype(F32)
                    * numbers[m][part : part + 1, :]
                ).astype(BF16)
            )
        total = total + dot_nt(jnp.concatenate(rows, axis=0), place)
    grads_t[...] = total.astype(BF16)
    other = (1 - core[0]) * 256
    mate[pl.ds(0, 256), :] = grads_t[pl.ds(pl.multiple_of(other, 256), 256), :]
    mate[pl.ds(256, 256), :] = grads_t[pl.ds(pl.multiple_of(WIDTH + other, 256), 256), :]


def put_proj(out, prod, offset):
    nz, ny, nx, nl, _ = SIZES
    for y in range(ny):
        for x in range(nx):
            for z in range(nz):
                row = ((z * ny + y) * nx + x) * 16
                for low in range(nl):
                    out[(y * nx + x) * nl + low, pl.ds(z * 32 + offset, 16), :] = prod[
                        row : row + 16, low * 128 : low * 128 + 128
                    ].astype(BF16)


def early_terms_kernel(core, feat, feat2, query_t, attn_t, mate, cot, cot2, out):
    nz, ny, nx, nl, _ = SIZES
    mine = pl.ds(pl.multiple_of(core[0] * 256, 256), 256)
    prod = dot_nt(feat[...], query_t[mine, :]) + dot_nt(feat2[...], mate[pl.ds(0, 256), :])
    put_proj(out, prod, 0)
    mine = pl.ds(pl.multiple_of(core[0] * WIDTH, WIDTH), WIDTH)
    prod = dot(attn_t[...], cot[:, mine]) + dot(mate[pl.ds(256, WIDTH), :], cot2[:, mine])
    for y in range(ny):
        for x in range(nx):
            for z in range(nz):
                row = ((z * ny + y) * nx + x) * 8
                for low in range(nl):
                    piece = prod[row : row + 8, low * 256 : low * 256 + 256]
                    both = jnp.concatenate([piece[:, :128], piece[:, 128:]], axis=0)
                    out[(y * nx + x) * nl + low, pl.ds(z * 32 + 16, 16), :] = both.astype(BF16)


def late_terms_kernel(core, feat, feat2, grads_t, mate, out):
    for part in range(2):
        mine = pl.ds(pl.multiple_of(part * WIDTH + core[0] * 256, 256), 256)
        prod = dot_nt(feat[...], grads_t[mine, :])
        prod = prod + dot_nt(feat2[...], mate[pl.ds(part * 256, 256), :])
        put_proj(out, prod, part * 16)


def feature_grad_kernel(query_t, grads_t, wq, wk, wv, out):
    total = dot_nt(query_t[...].T, wq[...])
    total = total + dot_nt(grads_t[pl.ds(0, WIDTH), :].T, wk[...])
    total = total + dot_nt(grads_t[pl.ds(WIDTH, WIDTH), :].T, wv[...])
    out[...] = total.astype(BF16)


def plane_sum_kernel(got, out):
    total = got[0].astype(F32)
    for i in range(1, got.shape[0]):
        total = total + got[i].astype(F32)
    total = total.astype(BF16)
    copies = SIZES[3] * SIZES[4]
    for z in range(SIZES[0]):
        for r in range(copies):
            out[z * copies + r] = total[z * 32 : z * 32 + 32]


def share_kernel(factor, early, late, proj, outs):
    nz, _, _, nl, nc = SIZES
    for low in range(nl):
        for c in range(nc):
            spot = low * nc + c
            first = early[spot].astype(F32)
            second = late[spot].astype(F32)
            for z in range(1, nz):
                first = first + early[z * nl * nc + spot].astype(F32)
                second = second + late[z * nl * nc + spot].astype(F32)
            first = first * factor
            second = second * factor
            cols = pl.ds(c * 256 + low * 128, 128)
            proj[0, :, cols] = first[:16].astype(BF16)
            proj[1, :, cols] = second[:16].astype(BF16)
            proj[2, :, cols] = second[16:].astype(BF16)
            for h in range(2):
                wide = pl.ds(c * WIDTH + low * 256 + h * 128, 128)
                outs[:, wide] = first[16 + 8 * h : 24 + 8 * h].astype(BF16)


def reduce_terms(terms):
    got = lax.all_to_all(terms, PLANE, 0, 0, tiled=True)
    peers = SIZES[0] * SIZES[3] * SIZES[4]
    part = call(plane_sum_kernel, "plane_sum", shape(peers, 32, 128), [VMEM], (got,), 1 << 20)
    return lax.all_to_all(part, LINE, 0, 0, tiled=True)


def shards(features, block_mask, expander_perm, cotangent, w_query, w_key, w_value, w_out):
    feat = features[0]
    cot = cotangent[0]
    mask = block_mask[0, 0]
    perms = expander_perm[0, 0]
    core = lax.axis_index("core").astype(jnp.int32).reshape(1)
    domains = SIZES[0] * SIZES[1] * SIZES[2]
    levels = domains.bit_length() - 1
    bits = [m * levels // EXPANDERS for m in range(EXPANDERS)]
    proj_flops = 2 * 2 * NODES * MODEL * WIDTH
    kv, kv_t = call(
        key_value_kernel, "key_value", (shape(NODES, MODEL), shape(MODEL, NODES)), [VMEM] * 3,
        (feat, w_key, w_value), proj_flops,
    )
    qa_t, feat_t = call(
        query_grad_kernel, "query_grad", (shape(MODEL, NODES), shape(MODEL, NODES)), [VMEM] * 4,
        (feat, w_query, cot, w_out), proj_flops,
    )
    far = [swap(kv_t, DOM, b) for b in bits]
    sent = [swap(qa_t, DOM, b) for b in bits]
    feat2 = swap(feat_t, ("core",), 0)
    cot2 = swap(cot, ("core",), 0)
    attn_t, query_t, mate, local_t, *numbers = call(
        attend_kernel, "attend",
        (shape(WIDTH, NODES), shape(WIDTH, NODES), shape(768, NODES), shape(MODEL, NODES, dtype=F32))
        + (shape(24, NODES, dtype=F32),) * 4,
        [SMEM, SMEM] + [VMEM] * 8,
        (core, mask, perms, kv, kv_t, qa_t, *far), 4 << 30,
        scratch=[pltpu.VMEM((EXPANDERS, MODEL, NODES), BF16)],
    )
    numbers = [swap(x, DOM, b) for x, b in zip(numbers, bits)]
    mate = swap(mate, ("core",), 0)
    early = call(
        early_terms_kernel, "early_terms", shape(16, 256, 128), [SMEM] + [VMEM] * 7,
        (core, feat_t, feat2, query_t, attn_t, mate, cot, cot2), 2 * proj_flops,
    )
    early = reduce_terms(early)
    grads_t, mate = call(
        owner_kernel, "owner", (shape(MODEL, NODES), shape(WIDTH, NODES)), [SMEM] + [VMEM] * 9,
        (core, local_t, *numbers, *sent), 2 << 30,
    )
    mate = swap(mate, ("core",), 0)
    late = call(
        late_terms_kernel, "late_terms", shape(16, 256, 128), [SMEM] + [VMEM] * 4,
        (core, feat_t, feat2, grads_t, mate), 2 * proj_flops,
    )
    late = reduce_terms(late)
    feature_grad = call(
        feature_grad_kernel, "feature_grad", shape(NODES, MODEL), [VMEM] * 5,
        (query_t, grads_t, w_query, w_key, w_value), 2 * proj_flops,
    )
    graphs = SIZES[3] * SIZES[4]
    factor = (graphs * domains * NODES) ** (-0.5)
    proj_grads, out_grad = call(
        functools.partial(share_kernel, factor), "share",
        (shape(3, 16, WIDTH), shape(8, MODEL)), [VMEM] * 2, (early, late), 1 << 20,
    )
    return (feature_grad[None], proj_grads, out_grad)


def solution(mesh):
    fine = Mesh(mesh.devices.reshape(SIZES), DOM + REP)
    placed = (
        P(REP, DOM, None),
        P(REP, DOM, None, None),
        P(REP, DOM, None, None),
        P(REP, DOM, None),
        P(),
        P(),
        P(),
        P(),
    )
    return jax.shard_map(
        shards,
        mesh=fine,
        in_specs=placed,
        out_specs=(P(REP, DOM, None), P(None, DOM, None), P(DOM, None)),
        check_vma=False,
    )
```

```python
import functools

import jax
import jax.numpy as jnp
from jax import lax
from jax.experimental import pallas as pl
from jax.experimental.pallas import tpu as pltpu
from jax.sharding import Mesh, PartitionSpec as P

HEADS = 8
HEAD_DIM = 64
EXPANDERS = 4
NODES = 256
WIDTH = 512
MODEL = 1024
DOM = ("z", "y", "xh")
REP = ("xl", "core")
PLANE = ("y", "xh", "xl")
SIZES = (8, 4, 2, 2, 2)
F32 = jnp.float32
BF16 = jnp.bfloat16
SCALE = HEAD_DIM ** (-0.5)
VMEM = pl.BlockSpec(memory_space=pltpu.VMEM)
SMEM = pl.BlockSpec(memory_space=pltpu.SMEM)


def dot(a, b):
    return jnp.dot(a, b, preferred_element_type=F32)


def dot_nt(a, b):
    return lax.dot_general(a, b, (((1,), (1,)), ((), ())), preferred_element_type=F32)


def call(body, name, outs, specs, args, flops, scratch=(), moved=2 << 20):
    return pl.pallas_call(
        body,
        out_shape=outs,
        in_specs=specs,
        out_specs=jax.tree.map(lambda _: VMEM, outs),
        scratch_shapes=scratch,
        compiler_params=pltpu.CompilerParams(vmem_limit_bytes=16 << 20),
        cost_estimate=pl.CostEstimate(flops=flops if name in ("owner", "attend") else 1024, bytes_accessed=1024, transcendentals=0),
        name=name,
    )(*args)


def shape(*dims, dtype=BF16):
    return jax.ShapeDtypeStruct(dims, dtype)


def swap(value, axes, bit):
    count = 1
    for axis in axes:
        count *= lax.axis_size(axis)
    return lax.ppermute(value, axes, [(i, i ^ 1 << bit) for i in range(count)])


def key_value_kernel(feat, wk, wv, kv, kv_t):
    for part, weight in enumerate((wk, wv)):
        span = pl.ds(part * WIDTH, WIDTH)
        got = dot(feat[...], weight[...]).astype(BF16)
        kv[:, span] = got
        kv_t[span, :] = got.T


def query_grad_kernel(feat, wq, cot, wo, kv_t, qa_t, all_t, mate_t):
    qa_t[pl.ds(0, WIDTH), :] = dot(feat[...], wq[...]).astype(BF16).T
    qa_t[pl.ds(WIDTH, WIDTH), :] = dot_nt(cot[...], wo[...]).astype(BF16).T
    all_t[pl.ds(0, MODEL), :] = kv_t[...]
    all_t[pl.ds(MODEL, MODEL), :] = qa_t[...]
    mate_t[pl.ds(0, MODEL), :] = feat[...].T
    mate_t[pl.ds(MODEL, MODEL), :] = cot[...].T


def one_hot(row):
    spots = lax.broadcasted_iota(jnp.int32, (NODES, NODES), 0)
    return jnp.where(spots == row, 1.0, 0.0).astype(BF16)


def attend_kernel(
    core, mask, perms, kv, kv_t, qa_t, r0, r1, r2, r3,
    attn_t, query_t, mate, local_t, d0, d1, d2, d3, far,
):
    far_in = (r0, r1, r2, r3)
    far_out = (d0, d1, d2, d3)
    for m in range(EXPANDERS):
        far[m] = dot(far_in[m][pl.ds(0, MODEL), :], one_hot(perms[m : m + 1, :])).astype(BF16)
        far_out[m][pl.ds(16, 8), :] = jnp.broadcast_to(perms[m : m + 1, :].astype(F32), (8, NODES))
    half = NODES // 2
    row_head = lax.broadcasted_iota(jnp.int32, (2 * HEAD_DIM, NODES), 0) // HEAD_DIM
    for head in range(HEADS):
        pair = pl.ds(head // 2 * 128, 128)
        pair_v = pl.ds(WIDTH + head // 2 * 128, 128)
        here = pl.ds(head * HEAD_DIM, HEAD_DIM)
        here_v = pl.ds(WIDTH + head * HEAD_DIM, HEAD_DIM)
        mine = row_head == head % 2
        zero = jnp.zeros((), BF16)
        query_h = qa_t[here, :]
        grad_h = qa_t[here_v, :]
        query_f = query_h.astype(F32)
        grad_f = grad_h.astype(F32)
        scores = dot(kv[:, pair], jnp.where(mine, qa_t[pair, :], zero)) * SCALE
        parts = []
        for source in range(2):
            row = scores[source * half : (source + 1) * half]
            keep = [
                jnp.where(mask[to, source] > 0, row[:, to * half : (to + 1) * half], -1e30)
                for to in range(2)
            ]
            parts.append(jnp.concatenate(keep, axis=1))
        scores = jnp.concatenate(parts, axis=0)
        far_s, far_dp = [], []
        for m in range(EXPANDERS):
            far_k = far[m, here, :].astype(F32)
            far_v = far[m, here_v, :].astype(F32)
            far_s.append(jnp.sum(query_f * far_k, axis=0, keepdims=True) * SCALE)
            far_dp.append(jnp.sum(grad_f * far_v, axis=0, keepdims=True))
        top = jnp.max(scores, axis=0, keepdims=True)
        for s in far_s:
            top = jnp.maximum(top, s)
        weights = jnp.exp(scores - top)
        far_w = [jnp.exp(s - top) for s in far_s]
        total = jnp.sum(weights, axis=0, keepdims=True) + (far_w[0] + far_w[1] + far_w[2] + far_w[3])
        inverse = 1.0 / total
        probs = weights * inverse
        far_p = [w * inverse for w in far_w]
        probs_b = probs.astype(BF16)
        out = dot(kv_t[here_v, :], probs_b)
        for m in range(EXPANDERS):
            out = out + far_p[m] * far[m, here_v, :].astype(F32)
        delta = jnp.sum(grad_f * out, axis=0, keepdims=True)
        out_b = out.astype(BF16)
        attn_t[here, :] = out_b
        dprob = dot(kv[:, pair_v], jnp.where(mine, qa_t[pair_v, :], zero))
        dscore_b = (probs * (dprob - delta)).astype(BF16)
        query_g = dot(kv_t[here, :], dscore_b)
        for m in range(EXPANDERS):
            dfar = far_p[m] * (far_dp[m] - delta)
            query_g = query_g + dfar * far[m, here, :].astype(F32)
            far_out[m][head : head + 1, :] = dfar * SCALE
            far_out[m][8 + head : 9 + head, :] = far_p[m]
        query_t[here, :] = (query_g * SCALE).astype(BF16)
        local_t[here, :] = dot_nt(query_h, dscore_b) * SCALE
        local_t[here_v, :] = dot_nt(grad_h, probs_b)
    mate[pl.ds(0, 256), :] = query_t[pl.ds(pl.multiple_of((1 - core[0]) * 256, 256), 256), :]
    mate[pl.ds(256, WIDTH), :] = attn_t[...]


def owner_kernel(start, *refs):
    *pairs, grads_t = refs
    count = len(pairs) // 2
    total = start[...]
    for numbers, sent in zip(pairs[:count], pairs[count:]):
        place = one_hot(numbers[16:17, :].astype(jnp.int32))
        rows = []
        first = sent.shape[0] - MODEL
        for part in range(2 * HEADS):
            rows.append(
                (
                    sent[pl.ds(first + part * HEAD_DIM, HEAD_DIM), :].astype(F32)
                    * numbers[part : part + 1, :]
                ).astype(BF16)
            )
        total = total + dot_nt(jnp.concatenate(rows, axis=0), place)
    grads_t[...] = total.astype(grads_t.dtype)


def put_proj(out, prod, offset):
    nz, ny, nx, nl, _ = SIZES
    for y in range(ny):
        for x in range(nx):
            for z in range(nz):
                row = ((z * ny + y) * nx + x) * 16
                for low in range(nl):
                    out[(y * nx + x) * nl + low, pl.ds(z * 32 + offset, 16), :] = prod[
                        row : row + 16, low * 128 : low * 128 + 128
                    ].astype(BF16)


def early_terms_kernel(core, own, theirs, query_t, attn_t, mate, out):
    nz, ny, nx, nl, _ = SIZES
    feat = pl.ds(0, MODEL)
    mine = pl.ds(pl.multiple_of(core[0] * 256, 256), 256)
    prod = dot_nt(own[feat, :], query_t[mine, :]) + dot_nt(theirs[feat, :], mate[pl.ds(0, 256), :])
    put_proj(out, prod, 0)
    mine = pl.ds(pl.multiple_of(MODEL + core[0] * WIDTH, WIDTH), WIDTH)
    prod = dot_nt(attn_t[...], own[mine, :]) + dot_nt(mate[pl.ds(256, WIDTH), :], theirs[mine, :])
    for y in range(ny):
        for x in range(nx):
            for z in range(nz):
                row = ((z * ny + y) * nx + x) * 8
                for low in range(nl):
                    piece = prod[row : row + 8, low * 256 : low * 256 + 256]
                    both = jnp.concatenate([piece[:, :128], piece[:, 128:]], axis=0)
                    out[(y * nx + x) * nl + low, pl.ds(z * 32 + 16, 16), :] = both.astype(BF16)


def late_terms_kernel(core, own, theirs, grads_t, mate, out):
    feat = pl.ds(0, MODEL)
    for part in range(2):
        mine = pl.ds(pl.multiple_of(part * WIDTH + core[0] * 256, 256), 256)
        prod = dot_nt(own[feat, :], grads_t[mine, :])
        prod = prod + dot_nt(theirs[feat, :], mate[mine, :])
        put_proj(out, prod, part * 16)


def feature_grad_kernel(query_t, grads_t, wq, wk, wv, out):
    total = dot_nt(query_t[...].T, wq[...])
    total = total + dot_nt(grads_t[pl.ds(0, WIDTH), :].T, wk[...])
    total = total + dot_nt(grads_t[pl.ds(WIDTH, WIDTH), :].T, wv[...])
    out[...] = total.astype(BF16)


def plane_sum_kernel(early, late, out):
    for part, got in enumerate((early, late)):
        total = got[0].astype(F32)
        for i in range(1, got.shape[0]):
            total = total + got[i].astype(F32)
        total = total.astype(BF16)
        for z in range(SIZES[0]):
            out[z, pl.ds(part * 32, 32), :] = total[z * 32 : z * 32 + 32]


def line_sum_kernel(factor, got, out):
    total = got[0].astype(F32)
    for z in range(1, SIZES[0]):
        total = total + got[z].astype(F32)
    out[...] = (total * factor).astype(BF16)


def place_kernel(got, proj, outs):
    _, _, _, nl, nc = SIZES
    for low in range(nl):
        for c in range(nc):
            share = got[low * nc + c].astype(F32)
            cols = pl.ds(c * 256 + low * 128, 128)
            proj[0, :, cols] = share[:16].astype(BF16)
            proj[1, :, cols] = share[32:48].astype(BF16)
            proj[2, :, cols] = share[48:].astype(BF16)
            for h in range(2):
                wide = pl.ds(c * WIDTH + low * 256 + h * 128, 128)
                outs[:, wide] = share[16 + 8 * h : 24 + 8 * h].astype(BF16)


def after(value, *others):
    return lax.optimization_barrier((value, *others))[0]


def shards(features, block_mask, expander_perm, cotangent, w_query, w_key, w_value, w_out):
    feat = features[0]
    cot = cotangent[0]
    mask = block_mask[0, 0]
    perms = expander_perm[0, 0]
    core = lax.axis_index("core").astype(jnp.int32).reshape(1)
    domains = SIZES[0] * SIZES[1] * SIZES[2]
    levels = domains.bit_length() - 1
    bits = [m * levels // EXPANDERS for m in range(EXPANDERS)]
    proj_flops = 2 * 2 * NODES * MODEL * WIDTH
    kv, kv_t = call(
        key_value_kernel, "key_value", (shape(NODES, MODEL), shape(MODEL, NODES)), [VMEM] * 3,
        (feat, w_key, w_value), proj_flops,
    )
    qa_t, all_t, own = call(
        query_grad_kernel, "query_grad",
        (shape(MODEL, NODES), shape(2 * MODEL, NODES), shape(2 * MODEL, NODES)), [VMEM] * 5,
        (feat, w_query, cot, w_out, kv_t), proj_flops,
    )
    far, sent = [None] * EXPANDERS, [None] * EXPANDERS
    for m in range(EXPANDERS):
        if bits[m] >= 3:
            far[m] = swap(kv_t, DOM, bits[m])
            sent[m] = swap(qa_t, DOM, bits[m])
        else:
            far[m] = sent[m] = swap(all_t, DOM, bits[m])
    theirs = swap(own, ("core",), 0)
    qa_here = after(qa_t, theirs)
    attn_t, query_t, mate, local_t, *numbers = call(
        attend_kernel, "attend",
        (shape(WIDTH, NODES), shape(WIDTH, NODES), shape(768, NODES), shape(MODEL, NODES, dtype=F32))
        + (shape(24, NODES, dtype=F32),) * 4,
        [SMEM, SMEM] + [VMEM] * 8,
        (core, mask, perms, kv, kv_t, qa_here, *far), 4 << 30,
        scratch=[pltpu.VMEM((EXPANDERS, MODEL, NODES), BF16)],
    )
    for m in range(EXPANDERS):
        numbers[m] = swap(numbers[m], DOM, bits[m])
    mate = swap(mate, ("core",), 0)
    early = call(
        early_terms_kernel, "early_terms", shape(16, 256, 128), [SMEM] + [VMEM] * 5,
        (core, own, theirs, query_t, attn_t, mate), 2 * proj_flops,
    )
    local_t = after(local_t, early)
    early = lax.all_to_all(early, PLANE, 0, 0, tiled=True)
    near = [m for m in range(EXPANDERS) if bits[m] < 3]
    line = [m for m in range(EXPANDERS) if bits[m] >= 3]
    local_t = call(
        owner_kernel, "owner_near", shape(MODEL, NODES, dtype=F32), [VMEM] * (1 + 2 * len(near)),
        (local_t, *(numbers[m] for m in near), *(sent[m] for m in near)), 1 << 30,
    )
    grads_t = call(
        owner_kernel, "owner", shape(MODEL, NODES), [VMEM] * (1 + 2 * len(line)),
        (local_t, *(numbers[m] for m in line), *(sent[m] for m in line)), 30 << 30,
    )
    mate = swap(grads_t, ("core",), 0)
    late = call(
        late_terms_kernel, "late_terms", shape(16, 256, 128), [SMEM] + [VMEM] * 4,
        (core, own, theirs, grads_t, mate), 2 * proj_flops,
    )
    grads_here = after(grads_t, late)
    late = lax.all_to_all(late, PLANE, 0, 0, tiled=True)
    feature_grad = call(
        feature_grad_kernel, "feature_grad", shape(NODES, MODEL), [VMEM] * 5,
        (query_t, grads_here, w_query, w_key, w_value), 2 * proj_flops,
    )
    graphs = SIZES[3] * SIZES[4]
    factor = (graphs * domains * NODES) ** (-0.5)
    part = call(plane_sum_kernel, "plane_sum", shape(SIZES[0], 64, 128), [VMEM] * 2, (early, late), 1 << 20)
    part = lax.all_to_all(part, "z", 0, 0, tiled=True)
    part = call(
        functools.partial(line_sum_kernel, factor), "line_sum", shape(64, 128), [VMEM], (part,), 1 << 20
    )
    part = lax.all_gather(part, REP, axis=0, tiled=False)
    proj_grads, out_grad = call(
        place_kernel, "place", (shape(3, 16, WIDTH), shape(8, MODEL)), [VMEM], (part,), 1 << 20
    )
    return (feature_grad[None], proj_grads, out_grad)


def solution(mesh):
    fine = Mesh(mesh.devices.reshape(SIZES), DOM + REP)
    placed = (
        P(REP, DOM, None),
        P(REP, DOM, None, None),
        P(REP, DOM, None, None),
        P(REP, DOM, None),
        P(),
        P(),
        P(),
        P(),
    )
    return jax.shard_map(
        shards,
        mesh=fine,
        in_specs=placed,
        out_specs=(P(REP, DOM, None), P(None, DOM, None), P(DOM, None)),
        check_vma=False,
    )
```

```python
import functools

import jax
import jax.numpy as jnp
from jax import lax
from jax.experimental import pallas as pl
from jax.experimental.pallas import tpu as pltpu
from jax.sharding import Mesh, PartitionSpec as P

HEADS = 8
HEAD_DIM = 64
EXPANDERS = 4
NODES = 256
WIDTH = 512
MODEL = 1024
DOM = ("z", "y", "xh")
REP = ("xl", "core")
PLANE = ("y", "xh", "xl")
SIZES = (8, 4, 2, 2, 2)
F32 = jnp.float32
BF16 = jnp.bfloat16
SCALE = HEAD_DIM ** (-0.5)
VMEM = pl.BlockSpec(memory_space=pltpu.VMEM)
SMEM = pl.BlockSpec(memory_space=pltpu.SMEM)


def dot(a, b):
    return jnp.dot(a, b, preferred_element_type=F32)


def dot_nt(a, b):
    return lax.dot_general(a, b, (((1,), (1,)), ((), ())), preferred_element_type=F32)


def call(body, name, outs, specs, args, flops, scratch=(), moved=2 << 20):
    return pl.pallas_call(
        body,
        out_shape=outs,
        in_specs=specs,
        out_specs=jax.tree.map(lambda _: VMEM, outs),
        scratch_shapes=scratch,
        compiler_params=pltpu.CompilerParams(vmem_limit_bytes=16 << 20),
        cost_estimate=pl.CostEstimate(flops=flops if name in ("owner", "attend") else 1024, bytes_accessed=1024, transcendentals=0),
        name=name,
    )(*args)


def shape(*dims, dtype=BF16):
    return jax.ShapeDtypeStruct(dims, dtype)


def swap(value, axes, bit):
    count = 1
    for axis in axes:
        count *= lax.axis_size(axis)
    return lax.ppermute(value, axes, [(i, i ^ 1 << bit) for i in range(count)])


PARTS = 4


def project_kernel(feat_h, wk_h, wv_h, wq_h, cot_h, wo_h, kv, kv_t, qa_t, own, feat, wk, wv, wq, cot, wo, sems):
    pairs = ((feat_h, feat), (wk_h, wk), (wv_h, wv), (wq_h, wq), (cot_h, cot), (wo_h, wo))
    copies = []
    for i, (source, target) in enumerate(pairs):
        size = target.shape[0] // PARTS
        copies.append([])
        for j in range(PARTS):
            rows = pl.ds(j * size, size)
            copy = pltpu.make_async_copy(source.at[rows, :], target.at[rows, :], sems.at[i, j])
            copy.start()
            copies[i].append(copy)

    def wait(i):
        for copy in copies[i]:
            copy.wait()

    wait(0)
    own[pl.ds(0, MODEL), :] = feat[...].T
    for part, weight in enumerate((wk, wv)):
        wait(1 + part)
        span = pl.ds(part * WIDTH, WIDTH)
        got = dot(feat[...], weight[...]).astype(BF16)
        kv[:, span] = got
        kv_t[span, :] = got.T
    wait(3)
    qa_t[pl.ds(0, WIDTH), :] = dot(feat[...], wq[...]).astype(BF16).T
    wait(4)
    own[pl.ds(MODEL, MODEL), :] = cot[...].T
    wait(5)
    qa_t[pl.ds(WIDTH, WIDTH), :] = dot_nt(cot[...], wo[...]).astype(BF16).T


def one_hot(row):
    spots = lax.broadcasted_iota(jnp.int32, (NODES, NODES), 0)
    return jnp.where(spots == row, 1.0, 0.0).astype(BF16)


def attend_kernel(
    core, mask, perms, kv, kv_t, qa_t, r0, r1, r2, r3,
    attn_t, query_t, mate, local_t, d0, d1, d2, d3, far,
):
    far_in = (r0, r1, r2, r3)
    far_out = (d0, d1, d2, d3)
    for m in range(EXPANDERS):
        far[m] = dot(far_in[m][pl.ds(0, MODEL), :], one_hot(perms[EXPANDERS - 1 - m : EXPANDERS - m, :])).astype(BF16)
        far_out[m][pl.ds(16, 8), :] = jnp.broadcast_to(perms[EXPANDERS - 1 - m : EXPANDERS - m, :].astype(F32), (8, NODES))
    half = NODES // 2
    row_head = lax.broadcasted_iota(jnp.int32, (2 * HEAD_DIM, NODES), 0) // HEAD_DIM
    for head in range(HEADS):
        pair = pl.ds(head // 2 * 128, 128)
        pair_v = pl.ds(WIDTH + head // 2 * 128, 128)
        here = pl.ds(head * HEAD_DIM, HEAD_DIM)
        here_v = pl.ds(WIDTH + head * HEAD_DIM, HEAD_DIM)
        mine = row_head == head % 2
        zero = jnp.zeros((), BF16)
        query_h = qa_t[here, :]
        grad_h = qa_t[here_v, :]
        query_f = query_h.astype(F32)
        grad_f = grad_h.astype(F32)
        scores = dot(kv[:, pair], jnp.where(mine, qa_t[pair, :], zero)) * SCALE
        parts = []
        for source in range(2):
            row = scores[source * half : (source + 1) * half]
            keep = [
                jnp.where(mask[to, source] > 0, row[:, to * half : (to + 1) * half], -1e30)
                for to in range(2)
            ]
            parts.append(jnp.concatenate(keep, axis=1))
        scores = jnp.concatenate(parts, axis=0)
        far_s, far_dp = [], []
        for m in range(EXPANDERS):
            far_k = far[m, here, :].astype(F32)
            far_v = far[m, here_v, :].astype(F32)
            far_s.append(jnp.sum(query_f * far_k, axis=0, keepdims=True) * SCALE)
            far_dp.append(jnp.sum(grad_f * far_v, axis=0, keepdims=True))
        top = jnp.max(scores, axis=0, keepdims=True)
        for s in far_s:
            top = jnp.maximum(top, s)
        weights = jnp.exp(scores - top)
        far_w = [jnp.exp(s - top) for s in far_s]
        total = jnp.sum(weights, axis=0, keepdims=True) + (far_w[0] + far_w[1] + far_w[2] + far_w[3])
        inverse = 1.0 / total
        probs = weights * inverse
        far_p = [w * inverse for w in far_w]
        probs_b = probs.astype(BF16)
        out = dot(kv_t[here_v, :], probs_b)
        for m in range(EXPANDERS):
            out = out + far_p[m] * far[m, here_v, :].astype(F32)
        delta = jnp.sum(grad_f * out, axis=0, keepdims=True)
        out_b = out.astype(BF16)
        attn_t[here, :] = out_b
        dprob = dot(kv[:, pair_v], jnp.where(mine, qa_t[pair_v, :], zero))
        dscore_b = (probs * (dprob - delta)).astype(BF16)
        query_g = dot(kv_t[here, :], dscore_b)
        for m in range(EXPANDERS):
            dfar = far_p[m] * (far_dp[m] - delta)
            query_g = query_g + dfar * far[m, here, :].astype(F32)
            far_out[m][head : head + 1, :] = dfar * SCALE
            far_out[m][8 + head : 9 + head, :] = far_p[m]
        query_t[here, :] = (query_g * SCALE).astype(BF16)
        local_t[here, :] = dot_nt(query_h, dscore_b) * SCALE
        local_t[here_v, :] = dot_nt(grad_h, probs_b)
    mate[pl.ds(0, 256), :] = query_t[pl.ds(pl.multiple_of((1 - core[0]) * 256, 256), 256), :]
    mate[pl.ds(256, WIDTH), :] = attn_t[...]


def owner_kernel(start, *refs):
    *pairs, grads_t = refs
    count = len(pairs) // 2
    total = start[...]
    for numbers, sent in zip(pairs[:count], pairs[count:]):
        place = one_hot(numbers[16:17, :].astype(jnp.int32))
        rows = []
        first = sent.shape[0] - MODEL
        for part in range(2 * HEADS):
            rows.append(
                (
                    sent[pl.ds(first + part * HEAD_DIM, HEAD_DIM), :].astype(F32)
                    * numbers[part : part + 1, :]
                ).astype(BF16)
            )
        total = total + dot_nt(jnp.concatenate(rows, axis=0), place)
    grads_t[...] = total.astype(grads_t.dtype)


def put_proj(out, prod, offset):
    nz, ny, nx, nl, _ = SIZES
    for y in range(ny):
        for x in range(nx):
            for z in range(nz):
                row = ((z * ny + y) * nx + x) * 16
                for low in range(nl):
                    out[(y * nx + x) * nl + low, pl.ds(z * 32 + offset, 16), :] = prod[
                        row : row + 16, low * 128 : low * 128 + 128
                    ].astype(BF16)


def early_terms_kernel(core, own, theirs, query_t, attn_t, mate, out):
    nz, ny, nx, nl, _ = SIZES
    feat = pl.ds(0, MODEL)
    mine = pl.ds(pl.multiple_of(core[0] * 256, 256), 256)
    prod = dot_nt(own[feat, :], query_t[mine, :]) + dot_nt(theirs[feat, :], mate[pl.ds(0, 256), :])
    put_proj(out, prod, 0)
    mine = pl.ds(pl.multiple_of(MODEL + core[0] * WIDTH, WIDTH), WIDTH)
    prod = dot_nt(attn_t[...], own[mine, :]) + dot_nt(mate[pl.ds(256, WIDTH), :], theirs[mine, :])
    for y in range(ny):
        for x in range(nx):
            for z in range(nz):
                row = ((z * ny + y) * nx + x) * 8
                for low in range(nl):
                    piece = prod[row : row + 8, low * 256 : low * 256 + 256]
                    both = jnp.concatenate([piece[:, :128], piece[:, 128:]], axis=0)
                    out[(y * nx + x) * nl + low, pl.ds(z * 32 + 16, 16), :] = both.astype(BF16)


def late_terms_kernel(core, own, theirs, grads_t, mate, out):
    feat = pl.ds(0, MODEL)
    for part in range(2):
        mine = pl.ds(pl.multiple_of(part * WIDTH + core[0] * 256, 256), 256)
        prod = dot_nt(own[feat, :], grads_t[mine, :])
        prod = prod + dot_nt(theirs[feat, :], mate[mine, :])
        put_proj(out, prod, part * 16)


def feature_grad_kernel(query_t, grads_t, wq, wk, wv, out):
    total = dot_nt(query_t[...].T, wq[...])
    total = total + dot_nt(grads_t[pl.ds(0, WIDTH), :].T, wk[...])
    total = total + dot_nt(grads_t[pl.ds(WIDTH, WIDTH), :].T, wv[...])
    out[...] = total.astype(BF16)


def plane_total(got):
    total = got[0].astype(F32)
    for i in range(1, got.shape[0]):
        total = total + got[i].astype(F32)
    return total.astype(BF16)


def early_sum_kernel(got, out):
    out[...] = plane_total(got)


def plane_sum_kernel(early, got, out):
    late = plane_total(got)
    for z in range(SIZES[0]):
        out[z, pl.ds(0, 32), :] = early[pl.ds(z * 32, 32), :]
        out[z, pl.ds(32, 32), :] = late[z * 32 : z * 32 + 32]


def line_sum_kernel(factor, got, out):
    total = got[0].astype(F32)
    for z in range(1, SIZES[0]):
        total = total + got[z].astype(F32)
    out[...] = (total * factor).astype(BF16)


def place_kernel(got, proj, outs):
    _, _, _, nl, nc = SIZES
    for low in range(nl):
        for c in range(nc):
            share = got[low * nc + c].astype(F32)
            cols = pl.ds(c * 256 + low * 128, 128)
            proj[0, :, cols] = share[:16].astype(BF16)
            proj[1, :, cols] = share[32:48].astype(BF16)
            proj[2, :, cols] = share[48:].astype(BF16)
            for h in range(2):
                wide = pl.ds(c * WIDTH + low * 256 + h * 128, 128)
                outs[:, wide] = share[16 + 8 * h : 24 + 8 * h].astype(BF16)


def after(value, *others):
    return lax.optimization_barrier((value, *others))[0]


def shards(features, block_mask, expander_perm, cotangent, w_query, w_key, w_value, w_out):
    feat = features[0]
    cot = cotangent[0]
    mask = block_mask[0, 0]
    perms = expander_perm[0, 0]
    core = lax.axis_index("core").astype(jnp.int32).reshape(1)
    domains = SIZES[0] * SIZES[1] * SIZES[2]
    levels = domains.bit_length() - 1
    bits = [m * levels // EXPANDERS for m in reversed(range(EXPANDERS))]
    proj_flops = 2 * 2 * NODES * MODEL * WIDTH
    kv, kv_t, qa_t, own = call(
        project_kernel, "project",
        (shape(NODES, MODEL), shape(MODEL, NODES), shape(MODEL, NODES), shape(2 * MODEL, NODES)),
        [pl.BlockSpec(memory_space=pl.ANY)] * 6,
        (feat, w_key, w_value, w_query, cot, w_out), 2 * proj_flops,
        scratch=[
            pltpu.VMEM(x.shape, BF16) for x in (feat, w_key, w_value, w_query, cot, w_out)
        ] + [pltpu.SemaphoreType.DMA((6, PARTS))],
    )
    far, sent = [None] * EXPANDERS, [None] * EXPANDERS
    for m in range(EXPANDERS):
        far[m] = swap(kv_t, DOM, bits[m])
    theirs = swap(own, ("core",), 0)
    for m in range(EXPANDERS):
        sent[m] = swap(qa_t, DOM, bits[m])
    qa_here = after(qa_t, theirs)
    attn_t, query_t, mate, local_t, *numbers = call(
        attend_kernel, "attend",
        (shape(WIDTH, NODES), shape(WIDTH, NODES), shape(768, NODES), shape(MODEL, NODES, dtype=F32))
        + (shape(24, NODES, dtype=F32),) * 4,
        [SMEM, SMEM] + [VMEM] * 8,
        (core, mask, perms, kv, kv_t, qa_here, *far), 4 << 30,
        scratch=[pltpu.VMEM((EXPANDERS, MODEL, NODES), BF16)],
    )
    for m in range(EXPANDERS):
        numbers[m] = swap(numbers[m], DOM, bits[m])
    mate = swap(mate, ("core",), 0)
    early = call(
        early_terms_kernel, "early_terms", shape(16, 256, 128), [SMEM] + [VMEM] * 5,
        (core, own, theirs, query_t, attn_t, mate), 2 * proj_flops,
    )
    local_t = after(local_t, early)
    early = lax.all_to_all(early, PLANE, 0, 0, tiled=True)
    near = [m for m in range(EXPANDERS) if bits[m] < 3]
    line = [m for m in range(EXPANDERS) if bits[m] >= 3]
    local_t = call(
        owner_kernel, "owner_near", shape(MODEL, NODES, dtype=F32), [VMEM] * (1 + 2 * len(near)),
        (local_t, *(numbers[m] for m in near), *(sent[m] for m in near)), 1 << 30,
    )
    grads_t = call(
        owner_kernel, "owner", shape(MODEL, NODES), [VMEM] * (1 + 2 * len(line)),
        (local_t, *(numbers[m] for m in line), *(sent[m] for m in line)), 30 << 30,
    )
    mate = swap(grads_t, ("core",), 0)
    late = call(
        late_terms_kernel, "late_terms", shape(16, 256, 128), [SMEM] + [VMEM] * 4,
        (core, own, theirs, grads_t, mate), 2 * proj_flops,
    )
    grads_here = after(grads_t, late)
    early = call(early_sum_kernel, "early_sum", shape(256, 128), [VMEM], (early,), 1 << 20)
    late = lax.all_to_all(late, PLANE, 0, 0, tiled=True)
    feature_grad = call(
        feature_grad_kernel, "feature_grad", shape(NODES, MODEL), [VMEM] * 5,
        (query_t, grads_here, w_query, w_key, w_value), 2 * proj_flops,
    )
    graphs = SIZES[3] * SIZES[4]
    factor = (graphs * domains * NODES) ** (-0.5)
    part = call(plane_sum_kernel, "plane_sum", shape(SIZES[0], 64, 128), [VMEM] * 2, (early, late), 1 << 20)
    part = lax.all_to_all(part, "z", 0, 0, tiled=True)
    part = call(
        functools.partial(line_sum_kernel, factor), "line_sum", shape(64, 128), [VMEM], (part,), 1 << 20
    )
    part = lax.all_gather(part, REP, axis=0, tiled=False)
    proj_grads, out_grad = call(
        place_kernel, "place", (shape(3, 16, WIDTH), shape(8, MODEL)), [VMEM], (part,), 1 << 20
    )
    return (feature_grad[None], proj_grads, out_grad)


def solution(mesh):
    fine = Mesh(mesh.devices.reshape(SIZES), DOM + REP)
    placed = (
        P(REP, DOM, None),
        P(REP, DOM, None, None),
        P(REP, DOM, None, None),
        P(REP, DOM, None),
        P(),
        P(),
        P(),
        P(),
    )
    return jax.shard_map(
        shards,
        mesh=fine,
        in_specs=placed,
        out_specs=(P(REP, DOM, None), P(None, DOM, None), P(DOM, None)),
        check_vma=False,
    )
```

```python
import functools

import jax
import jax.numpy as jnp
from jax import lax
from jax.experimental import pallas as pl
from jax.experimental.pallas import tpu as pltpu
from jax.sharding import Mesh, PartitionSpec as P

HEADS = 8
HEAD_DIM = 64
EXPANDERS = 4
NODES = 256
WIDTH = 512
MODEL = 1024
DOM = ("z", "y", "xh")
REP = ("xl", "core")
PLANE = ("y", "xh", "xl")
SIZES = (8, 4, 2, 2, 2)
F32 = jnp.float32
BF16 = jnp.bfloat16
SCALE = HEAD_DIM ** (-0.5)
VMEM = pl.BlockSpec(memory_space=pltpu.VMEM)
SMEM = pl.BlockSpec(memory_space=pltpu.SMEM)
HERE = pl.BlockSpec(memory_space=pl.ANY)


def dot(a, b):
    return jnp.dot(a, b, preferred_element_type=F32)


def dot_nt(a, b):
    return lax.dot_general(a, b, (((1,), (1,)), ((), ())), preferred_element_type=F32)


def call(body, name, outs, specs, args, flops, scratch=(), moved=2 << 20, room=16, results=VMEM):
    return pl.pallas_call(
        body,
        out_shape=outs,
        in_specs=specs,
        out_specs=jax.tree.map(lambda _: results, outs),
        scratch_shapes=scratch,
        compiler_params=pltpu.CompilerParams(vmem_limit_bytes=room << 20),
        cost_estimate=pl.CostEstimate(flops=flops if name in ("owner", "attend") else 1024, bytes_accessed=1024, transcendentals=0),
        name=name,
    )(*args)


def staged(body, name, outs, args, flops, rows=None, scalars=()):
    rows = rows or {}
    several = isinstance(outs, tuple)
    results = outs if several else (outs,)
    sizes = [(x.shape[0] - rows.get(i, 0),) + x.shape[1:] for i, x in enumerate(args)]

    def kernel(*refs):
        refs = list(refs)
        small, refs = refs[: len(scalars)], refs[len(scalars) :]
        given, refs = refs[: len(args)], refs[len(args) :]
        wanted, refs = refs[: len(results)], refs[len(results) :]
        held, refs = refs[: len(args)], refs[len(args) :]
        made, (in_sems, out_sems) = refs[: len(results)], refs[len(results) :]
        copies = []
        for i, (source, target) in enumerate(zip(given, held)):
            size = target.shape[0] // 2
            if size % 16:
                size = target.shape[0]
            for j in range(target.shape[0] // size):
                copy = pltpu.make_async_copy(
                    source.at[pl.ds(rows.get(i, 0) + j * size, size)],
                    target.at[pl.ds(j * size, size)],
                    in_sems.at[i, j],
                )
                copy.start()
                copies.append(copy)
        for copy in copies:
            copy.wait()
        body(*small, *held, *made)
        copies = []
        for i, (source, target) in enumerate(zip(made, wanted)):
            copies.append(pltpu.make_async_copy(source, target, out_sems.at[i]))
            copies[-1].start()
        for copy in copies:
            copy.wait()

    scratch = [pltpu.VMEM(size, x.dtype) for size, x in zip(sizes, args)]
    scratch += [pltpu.VMEM(x.shape, x.dtype) for x in results]
    scratch += [pltpu.SemaphoreType.DMA((len(args), 2)), pltpu.SemaphoreType.DMA((len(results),))]
    return call(
        kernel, name, outs, [SMEM] * len(scalars) + [HERE] * len(args), (*scalars, *args), flops,
        scratch=scratch, room=60, results=HERE,
    )


def shape(*dims, dtype=BF16):
    return jax.ShapeDtypeStruct(dims, dtype)


def swap(value, axes, bit):
    count = 1
    for axis in axes:
        count *= lax.axis_size(axis)
    return lax.ppermute(value, axes, [(i, i ^ 1 << bit) for i in range(count)])


PARTS = 4


def project_kernel(
    feat_h, wk_h, wv_h, wq_h, cot_h, wo_h, kv_h, kv_t_h, qa_t_h, all_h, own_h,
    feat, wk, wv, wq, cot, wo, kv, all_t, own, in_sems, out_sems,
):
    pairs = ((feat_h, feat), (wk_h, wk), (wv_h, wv), (wq_h, wq), (cot_h, cot), (wo_h, wo))
    copies = []
    for i, (source, target) in enumerate(pairs):
        size = target.shape[0] // PARTS
        copies.append([])
        for j in range(PARTS):
            rows = pl.ds(j * size, size)
            copy = pltpu.make_async_copy(source.at[rows, :], target.at[rows, :], in_sems.at[i, j])
            copy.start()
            copies[i].append(copy)
    sends = []

    def wait(i):
        for copy in copies[i]:
            copy.wait()

    def send(source, target):
        copy = pltpu.make_async_copy(source, target, out_sems.at[len(sends)])
        copy.start()
        sends.append(copy)

    keys = pl.ds(0, WIDTH)
    values = pl.ds(WIDTH, WIDTH)
    top = pl.ds(0, MODEL)
    wait(0)
    for part, span in enumerate((keys, values)):
        wait(1 + part)
        got = dot(feat[...], (wk, wv)[part][...]).astype(BF16)
        kv[:, span] = got
        all_t[span, :] = got.T
        send(all_t.at[span, :], kv_t_h.at[span, :])
        send(all_t.at[span, :], all_h.at[span, :])
    send(kv, kv_h)
    wait(3)
    span = pl.ds(MODEL, WIDTH)
    all_t[span, :] = dot(feat[...], wq[...]).astype(BF16).T
    send(all_t.at[span, :], qa_t_h.at[keys, :])
    send(all_t.at[span, :], all_h.at[span, :])
    own[top, :] = feat[...].T
    send(own.at[top, :], own_h.at[top, :])
    wait(4)
    wait(5)
    span = pl.ds(MODEL + WIDTH, WIDTH)
    all_t[span, :] = dot_nt(cot[...], wo[...]).astype(BF16).T
    send(all_t.at[span, :], qa_t_h.at[values, :])
    send(all_t.at[span, :], all_h.at[span, :])
    rest = pl.ds(MODEL, MODEL)
    own[rest, :] = cot[...].T
    send(own.at[rest, :], own_h.at[rest, :])
    for copy in sends:
        copy.wait()


def one_hot(row):
    spots = lax.broadcasted_iota(jnp.int32, (NODES, NODES), 0)
    return jnp.where(spots == row, 1.0, 0.0).astype(BF16)


def attend_kernel(
    core, mask, perms, kv_h, kv_t_h, qa_t_h, r0, r1, r2, r3,
    attn_h, query_h_t, mate_h, local_h, g0, g1, g2, g3,
    far, kv, kv_t, qa_t, far_in, attn_t, query_t, local_t, d0, d1, d2, d3, in_sems, out_sems,
):
    far_out = (d0, d1, d2, d3)
    fetched = []
    pairs = [(r, far_in.at[m]) for m, r in enumerate((r0, r1, r2, r3))]
    pairs += [(kv_h, kv), (qa_t_h, qa_t), (kv_t_h, kv_t)]
    for i, (source, target) in enumerate(pairs):
        size = target.shape[0] // 2
        fetched.append([])
        for j in range(2):
            rows = pl.ds(j * size, size)
            copy = pltpu.make_async_copy(source.at[rows, :], target.at[rows, :], in_sems.at[i, j])
            copy.start()
            fetched[i].append(copy)
    sends = []

    def send(source, target):
        copy = pltpu.make_async_copy(source, target, out_sems.at[len(sends)])
        copy.start()
        sends.append(copy)

    for m in range(EXPANDERS):
        for copy in fetched[m]:
            copy.wait()
        far[m] = dot(far_in[m], one_hot(perms[m : m + 1, :])).astype(BF16)
        far_out[m][pl.ds(16, 8), :] = jnp.broadcast_to(perms[m : m + 1, :].astype(F32), (8, NODES))
    for group in fetched[EXPANDERS:]:
        for copy in group:
            copy.wait()
    half = NODES // 2
    row_head = lax.broadcasted_iota(jnp.int32, (2 * HEAD_DIM, NODES), 0) // HEAD_DIM
    for head in range(HEADS):
        pair = pl.ds(head // 2 * 128, 128)
        pair_v = pl.ds(WIDTH + head // 2 * 128, 128)
        here = pl.ds(head * HEAD_DIM, HEAD_DIM)
        here_v = pl.ds(WIDTH + head * HEAD_DIM, HEAD_DIM)
        mine = row_head == head % 2
        zero = jnp.zeros((), BF16)
        query_h = qa_t[here, :]
        grad_h = qa_t[here_v, :]
        query_f = query_h.astype(F32)
        grad_f = grad_h.astype(F32)
        scores = dot(kv[:, pair], jnp.where(mine, qa_t[pair, :], zero)) * SCALE
        parts = []
        for source in range(2):
            row = scores[source * half : (source + 1) * half]
            keep = [
                jnp.where(mask[to, source] > 0, row[:, to * half : (to + 1) * half], -1e30)
                for to in range(2)
            ]
            parts.append(jnp.concatenate(keep, axis=1))
        scores = jnp.concatenate(parts, axis=0)
        far_s, far_dp = [], []
        for m in range(EXPANDERS):
            far_k = far[m, here, :].astype(F32)
            far_v = far[m, here_v, :].astype(F32)
            far_s.append(jnp.sum(query_f * far_k, axis=0, keepdims=True) * SCALE)
            far_dp.append(jnp.sum(grad_f * far_v, axis=0, keepdims=True))
        top = jnp.max(scores, axis=0, keepdims=True)
        for s in far_s:
            top = jnp.maximum(top, s)
        weights = jnp.exp(scores - top)
        far_w = [jnp.exp(s - top) for s in far_s]
        total = jnp.sum(weights, axis=0, keepdims=True) + (far_w[0] + far_w[1] + far_w[2] + far_w[3])
        inverse = 1.0 / total
        probs = weights * inverse
        far_p = [w * inverse for w in far_w]
        probs_b = probs.astype(BF16)
        out = dot(kv_t[here_v, :], probs_b)
        for m in range(EXPANDERS):
            out = out + far_p[m] * far[m, here_v, :].astype(F32)
        delta = jnp.sum(grad_f * out, axis=0, keepdims=True)
        out_b = out.astype(BF16)
        attn_t[here, :] = out_b
        dprob = dot(kv[:, pair_v], jnp.where(mine, qa_t[pair_v, :], zero))
        dscore_b = (probs * (dprob - delta)).astype(BF16)
        query_g = dot(kv_t[here, :], dscore_b)
        for m in range(EXPANDERS):
            dfar = far_p[m] * (far_dp[m] - delta)
            query_g = query_g + dfar * far[m, here, :].astype(F32)
            far_out[m][head : head + 1, :] = dfar * SCALE
            far_out[m][8 + head : 9 + head, :] = far_p[m]
        query_t[here, :] = (query_g * SCALE).astype(BF16)
        local_t[here, :] = dot_nt(query_h, dscore_b) * SCALE
        local_t[here_v, :] = dot_nt(grad_h, probs_b)
        send(local_t.at[here, :], local_h.at[here, :])
        send(local_t.at[here_v, :], local_h.at[here_v, :])
        send(attn_t.at[here, :], attn_h.at[here, :])
        send(attn_t.at[here, :], mate_h.at[pl.ds(256 + head * HEAD_DIM, HEAD_DIM), :])
        send(query_t.at[here, :], query_h_t.at[here, :])
    other = pl.ds(pl.multiple_of((1 - core[0]) * 256, 256), 256)
    send(query_t.at[other, :], mate_h.at[pl.ds(0, 256), :])
    for source, target in zip(far_out, (g0, g1, g2, g3)):
        send(source, target)
    for copy in sends:
        copy.wait()


def owner_kernel(start, *refs):
    *pairs, grads_t = refs
    count = len(pairs) // 2
    total = start[...]
    for numbers, sent in zip(pairs[:count], pairs[count:]):
        place = one_hot(numbers[16:17, :].astype(jnp.int32))
        rows = []
        first = sent.shape[0] - MODEL
        for part in range(2 * HEADS):
            rows.append(
                (
                    sent[pl.ds(first + part * HEAD_DIM, HEAD_DIM), :].astype(F32)
                    * numbers[part : part + 1, :]
                ).astype(BF16)
            )
        total = total + dot_nt(jnp.concatenate(rows, axis=0), place)
    grads_t[...] = total.astype(grads_t.dtype)


def put_proj(out, prod, offset):
    nz, ny, nx, nl, _ = SIZES
    for y in range(ny):
        for x in range(nx):
            for z in range(nz):
                row = ((z * ny + y) * nx + x) * 16
                for low in range(nl):
                    out[(y * nx + x) * nl + low, pl.ds(z * 32 + offset, 16), :] = prod[
                        row : row + 16, low * 128 : low * 128 + 128
                    ].astype(BF16)


def early_terms_kernel(core, own, theirs, query_t, attn_t, mate, out):
    nz, ny, nx, nl, _ = SIZES
    feat = pl.ds(0, MODEL)
    mine = pl.ds(pl.multiple_of(core[0] * 256, 256), 256)
    prod = dot_nt(own[feat, :], query_t[mine, :]) + dot_nt(theirs[feat, :], mate[pl.ds(0, 256), :])
    put_proj(out, prod, 0)
    mine = pl.ds(pl.multiple_of(MODEL + core[0] * WIDTH, WIDTH), WIDTH)
    prod = dot_nt(attn_t[...], own[mine, :]) + dot_nt(mate[pl.ds(256, WIDTH), :], theirs[mine, :])
    for y in range(ny):
        for x in range(nx):
            for z in range(nz):
                row = ((z * ny + y) * nx + x) * 8
                for low in range(nl):
                    piece = prod[row : row + 8, low * 256 : low * 256 + 256]
                    both = jnp.concatenate([piece[:, :128], piece[:, 128:]], axis=0)
                    out[(y * nx + x) * nl + low, pl.ds(z * 32 + 16, 16), :] = both.astype(BF16)


def late_terms_kernel(core, own, theirs, grads_t, mate, out):
    feat = pl.ds(0, MODEL)
    for part in range(2):
        mine = pl.ds(pl.multiple_of(part * WIDTH + core[0] * 256, 256), 256)
        prod = dot_nt(own[feat, :], grads_t[mine, :])
        prod = prod + dot_nt(theirs[feat, :], mate[mine, :])
        put_proj(out, prod, part * 16)


def feature_grad_kernel(query_t, grads_t, wq, wk, wv, out):
    total = dot_nt(query_t[...].T, wq[...])
    total = total + dot_nt(grads_t[pl.ds(0, WIDTH), :].T, wk[...])
    total = total + dot_nt(grads_t[pl.ds(WIDTH, WIDTH), :].T, wv[...])
    out[...] = total.astype(BF16)


def plane_total(got):
    total = got[0].astype(F32)
    for i in range(1, got.shape[0]):
        total = total + got[i].astype(F32)
    return total.astype(BF16)


def early_sum_kernel(got, out):
    out[...] = plane_total(got)


def plane_sum_kernel(early, got, out):
    late = plane_total(got)
    for z in range(SIZES[0]):
        out[z, pl.ds(0, 32), :] = early[pl.ds(z * 32, 32), :]
        out[z, pl.ds(32, 32), :] = late[z * 32 : z * 32 + 32]


def line_sum_kernel(factor, got, out):
    total = got[0].astype(F32)
    for z in range(1, SIZES[0]):
        total = total + got[z].astype(F32)
    out[...] = (total * factor).astype(BF16)


def place_kernel(got, proj, outs):
    _, _, _, nl, nc = SIZES
    for low in range(nl):
        for c in range(nc):
            share = got[low * nc + c].astype(F32)
            cols = pl.ds(c * 256 + low * 128, 128)
            proj[0, :, cols] = share[:16].astype(BF16)
            proj[1, :, cols] = share[32:48].astype(BF16)
            proj[2, :, cols] = share[48:].astype(BF16)
            for h in range(2):
                wide = pl.ds(c * WIDTH + low * 256 + h * 128, 128)
                outs[:, wide] = share[16 + 8 * h : 24 + 8 * h].astype(BF16)


def after(value, *others):
    return lax.optimization_barrier((value, *others))[0]


def shards(features, block_mask, expander_perm, cotangent, w_query, w_key, w_value, w_out):
    feat = features[0]
    cot = cotangent[0]
    mask = block_mask[0, 0]
    perms = expander_perm[0, 0]
    core = lax.axis_index("core").astype(jnp.int32).reshape(1)
    domains = SIZES[0] * SIZES[1] * SIZES[2]
    levels = domains.bit_length() - 1
    bits = [m * levels // EXPANDERS for m in range(EXPANDERS)]
    proj_flops = 2 * 2 * NODES * MODEL * WIDTH
    kv, kv_t, qa_t, all_t, own = call(
        project_kernel, "project",
        (shape(NODES, MODEL), shape(MODEL, NODES), shape(MODEL, NODES))
        + (shape(2 * MODEL, NODES),) * 2,
        [HERE] * 6, (feat, w_key, w_value, w_query, cot, w_out), 2 * proj_flops,
        scratch=[pltpu.VMEM(x.shape, BF16) for x in (feat, w_key, w_value, w_query, cot, w_out)]
        + [pltpu.VMEM((NODES, MODEL), BF16), pltpu.VMEM((2 * MODEL, NODES), BF16)]
        + [pltpu.VMEM((2 * MODEL, NODES), BF16)]
        + [pltpu.SemaphoreType.DMA((6, PARTS)), pltpu.SemaphoreType.DMA((11,))],
        room=60, results=HERE,
    )
    far, sent = [None] * EXPANDERS, [None] * EXPANDERS
    for m in range(EXPANDERS):
        if bits[m] >= 3:
            far[m] = swap(kv_t, DOM, bits[m])
            sent[m] = swap(qa_t, DOM, bits[m])
        else:
            far[m] = sent[m] = swap(all_t, DOM, bits[m])
    theirs = swap(own, ("core",), 0)
    qa_here = after(qa_t, theirs)
    attn_t, query_t, mate, local_t, *numbers = call(
        attend_kernel, "attend",
        (shape(WIDTH, NODES), shape(WIDTH, NODES), shape(768, NODES), shape(MODEL, NODES, dtype=F32))
        + (shape(24, NODES, dtype=F32),) * 4,
        [SMEM, SMEM, VMEM] + [HERE] * 7,
        (core, mask, perms, kv, kv_t, qa_here, *far), 4 << 30,
        scratch=[pltpu.VMEM((EXPANDERS, MODEL, NODES), BF16), pltpu.VMEM((NODES, MODEL), BF16)]
        + [pltpu.VMEM((MODEL, NODES), BF16)] * 2
        + [pltpu.VMEM((EXPANDERS, MODEL, NODES), BF16)]
        + [pltpu.VMEM((WIDTH, NODES), BF16)] * 2
        + [pltpu.VMEM((MODEL, NODES), F32)]
        + [pltpu.VMEM((24, NODES), F32)] * 4
        + [pltpu.SemaphoreType.DMA((7, 2)), pltpu.SemaphoreType.DMA((5 * HEADS + 5,))],
        room=60, results=HERE,
    )
    for m in range(EXPANDERS):
        numbers[m] = swap(numbers[m], DOM, bits[m])
    mate = swap(mate, ("core",), 0)
    early = staged(
        early_terms_kernel, "early_terms", shape(16, 256, 128),
        (own, theirs, query_t, attn_t, mate), 2 * proj_flops, scalars=(core,),
    )
    local_t = after(local_t, early)
    early = lax.all_to_all(early, PLANE, 0, 0, tiled=True)
    near = [m for m in range(EXPANDERS) if bits[m] < 3]
    line = [m for m in range(EXPANDERS) if bits[m] >= 3]
    far_rows = {1 + len(near) + i: sent[m].shape[0] - MODEL for i, m in enumerate(near)}
    local_t = staged(
        owner_kernel, "owner_near", shape(MODEL, NODES, dtype=F32),
        (local_t, *(numbers[m] for m in near), *(sent[m] for m in near)), 1 << 30, rows=far_rows,
    )
    grads_t = call(
        owner_kernel, "owner", shape(MODEL, NODES), [VMEM] * (1 + 2 * len(line)),
        (local_t, *(numbers[m] for m in line), *(sent[m] for m in line)), 30 << 30,
    )
    mate = swap(grads_t, ("core",), 0)
    late = call(
        late_terms_kernel, "late_terms", shape(16, 256, 128), [SMEM] + [VMEM] * 4,
        (core, own, theirs, grads_t, mate), 2 * proj_flops,
    )
    grads_here = after(grads_t, late)
    early = call(early_sum_kernel, "early_sum", shape(256, 128), [VMEM], (early,), 1 << 20)
    late = lax.all_to_all(late, PLANE, 0, 0, tiled=True)
    feature_grad = call(
        feature_grad_kernel, "feature_grad", shape(NODES, MODEL), [VMEM] * 5,
        (query_t, grads_here, w_query, w_key, w_value), 2 * proj_flops,
    )
    graphs = SIZES[3] * SIZES[4]
    factor = (graphs * domains * NODES) ** (-0.5)
    part = call(plane_sum_kernel, "plane_sum", shape(SIZES[0], 64, 128), [VMEM] * 2, (early, late), 1 << 20)
    part = lax.all_to_all(part, "z", 0, 0, tiled=True)
    part = call(
        functools.partial(line_sum_kernel, factor), "line_sum", shape(64, 128), [VMEM], (part,), 1 << 20
    )
    part = lax.all_gather(part, REP, axis=0, tiled=False)
    proj_grads, out_grad = call(
        place_kernel, "place", (shape(3, 16, WIDTH), shape(8, MODEL)), [VMEM], (part,), 1 << 20
    )
    return (feature_grad[None], proj_grads, out_grad)


def solution(mesh):
    fine = Mesh(mesh.devices.reshape(SIZES), DOM + REP)
    placed = (
        P(REP, DOM, None),
        P(REP, DOM, None, None),
        P(REP, DOM, None, None),
        P(REP, DOM, None),
        P(),
        P(),
        P(),
        P(),
    )
    return jax.shard_map(
        shards,
        mesh=fine,
        in_specs=placed,
        out_specs=(P(REP, DOM, None), P(None, DOM, None), P(DOM, None)),
        check_vma=False,
    )
```

```python
import functools

import jax
import jax.numpy as jnp
from jax import lax
from jax.experimental import pallas as pl
from jax.experimental.pallas import tpu as pltpu
from jax.sharding import Mesh, PartitionSpec as P

HEADS = 8
HEAD_DIM = 64
EXPANDERS = 4
NODES = 256
WIDTH = 512
MODEL = 1024
DOM = ("z", "y", "xh")
REP = ("xl", "core")
PLANE = ("y", "xh", "xl")
SIZES = (8, 4, 2, 2, 2)
F32 = jnp.float32
BF16 = jnp.bfloat16
SCALE = HEAD_DIM ** (-0.5)
VMEM = pl.BlockSpec(memory_space=pltpu.VMEM)
SMEM = pl.BlockSpec(memory_space=pltpu.SMEM)
HERE = pl.BlockSpec(memory_space=pl.ANY)


def dot(a, b):
    return jnp.dot(a, b, preferred_element_type=F32)


def dot_nt(a, b):
    return lax.dot_general(a, b, (((1,), (1,)), ((), ())), preferred_element_type=F32)


def call(body, name, outs, specs, args, flops, scratch=(), moved=2 << 20, room=16, results=VMEM):
    return pl.pallas_call(
        body,
        out_shape=outs,
        in_specs=specs,
        out_specs=jax.tree.map(lambda _: results, outs),
        scratch_shapes=scratch,
        compiler_params=pltpu.CompilerParams(vmem_limit_bytes=room << 20),
        cost_estimate=pl.CostEstimate(flops=flops if name in ("owner", "attend") else 1024, bytes_accessed=1024, transcendentals=0),
        name=name,
    )(*args)


def staged(body, name, outs, args, flops, rows=None, scalars=()):
    rows = rows or {}
    several = isinstance(outs, tuple)
    results = outs if several else (outs,)
    sizes = [(x.shape[0] - rows.get(i, 0),) + x.shape[1:] for i, x in enumerate(args)]

    def kernel(*refs):
        refs = list(refs)
        small, refs = refs[: len(scalars)], refs[len(scalars) :]
        given, refs = refs[: len(args)], refs[len(args) :]
        wanted, refs = refs[: len(results)], refs[len(results) :]
        held, refs = refs[: len(args)], refs[len(args) :]
        made, (in_sems, out_sems) = refs[: len(results)], refs[len(results) :]
        copies = []
        for i, (source, target) in enumerate(zip(given, held)):
            size = target.shape[0] // 2
            if size % 16:
                size = target.shape[0]
            for j in range(target.shape[0] // size):
                copy = pltpu.make_async_copy(
                    source.at[pl.ds(rows.get(i, 0) + j * size, size)],
                    target.at[pl.ds(j * size, size)],
                    in_sems.at[i, j],
                )
                copy.start()
                copies.append(copy)
        for copy in copies:
            copy.wait()
        body(*small, *held, *made)
        copies = []
        for i, (source, target) in enumerate(zip(made, wanted)):
            copies.append(pltpu.make_async_copy(source, target, out_sems.at[i]))
            copies[-1].start()
        for copy in copies:
            copy.wait()

    scratch = [pltpu.VMEM(size, x.dtype) for size, x in zip(sizes, args)]
    scratch += [pltpu.VMEM(x.shape, x.dtype) for x in results]
    scratch += [pltpu.SemaphoreType.DMA((len(args), 2)), pltpu.SemaphoreType.DMA((len(results),))]
    return call(
        kernel, name, outs, [SMEM] * len(scalars) + [HERE] * len(args), (*scalars, *args), flops,
        scratch=scratch, room=60, results=HERE,
    )


def shape(*dims, dtype=BF16):
    return jax.ShapeDtypeStruct(dims, dtype)


def swap(value, axes, bit):
    count = 1
    for axis in axes:
        count *= lax.axis_size(axis)
    return lax.ppermute(value, axes, [(i, i ^ 1 << bit) for i in range(count)])


PARTS = 4


def project_kernel(
    feat_h, wk_h, wv_h, wq_h, cot_h, wo_h, kv_h, kv_t_h, qa_t_h, all_h, own_h,
    feat, wk, wv, wq, cot, wo, kv, all_t, own, in_sems, out_sems,
):
    pairs = ((feat_h, feat), (wk_h, wk), (wv_h, wv), (wq_h, wq), (cot_h, cot), (wo_h, wo))
    copies = []
    for i, (source, target) in enumerate(pairs):
        size = target.shape[0] // PARTS
        copies.append([])
        for j in range(PARTS):
            rows = pl.ds(j * size, size)
            copy = pltpu.make_async_copy(source.at[rows, :], target.at[rows, :], in_sems.at[i, j])
            copy.start()
            copies[i].append(copy)
    sends = []

    def wait(i):
        for copy in copies[i]:
            copy.wait()

    def send(source, target):
        copy = pltpu.make_async_copy(source, target, out_sems.at[len(sends)])
        copy.start()
        sends.append(copy)

    keys = pl.ds(0, WIDTH)
    values = pl.ds(WIDTH, WIDTH)
    top = pl.ds(0, MODEL)
    wait(0)
    for part, span in enumerate((keys, values)):
        wait(1 + part)
        got = dot(feat[...], (wk, wv)[part][...]).astype(BF16)
        kv[:, span] = got
        all_t[span, :] = got.T
        send(all_t.at[span, :], kv_t_h.at[span, :])
        send(all_t.at[span, :], all_h.at[span, :])
    send(kv, kv_h)
    wait(3)
    span = pl.ds(MODEL, WIDTH)
    all_t[span, :] = dot(feat[...], wq[...]).astype(BF16).T
    send(all_t.at[span, :], qa_t_h.at[keys, :])
    send(all_t.at[span, :], all_h.at[span, :])
    own[top, :] = feat[...].T
    send(own.at[top, :], own_h.at[top, :])
    wait(4)
    wait(5)
    span = pl.ds(MODEL + WIDTH, WIDTH)
    all_t[span, :] = dot_nt(cot[...], wo[...]).astype(BF16).T
    send(all_t.at[span, :], qa_t_h.at[values, :])
    send(all_t.at[span, :], all_h.at[span, :])
    rest = pl.ds(MODEL, MODEL)
    own[rest, :] = cot[...].T
    send(own.at[rest, :], own_h.at[rest, :])
    for copy in sends:
        copy.wait()


def one_hot(row):
    spots = lax.broadcasted_iota(jnp.int32, (NODES, NODES), 0)
    return jnp.where(spots == row, 1.0, 0.0).astype(BF16)


def attend_kernel(
    core, mask, perms, kv_h, kv_t_h, qa_t_h, r0, r1, r2, r3,
    attn_h, query_h_t, mate_h, local_h, g0, g1, g2, g3,
    far, kv, kv_t, qa_t, far_in, attn_t, query_t, local_t, d0, d1, d2, d3, in_sems, out_sems,
):
    far_out = (d0, d1, d2, d3)
    fetched = []
    pairs = [(r, far_in.at[m]) for m, r in enumerate((r0, r1, r2, r3))]
    pairs += [(kv_h, kv), (qa_t_h, qa_t), (kv_t_h, kv_t)]
    for i, (source, target) in enumerate(pairs):
        size = target.shape[0] // 2
        fetched.append([])
        for j in range(2):
            rows = pl.ds(j * size, size)
            copy = pltpu.make_async_copy(source.at[rows, :], target.at[rows, :], in_sems.at[i, j])
            copy.start()
            fetched[i].append(copy)
    sends = []

    def send(source, target):
        copy = pltpu.make_async_copy(source, target, out_sems.at[len(sends)])
        copy.start()
        sends.append(copy)

    for m in range(EXPANDERS):
        for copy in fetched[m]:
            copy.wait()
        far[m] = dot(far_in[m], one_hot(perms[m : m + 1, :])).astype(BF16)
        far_out[m][pl.ds(16, 8), :] = jnp.broadcast_to(perms[m : m + 1, :].astype(F32), (8, NODES))
    for group in fetched[EXPANDERS:]:
        for copy in group:
            copy.wait()
    half = NODES // 2
    row_head = lax.broadcasted_iota(jnp.int32, (2 * HEAD_DIM, NODES), 0) // HEAD_DIM
    for head in range(HEADS):
        pair = pl.ds(head // 2 * 128, 128)
        pair_v = pl.ds(WIDTH + head // 2 * 128, 128)
        here = pl.ds(head * HEAD_DIM, HEAD_DIM)
        here_v = pl.ds(WIDTH + head * HEAD_DIM, HEAD_DIM)
        mine = row_head == head % 2
        zero = jnp.zeros((), BF16)
        query_h = qa_t[here, :]
        grad_h = qa_t[here_v, :]
        query_f = query_h.astype(F32)
        grad_f = grad_h.astype(F32)
        scores = dot(kv[:, pair], jnp.where(mine, qa_t[pair, :], zero)) * SCALE
        parts = []
        for source in range(2):
            row = scores[source * half : (source + 1) * half]
            keep = [
                jnp.where(mask[to, source] > 0, row[:, to * half : (to + 1) * half], -1e30)
                for to in range(2)
            ]
            parts.append(jnp.concatenate(keep, axis=1))
        scores = jnp.concatenate(parts, axis=0)
        far_s, far_dp = [], []
        for m in range(EXPANDERS):
            far_k = far[m, here, :].astype(F32)
            far_v = far[m, here_v, :].astype(F32)
            far_s.append(jnp.sum(query_f * far_k, axis=0, keepdims=True) * SCALE)
            far_dp.append(jnp.sum(grad_f * far_v, axis=0, keepdims=True))
        top = jnp.max(scores, axis=0, keepdims=True)
        for s in far_s:
            top = jnp.maximum(top, s)
        weights = jnp.exp(scores - top)
        far_w = [jnp.exp(s - top) for s in far_s]
        total = jnp.sum(weights, axis=0, keepdims=True) + (far_w[0] + far_w[1] + far_w[2] + far_w[3])
        inverse = 1.0 / total
        probs = weights * inverse
        far_p = [w * inverse for w in far_w]
        probs_b = probs.astype(BF16)
        out = dot(kv_t[here_v, :], probs_b)
        for m in range(EXPANDERS):
            out = out + far_p[m] * far[m, here_v, :].astype(F32)
        delta = jnp.sum(grad_f * out, axis=0, keepdims=True)
        out_b = out.astype(BF16)
        attn_t[here, :] = out_b
        dprob = dot(kv[:, pair_v], jnp.where(mine, qa_t[pair_v, :], zero))
        dscore_b = (probs * (dprob - delta)).astype(BF16)
        query_g = dot(kv_t[here, :], dscore_b)
        for m in range(EXPANDERS):
            dfar = far_p[m] * (far_dp[m] - delta)
            query_g = query_g + dfar * far[m, here, :].astype(F32)
            far_out[m][head : head + 1, :] = dfar * SCALE
            far_out[m][8 + head : 9 + head, :] = far_p[m]
        query_t[here, :] = (query_g * SCALE).astype(BF16)
        local_t[here, :] = dot_nt(query_h, dscore_b) * SCALE
        local_t[here_v, :] = dot_nt(grad_h, probs_b)
        send(local_t.at[here, :], local_h.at[here, :])
        send(local_t.at[here_v, :], local_h.at[here_v, :])
        send(attn_t.at[here, :], attn_h.at[here, :])
        send(attn_t.at[here, :], mate_h.at[pl.ds(256 + head * HEAD_DIM, HEAD_DIM), :])
        send(query_t.at[here, :], query_h_t.at[here, :])
    other = pl.ds(pl.multiple_of((1 - core[0]) * 256, 256), 256)
    send(query_t.at[other, :], mate_h.at[pl.ds(0, 256), :])
    for source, target in zip(far_out, (g0, g1, g2, g3)):
        send(source, target)
    for copy in sends:
        copy.wait()


def owner_kernel(start, *refs):
    *pairs, grads_t = refs
    count = len(pairs) // 2
    total = start[...]
    for numbers, sent in zip(pairs[:count], pairs[count:]):
        place = one_hot(numbers[16:17, :].astype(jnp.int32))
        rows = []
        first = sent.shape[0] - MODEL
        for part in range(2 * HEADS):
            rows.append(
                (
                    sent[pl.ds(first + part * HEAD_DIM, HEAD_DIM), :].astype(F32)
                    * numbers[part : part + 1, :]
                ).astype(BF16)
            )
        total = total + dot_nt(jnp.concatenate(rows, axis=0), place)
    grads_t[...] = total.astype(grads_t.dtype)


def put_proj(out, prod, offset):
    nz, ny, nx, nl, _ = SIZES
    for y in range(ny):
        for x in range(nx):
            for z in range(nz):
                row = ((z * ny + y) * nx + x) * 16
                for low in range(nl):
                    out[(y * nx + x) * nl + low, pl.ds(z * 32 + offset, 16), :] = prod[
                        row : row + 16, low * 128 : low * 128 + 128
                    ].astype(BF16)


def early_terms_kernel(core, own, theirs, query_t, attn_t, mate, out):
    nz, ny, nx, nl, _ = SIZES
    feat = pl.ds(0, MODEL)
    mine = pl.ds(pl.multiple_of(core[0] * 256, 256), 256)
    prod = dot_nt(own[feat, :], query_t[mine, :]) + dot_nt(theirs[feat, :], mate[pl.ds(0, 256), :])
    put_proj(out, prod, 0)
    mine = pl.ds(pl.multiple_of(MODEL + core[0] * WIDTH, WIDTH), WIDTH)
    prod = dot_nt(attn_t[...], own[mine, :]) + dot_nt(mate[pl.ds(256, WIDTH), :], theirs[mine, :])
    for y in range(ny):
        for x in range(nx):
            for z in range(nz):
                row = ((z * ny + y) * nx + x) * 8
                for low in range(nl):
                    piece = prod[row : row + 8, low * 256 : low * 256 + 256]
                    both = jnp.concatenate([piece[:, :128], piece[:, 128:]], axis=0)
                    out[(y * nx + x) * nl + low, pl.ds(z * 32 + 16, 16), :] = both.astype(BF16)


def late_terms_kernel(core, own, theirs, grads_t, mate, out):
    feat = pl.ds(0, MODEL)
    for part in range(2):
        mine = pl.ds(pl.multiple_of(part * WIDTH + core[0] * 256, 256), 256)
        prod = dot_nt(own[feat, :], grads_t[mine, :])
        prod = prod + dot_nt(theirs[feat, :], mate[mine, :])
        put_proj(out, prod, part * 16)


def feature_grad_kernel(query_t, grads_t, wq, wk, wv, out):
    total = dot_nt(query_t[...].T, wq[...])
    total = total + dot_nt(grads_t[pl.ds(0, WIDTH), :].T, wk[...])
    total = total + dot_nt(grads_t[pl.ds(WIDTH, WIDTH), :].T, wv[...])
    out[...] = total.astype(BF16)


def plane_total(got):
    total = got[0].astype(F32)
    for i in range(1, got.shape[0]):
        total = total + got[i].astype(F32)
    return total.astype(BF16)


def early_sum_kernel(got, out):
    out[...] = plane_total(got)


def plane_sum_kernel(early, got, out):
    late = plane_total(got)
    for z in range(SIZES[0]):
        out[z, pl.ds(0, 32), :] = early[pl.ds(z * 32, 32), :]
        out[z, pl.ds(32, 32), :] = late[z * 32 : z * 32 + 32]


def line_sum_kernel(factor, got, out):
    total = got[0].astype(F32)
    for z in range(1, SIZES[0]):
        total = total + got[z].astype(F32)
    out[...] = (total * factor).astype(BF16)


def place_kernel(got, proj, outs):
    _, _, _, nl, nc = SIZES
    for low in range(nl):
        for c in range(nc):
            share = got[low * nc + c].astype(F32)
            cols = pl.ds(c * 256 + low * 128, 128)
            proj[0, :, cols] = share[:16].astype(BF16)
            proj[1, :, cols] = share[32:48].astype(BF16)
            proj[2, :, cols] = share[48:].astype(BF16)
            for h in range(2):
                wide = pl.ds(c * WIDTH + low * 256 + h * 128, 128)
                outs[:, wide] = share[16 + 8 * h : 24 + 8 * h].astype(BF16)


def after(value, *others):
    return lax.optimization_barrier((value, *others))[0]


def shards(features, block_mask, expander_perm, cotangent, w_query, w_key, w_value, w_out):
    feat = features[0]
    cot = cotangent[0]
    mask = block_mask[0, 0]
    perms = expander_perm[0, 0]
    core = lax.axis_index("core").astype(jnp.int32).reshape(1)
    domains = SIZES[0] * SIZES[1] * SIZES[2]
    levels = domains.bit_length() - 1
    bits = [m * levels // EXPANDERS for m in range(EXPANDERS)]
    proj_flops = 2 * 2 * NODES * MODEL * WIDTH
    kv, kv_t, qa_t, all_t, own = call(
        project_kernel, "project",
        (shape(NODES, MODEL), shape(MODEL, NODES), shape(MODEL, NODES))
        + (shape(2 * MODEL, NODES),) * 2,
        [HERE] * 6, (feat, w_key, w_value, w_query, cot, w_out), 2 * proj_flops,
        scratch=[pltpu.VMEM(x.shape, BF16) for x in (feat, w_key, w_value, w_query, cot, w_out)]
        + [pltpu.VMEM((NODES, MODEL), BF16), pltpu.VMEM((2 * MODEL, NODES), BF16)]
        + [pltpu.VMEM((2 * MODEL, NODES), BF16)]
        + [pltpu.SemaphoreType.DMA((6, PARTS)), pltpu.SemaphoreType.DMA((11,))],
        room=60, results=HERE,
    )
    far, sent = [None] * EXPANDERS, [None] * EXPANDERS
    for m in range(EXPANDERS):
        if bits[m] >= 3:
            far[m] = swap(kv_t, DOM, bits[m])
            sent[m] = swap(qa_t, DOM, bits[m])
        else:
            far[m] = sent[m] = swap(all_t, DOM, bits[m])
    theirs = swap(own, ("core",), 0)
    qa_here = after(qa_t, theirs)
    attn_t, query_t, mate, local_t, *numbers = call(
        attend_kernel, "attend",
        (shape(WIDTH, NODES), shape(WIDTH, NODES), shape(768, NODES), shape(MODEL, NODES, dtype=F32))
        + (shape(24, NODES, dtype=F32),) * 4,
        [SMEM, SMEM, VMEM] + [HERE] * 7,
        (core, mask, perms, kv, kv_t, qa_here, *far), 4 << 30,
        scratch=[pltpu.VMEM((EXPANDERS, MODEL, NODES), BF16), pltpu.VMEM((NODES, MODEL), BF16)]
        + [pltpu.VMEM((MODEL, NODES), BF16)] * 2
        + [pltpu.VMEM((EXPANDERS, MODEL, NODES), BF16)]
        + [pltpu.VMEM((WIDTH, NODES), BF16)] * 2
        + [pltpu.VMEM((MODEL, NODES), F32)]
        + [pltpu.VMEM((24, NODES), F32)] * 4
        + [pltpu.SemaphoreType.DMA((7, 2)), pltpu.SemaphoreType.DMA((5 * HEADS + 5,))],
        room=60, results=HERE,
    )
    mate = swap(mate, ("core",), 0)
    early = staged(
        early_terms_kernel, "early_terms", shape(16, 256, 128),
        (own, theirs, query_t, attn_t, mate), 2 * proj_flops, scalars=(core,),
    )
    local_t = after(local_t, early)
    early, *numbers = lax.optimization_barrier((early, *numbers))
    for m in range(EXPANDERS):
        numbers[m] = swap(numbers[m], DOM, bits[m])
    early = lax.all_to_all(early, PLANE, 0, 0, tiled=True)
    near = [m for m in range(EXPANDERS) if bits[m] < 3]
    line = [m for m in range(EXPANDERS) if bits[m] >= 3]
    far_rows = {1 + len(near) + i: sent[m].shape[0] - MODEL for i, m in enumerate(near)}
    local_t = staged(
        owner_kernel, "owner_near", shape(MODEL, NODES, dtype=F32),
        (local_t, *(numbers[m] for m in near), *(sent[m] for m in near)), 1 << 30, rows=far_rows,
    )
    grads_t = call(
        owner_kernel, "owner", shape(MODEL, NODES), [VMEM] * (1 + 2 * len(line)),
        (local_t, *(numbers[m] for m in line), *(sent[m] for m in line)), 4 << 30,
    )
    mate = swap(grads_t, ("core",), 0)
    late = call(
        late_terms_kernel, "late_terms", shape(16, 256, 128), [SMEM] + [VMEM] * 4,
        (core, own, theirs, grads_t, mate), 2 * proj_flops,
    )
    grads_here = after(grads_t, late)
    early = call(early_sum_kernel, "early_sum", shape(256, 128), [VMEM], (early,), 1 << 20)
    late = lax.all_to_all(late, PLANE, 0, 0, tiled=True)
    feature_grad = call(
        feature_grad_kernel, "feature_grad", shape(NODES, MODEL), [VMEM] * 5,
        (query_t, grads_here, w_query, w_key, w_value), 2 * proj_flops,
    )
    graphs = SIZES[3] * SIZES[4]
    factor = (graphs * domains * NODES) ** (-0.5)
    part = call(plane_sum_kernel, "plane_sum", shape(SIZES[0], 64, 128), [VMEM] * 2, (early, late), 1 << 20)
    part = lax.all_to_all(part, "z", 0, 0, tiled=True)
    part = call(
        functools.partial(line_sum_kernel, factor), "line_sum", shape(64, 128), [VMEM], (part,), 1 << 20
    )
    part = lax.all_gather(part, REP, axis=0, tiled=False)
    proj_grads, out_grad = call(
        place_kernel, "place", (shape(3, 16, WIDTH), shape(8, MODEL)), [VMEM], (part,), 1 << 20
    )
    return (feature_grad[None], proj_grads, out_grad)


def solution(mesh):
    fine = Mesh(mesh.devices.reshape(SIZES), DOM + REP)
    placed = (
        P(REP, DOM, None),
        P(REP, DOM, None, None),
        P(REP, DOM, None, None),
        P(REP, DOM, None),
        P(),
        P(),
        P(),
        P(),
    )
    return jax.shard_map(
        shards,
        mesh=fine,
        in_specs=placed,
        out_specs=(P(REP, DOM, None), P(None, DOM, None), P(DOM, None)),
        check_vma=False,
    )
```

```python
import functools

import jax
import jax.numpy as jnp
from jax import lax
from jax.experimental import pallas as pl
from jax.experimental.pallas import tpu as pltpu
from jax.sharding import Mesh, PartitionSpec as P

HEADS = 8
HEAD_DIM = 64
EXPANDERS = 4
NODES = 256
WIDTH = 512
MODEL = 1024
DOM = ("z", "y", "xh")
REP = ("xl", "core")
PLANE = ("y", "xh", "xl")
SIZES = (8, 4, 2, 2, 2)
F32 = jnp.float32
BF16 = jnp.bfloat16
SCALE = HEAD_DIM ** (-0.5)
VMEM = pl.BlockSpec(memory_space=pltpu.VMEM)
SMEM = pl.BlockSpec(memory_space=pltpu.SMEM)
HERE = pl.BlockSpec(memory_space=pl.ANY)


def dot(a, b):
    return jnp.dot(a, b, preferred_element_type=F32)


def dot_nt(a, b):
    return lax.dot_general(a, b, (((1,), (1,)), ((), ())), preferred_element_type=F32)


def call(body, name, outs, specs, args, flops, scratch=(), moved=2 << 20, room=16, results=VMEM):
    return pl.pallas_call(
        body,
        out_shape=outs,
        in_specs=specs,
        out_specs=jax.tree.map(lambda _: results, outs),
        scratch_shapes=scratch,
        compiler_params=pltpu.CompilerParams(vmem_limit_bytes=room << 20),
        cost_estimate=pl.CostEstimate(flops=flops if name in ("owner", "attend") else 1024, bytes_accessed=1024, transcendentals=0),
        name=name,
    )(*args)


def staged(body, name, outs, args, flops, rows=None, scalars=()):
    rows = rows or {}
    several = isinstance(outs, tuple)
    results = outs if several else (outs,)
    sizes = [(x.shape[0] - rows.get(i, 0),) + x.shape[1:] for i, x in enumerate(args)]

    def kernel(*refs):
        refs = list(refs)
        small, refs = refs[: len(scalars)], refs[len(scalars) :]
        given, refs = refs[: len(args)], refs[len(args) :]
        wanted, refs = refs[: len(results)], refs[len(results) :]
        held, refs = refs[: len(args)], refs[len(args) :]
        made, (in_sems, out_sems) = refs[: len(results)], refs[len(results) :]
        copies = []
        for i, (source, target) in enumerate(zip(given, held)):
            pieces = 4 if target.shape[0] % 4 == 0 else 1
            if len(target.shape) == 2 and target.shape[0] % 64:
                pieces = 1
            size = target.shape[0] // pieces
            for j in range(pieces):
                copy = pltpu.make_async_copy(
                    source.at[pl.ds(rows.get(i, 0) + j * size, size)],
                    target.at[pl.ds(j * size, size)],
                    in_sems.at[i, j],
                )
                copy.start()
                copies.append(copy)
        for copy in copies:
            copy.wait()
        body(*small, *held, *made)
        copies = []
        for i, (source, target) in enumerate(zip(made, wanted)):
            copies.append(pltpu.make_async_copy(source, target, out_sems.at[i]))
            copies[-1].start()
        for copy in copies:
            copy.wait()

    scratch = [pltpu.VMEM(size, x.dtype) for size, x in zip(sizes, args)]
    scratch += [pltpu.VMEM(x.shape, x.dtype) for x in results]
    scratch += [pltpu.SemaphoreType.DMA((len(args), 4)), pltpu.SemaphoreType.DMA((len(results),))]
    return call(
        kernel, name, outs, [SMEM] * len(scalars) + [HERE] * len(args), (*scalars, *args), flops,
        scratch=scratch, room=60, results=HERE,
    )


def shape(*dims, dtype=BF16):
    return jax.ShapeDtypeStruct(dims, dtype)


def swap(value, axes, bit):
    count = 1
    for axis in axes:
        count *= lax.axis_size(axis)
    return lax.ppermute(value, axes, [(i, i ^ 1 << bit) for i in range(count)])


PARTS = 4


def project_kernel(
    feat_h, wk_h, wv_h, wq_h, cot_h, wo_h, kv_h, kv_t_h, qa_t_h, all_h, own_h,
    feat, wk, wv, wq, cot, wo, kv, all_t, own, in_sems, out_sems,
):
    pairs = ((feat_h, feat), (wk_h, wk), (wv_h, wv), (wq_h, wq), (cot_h, cot), (wo_h, wo))
    copies = []
    for i, (source, target) in enumerate(pairs):
        size = target.shape[0] // PARTS
        copies.append([])
        for j in range(PARTS):
            rows = pl.ds(j * size, size)
            copy = pltpu.make_async_copy(source.at[rows, :], target.at[rows, :], in_sems.at[i, j])
            copy.start()
            copies[i].append(copy)
    sends = []

    def wait(i):
        for copy in copies[i]:
            copy.wait()

    def send(source, target):
        copy = pltpu.make_async_copy(source, target, out_sems.at[len(sends)])
        copy.start()
        sends.append(copy)

    keys = pl.ds(0, WIDTH)
    values = pl.ds(WIDTH, WIDTH)
    top = pl.ds(0, MODEL)
    wait(0)
    for part, span in enumerate((keys, values)):
        wait(1 + part)
        got = dot(feat[...], (wk, wv)[part][...]).astype(BF16)
        kv[:, span] = got
        all_t[span, :] = got.T
        send(all_t.at[span, :], kv_t_h.at[span, :])
        send(all_t.at[span, :], all_h.at[span, :])
    send(kv, kv_h)
    wait(3)
    span = pl.ds(MODEL, WIDTH)
    all_t[span, :] = dot(feat[...], wq[...]).astype(BF16).T
    send(all_t.at[span, :], qa_t_h.at[keys, :])
    send(all_t.at[span, :], all_h.at[span, :])
    own[top, :] = feat[...].T
    send(own.at[top, :], own_h.at[top, :])
    wait(4)
    wait(5)
    span = pl.ds(MODEL + WIDTH, WIDTH)
    all_t[span, :] = dot_nt(cot[...], wo[...]).astype(BF16).T
    send(all_t.at[span, :], qa_t_h.at[values, :])
    send(all_t.at[span, :], all_h.at[span, :])
    rest = pl.ds(MODEL, MODEL)
    own[rest, :] = cot[...].T
    send(own.at[rest, :], own_h.at[rest, :])
    for copy in sends:
        copy.wait()


def one_hot(row):
    spots = lax.broadcasted_iota(jnp.int32, (NODES, NODES), 0)
    return jnp.where(spots == row, 1.0, 0.0).astype(BF16)


def attend_kernel(
    core, mask, perms, kv_h, kv_t_h, qa_t_h, r0, r1, r2, r3,
    attn_h, query_h_t, mate_h, local_h, g0, g1, g2, g3,
    far, kv, kv_t, qa_t, far_in, attn_t, query_t, local_t, d0, d1, d2, d3, in_sems, out_sems,
):
    far_out = (d0, d1, d2, d3)
    fetched = []
    pairs = [(r, far_in.at[m]) for m, r in enumerate((r0, r1, r2, r3))]
    pairs += [(kv_h, kv), (qa_t_h, qa_t), (kv_t_h, kv_t)]
    for i, (source, target) in enumerate(pairs):
        size = target.shape[0] // 2
        fetched.append([])
        for j in range(2):
            rows = pl.ds(j * size, size)
            copy = pltpu.make_async_copy(source.at[rows, :], target.at[rows, :], in_sems.at[i, j])
            copy.start()
            fetched[i].append(copy)
    sends = []

    def send(source, target):
        copy = pltpu.make_async_copy(source, target, out_sems.at[len(sends)])
        copy.start()
        sends.append(copy)

    for m in range(EXPANDERS):
        for copy in fetched[m]:
            copy.wait()
        far[m] = dot(far_in[m], one_hot(perms[m : m + 1, :])).astype(BF16)
        far_out[m][pl.ds(16, 8), :] = jnp.broadcast_to(perms[m : m + 1, :].astype(F32), (8, NODES))
    for group in fetched[EXPANDERS:]:
        for copy in group:
            copy.wait()
    half = NODES // 2
    row_head = lax.broadcasted_iota(jnp.int32, (2 * HEAD_DIM, NODES), 0) // HEAD_DIM
    for head in range(HEADS):
        pair = pl.ds(head // 2 * 128, 128)
        pair_v = pl.ds(WIDTH + head // 2 * 128, 128)
        here = pl.ds(head * HEAD_DIM, HEAD_DIM)
        here_v = pl.ds(WIDTH + head * HEAD_DIM, HEAD_DIM)
        mine = row_head == head % 2
        zero = jnp.zeros((), BF16)
        query_h = qa_t[here, :]
        grad_h = qa_t[here_v, :]
        query_f = query_h.astype(F32)
        grad_f = grad_h.astype(F32)
        scores = dot(kv[:, pair], jnp.where(mine, qa_t[pair, :], zero)) * SCALE
        parts = []
        for source in range(2):
            row = scores[source * half : (source + 1) * half]
            keep = [
                jnp.where(mask[to, source] > 0, row[:, to * half : (to + 1) * half], -1e30)
                for to in range(2)
            ]
            parts.append(jnp.concatenate(keep, axis=1))
        scores = jnp.concatenate(parts, axis=0)
        far_s, far_dp = [], []
        for m in range(EXPANDERS):
            far_k = far[m, here, :].astype(F32)
            far_v = far[m, here_v, :].astype(F32)
            far_s.append(jnp.sum(query_f * far_k, axis=0, keepdims=True) * SCALE)
            far_dp.append(jnp.sum(grad_f * far_v, axis=0, keepdims=True))
        top = jnp.max(scores, axis=0, keepdims=True)
        for s in far_s:
            top = jnp.maximum(top, s)
        weights = jnp.exp(scores - top)
        far_w = [jnp.exp(s - top) for s in far_s]
        total = jnp.sum(weights, axis=0, keepdims=True) + (far_w[0] + far_w[1] + far_w[2] + far_w[3])
        inverse = 1.0 / total
        probs = weights * inverse
        far_p = [w * inverse for w in far_w]
        probs_b = probs.astype(BF16)
        out = dot(kv_t[here_v, :], probs_b)
        for m in range(EXPANDERS):
            out = out + far_p[m] * far[m, here_v, :].astype(F32)
        delta = jnp.sum(grad_f * out, axis=0, keepdims=True)
        out_b = out.astype(BF16)
        attn_t[here, :] = out_b
        dprob = dot(kv[:, pair_v], jnp.where(mine, qa_t[pair_v, :], zero))
        dscore_b = (probs * (dprob - delta)).astype(BF16)
        query_g = dot(kv_t[here, :], dscore_b)
        for m in range(EXPANDERS):
            dfar = far_p[m] * (far_dp[m] - delta)
            query_g = query_g + dfar * far[m, here, :].astype(F32)
            far_out[m][head : head + 1, :] = dfar * SCALE
            far_out[m][8 + head : 9 + head, :] = far_p[m]
        query_t[here, :] = (query_g * SCALE).astype(BF16)
        local_t[here, :] = dot_nt(query_h, dscore_b) * SCALE
        local_t[here_v, :] = dot_nt(grad_h, probs_b)
        send(local_t.at[here, :], local_h.at[here, :])
        send(local_t.at[here_v, :], local_h.at[here_v, :])
        send(attn_t.at[here, :], attn_h.at[here, :])
        send(attn_t.at[here, :], mate_h.at[pl.ds(256 + head * HEAD_DIM, HEAD_DIM), :])
        send(query_t.at[here, :], query_h_t.at[here, :])
    other = pl.ds(pl.multiple_of((1 - core[0]) * 256, 256), 256)
    send(query_t.at[other, :], mate_h.at[pl.ds(0, 256), :])
    for source, target in zip(far_out, (g0, g1, g2, g3)):
        send(source, target)
    for copy in sends:
        copy.wait()


def owner_kernel(start, *refs):
    *pairs, grads_t = refs
    count = len(pairs) // 2
    total = start[...]
    for numbers, sent in zip(pairs[:count], pairs[count:]):
        place = one_hot(numbers[16:17, :].astype(jnp.int32))
        rows = []
        first = sent.shape[0] - MODEL
        for part in range(2 * HEADS):
            rows.append(
                (
                    sent[pl.ds(first + part * HEAD_DIM, HEAD_DIM), :].astype(F32)
                    * numbers[part : part + 1, :]
                ).astype(BF16)
            )
        total = total + dot_nt(jnp.concatenate(rows, axis=0), place)
    grads_t[...] = total.astype(grads_t.dtype)


def put_proj(out, prod, offset):
    nz, ny, nx, nl, _ = SIZES
    for y in range(ny):
        for x in range(nx):
            for z in range(nz):
                row = ((z * ny + y) * nx + x) * 16
                for low in range(nl):
                    out[(y * nx + x) * nl + low, pl.ds(z * 32 + offset, 16), :] = prod[
                        row : row + 16, low * 128 : low * 128 + 128
                    ].astype(BF16)


def early_terms_kernel(core, own, theirs, query_t, attn_t, mate, out):
    nz, ny, nx, nl, _ = SIZES
    feat = pl.ds(0, MODEL)
    mine = pl.ds(pl.multiple_of(core[0] * 256, 256), 256)
    prod = dot_nt(own[feat, :], query_t[mine, :]) + dot_nt(theirs[feat, :], mate[pl.ds(0, 256), :])
    put_proj(out, prod, 0)
    mine = pl.ds(pl.multiple_of(MODEL + core[0] * WIDTH, WIDTH), WIDTH)
    prod = dot_nt(attn_t[...], own[mine, :]) + dot_nt(mate[pl.ds(256, WIDTH), :], theirs[mine, :])
    for y in range(ny):
        for x in range(nx):
            for z in range(nz):
                row = ((z * ny + y) * nx + x) * 8
                for low in range(nl):
                    piece = prod[row : row + 8, low * 256 : low * 256 + 256]
                    both = jnp.concatenate([piece[:, :128], piece[:, 128:]], axis=0)
                    out[(y * nx + x) * nl + low, pl.ds(z * 32 + 16, 16), :] = both.astype(BF16)


def late_terms_kernel(core, own, theirs, grads_t, mate, out):
    feat = pl.ds(0, MODEL)
    for part in range(2):
        mine = pl.ds(pl.multiple_of(part * WIDTH + core[0] * 256, 256), 256)
        prod = dot_nt(own[feat, :], grads_t[mine, :])
        prod = prod + dot_nt(theirs[feat, :], mate[mine, :])
        put_proj(out, prod, part * 16)


def feature_grad_kernel(query_t, grads_t, wq, wk, wv, out):
    total = dot_nt(query_t[...].T, wq[...])
    total = total + dot_nt(grads_t[pl.ds(0, WIDTH), :].T, wk[...])
    total = total + dot_nt(grads_t[pl.ds(WIDTH, WIDTH), :].T, wv[...])
    out[...] = total.astype(BF16)


def plane_total(got):
    total = got[0].astype(F32)
    for i in range(1, got.shape[0]):
        total = total + got[i].astype(F32)
    return total.astype(BF16)


def early_sum_kernel(got, out):
    out[...] = plane_total(got)


def plane_sum_kernel(early, got, out):
    late = plane_total(got)
    for z in range(SIZES[0]):
        out[z, pl.ds(0, 32), :] = early[pl.ds(z * 32, 32), :]
        out[z, pl.ds(32, 32), :] = late[z * 32 : z * 32 + 32]


def line_sum_kernel(factor, got, out):
    total = got[0].astype(F32)
    for z in range(1, SIZES[0]):
        total = total + got[z].astype(F32)
    out[...] = (total * factor).astype(BF16)


def place_kernel(got, proj, outs):
    _, _, _, nl, nc = SIZES
    for low in range(nl):
        for c in range(nc):
            share = got[low * nc + c].astype(F32)
            cols = pl.ds(c * 256 + low * 128, 128)
            proj[0, :, cols] = share[:16].astype(BF16)
            proj[1, :, cols] = share[32:48].astype(BF16)
            proj[2, :, cols] = share[48:].astype(BF16)
            for h in range(2):
                wide = pl.ds(c * WIDTH + low * 256 + h * 128, 128)
                outs[:, wide] = share[16 + 8 * h : 24 + 8 * h].astype(BF16)


def after(value, *others):
    return lax.optimization_barrier((value, *others))[0]


def shards(features, block_mask, expander_perm, cotangent, w_query, w_key, w_value, w_out):
    feat = features[0]
    cot = cotangent[0]
    mask = block_mask[0, 0]
    perms = expander_perm[0, 0]
    core = lax.axis_index("core").astype(jnp.int32).reshape(1)
    domains = SIZES[0] * SIZES[1] * SIZES[2]
    levels = domains.bit_length() - 1
    bits = [m * levels // EXPANDERS for m in range(EXPANDERS)]
    proj_flops = 2 * 2 * NODES * MODEL * WIDTH
    kv, kv_t, qa_t, all_t, own = call(
        project_kernel, "project",
        (shape(NODES, MODEL), shape(MODEL, NODES), shape(MODEL, NODES))
        + (shape(2 * MODEL, NODES),) * 2,
        [HERE] * 6, (feat, w_key, w_value, w_query, cot, w_out), 2 * proj_flops,
        scratch=[pltpu.VMEM(x.shape, BF16) for x in (feat, w_key, w_value, w_query, cot, w_out)]
        + [pltpu.VMEM((NODES, MODEL), BF16), pltpu.VMEM((2 * MODEL, NODES), BF16)]
        + [pltpu.VMEM((2 * MODEL, NODES), BF16)]
        + [pltpu.SemaphoreType.DMA((6, PARTS)), pltpu.SemaphoreType.DMA((11,))],
        room=60, results=HERE,
    )
    far, sent = [None] * EXPANDERS, [None] * EXPANDERS
    for m in range(EXPANDERS):
        if bits[m] >= 3:
            far[m] = swap(kv_t, DOM, bits[m])
            sent[m] = swap(qa_t, DOM, bits[m])
        else:
            far[m] = sent[m] = swap(all_t, DOM, bits[m])
    theirs = swap(own, ("core",), 0)
    qa_here = after(qa_t, theirs)
    attn_t, query_t, mate, local_t, *numbers = call(
        attend_kernel, "attend",
        (shape(WIDTH, NODES), shape(WIDTH, NODES), shape(768, NODES), shape(MODEL, NODES, dtype=F32))
        + (shape(24, NODES, dtype=F32),) * 4,
        [SMEM, SMEM, VMEM] + [HERE] * 7,
        (core, mask, perms, kv, kv_t, qa_here, *far), 4 << 30,
        scratch=[pltpu.VMEM((EXPANDERS, MODEL, NODES), BF16), pltpu.VMEM((NODES, MODEL), BF16)]
        + [pltpu.VMEM((MODEL, NODES), BF16)] * 2
        + [pltpu.VMEM((EXPANDERS, MODEL, NODES), BF16)]
        + [pltpu.VMEM((WIDTH, NODES), BF16)] * 2
        + [pltpu.VMEM((MODEL, NODES), F32)]
        + [pltpu.VMEM((24, NODES), F32)] * 4
        + [pltpu.SemaphoreType.DMA((7, 2)), pltpu.SemaphoreType.DMA((5 * HEADS + 5,))],
        room=60, results=HERE,
    )
    for m in range(EXPANDERS):
        if bits[m] < 3:
            numbers[m] = swap(numbers[m], DOM, bits[m])
    mate = swap(mate, ("core",), 0)
    early = staged(
        early_terms_kernel, "early_terms", shape(16, 256, 128),
        (own, theirs, query_t, attn_t, mate), 2 * proj_flops, scalars=(core,),
    )
    local_t = after(local_t, early)
    late_m = [m for m in range(EXPANDERS) if bits[m] >= 3]
    early, *held = lax.optimization_barrier((early, *(numbers[m] for m in late_m)))
    for m, x in zip(late_m, held):
        numbers[m] = swap(x, DOM, bits[m])
    early = lax.all_to_all(early, PLANE, 0, 0, tiled=True)
    near = [m for m in range(EXPANDERS) if bits[m] < 3]
    line = [m for m in range(EXPANDERS) if bits[m] >= 3]
    far_rows = {1 + len(near) + i: sent[m].shape[0] - MODEL for i, m in enumerate(near)}
    local_t = staged(
        owner_kernel, "owner_near", shape(MODEL, NODES, dtype=F32),
        (local_t, *(numbers[m] for m in near), *(sent[m] for m in near)), 1 << 30, rows=far_rows,
    )
    grads_t = call(
        owner_kernel, "owner", shape(MODEL, NODES), [VMEM] * (1 + 2 * len(line)),
        (local_t, *(numbers[m] for m in line), *(sent[m] for m in line)), 30 << 30,
    )
    mate = swap(grads_t, ("core",), 0)
    late = call(
        late_terms_kernel, "late_terms", shape(16, 256, 128), [SMEM] + [VMEM] * 4,
        (core, own, theirs, grads_t, mate), 2 * proj_flops,
    )
    grads_here = after(grads_t, late)
    early = staged(early_sum_kernel, "early_sum", shape(256, 128), (early,), 1 << 20)
    late = lax.all_to_all(late, PLANE, 0, 0, tiled=True)
    feature_grad = call(
        feature_grad_kernel, "feature_grad", shape(NODES, MODEL), [VMEM] * 5,
        (query_t, grads_here, w_query, w_key, w_value), 2 * proj_flops,
    )
    graphs = SIZES[3] * SIZES[4]
    factor = (graphs * domains * NODES) ** (-0.5)
    part = staged(plane_sum_kernel, "plane_sum", shape(SIZES[0], 64, 128), (early, late), 1 << 20)
    part = lax.all_to_all(part, "z", 0, 0, tiled=True)
    part = call(
        functools.partial(line_sum_kernel, factor), "line_sum", shape(64, 128), [VMEM], (part,), 1 << 20
    )
    part = lax.all_gather(part, REP, axis=0, tiled=False)
    proj_grads, out_grad = call(
        place_kernel, "place", (shape(3, 16, WIDTH), shape(8, MODEL)), [VMEM], (part,), 1 << 20
    )
    return (feature_grad[None], proj_grads, out_grad)


def solution(mesh):
    fine = Mesh(mesh.devices.reshape(SIZES), DOM + REP)
    placed = (
        P(REP, DOM, None),
        P(REP, DOM, None, None),
        P(REP, DOM, None, None),
        P(REP, DOM, None),
        P(),
        P(),
        P(),
        P(),
    )
    return jax.shard_map(
        shards,
        mesh=fine,
        in_specs=placed,
        out_specs=(P(REP, DOM, None), P(None, DOM, None), P(DOM, None)),
        check_vma=False,
    )
```

```python
import functools

import jax
import jax.numpy as jnp
from jax import lax
from jax.experimental import pallas as pl
from jax.experimental.pallas import tpu as pltpu
from jax.sharding import Mesh, PartitionSpec as P

HEADS = 8
HEAD_DIM = 64
EXPANDERS = 4
NODES = 256
WIDTH = 512
MODEL = 1024
DOM = ("z", "y", "xh")
REP = ("xl", "core")
PLANE = ("y", "xh", "xl")
SIZES = (8, 4, 2, 2, 2)
F32 = jnp.float32
BF16 = jnp.bfloat16
SCALE = HEAD_DIM ** (-0.5)
VMEM = pl.BlockSpec(memory_space=pltpu.VMEM)
SMEM = pl.BlockSpec(memory_space=pltpu.SMEM)
HERE = pl.BlockSpec(memory_space=pl.ANY)


def dot(a, b):
    return jnp.dot(a, b, preferred_element_type=F32)


def dot_nt(a, b):
    return lax.dot_general(a, b, (((1,), (1,)), ((), ())), preferred_element_type=F32)


def call(body, name, outs, specs, args, flops, scratch=(), moved=2 << 20, room=16, results=VMEM):
    return pl.pallas_call(
        body,
        out_shape=outs,
        in_specs=specs,
        out_specs=jax.tree.map(lambda _: results, outs),
        scratch_shapes=scratch,
        compiler_params=pltpu.CompilerParams(vmem_limit_bytes=room << 20),
        cost_estimate=pl.CostEstimate(flops=flops if name in ("owner", "attend") else 1024, bytes_accessed=1024, transcendentals=0),
        name=name,
    )(*args)


def staged(body, name, outs, args, flops, rows=None, scalars=(), first=None):
    rows = rows or {}
    several = isinstance(outs, tuple)
    results = outs if several else (outs,)
    sizes = [(x.shape[0] - rows.get(i, 0),) + x.shape[1:] for i, x in enumerate(args)]

    def kernel(*refs):
        refs = list(refs)
        small, refs = refs[: len(scalars)], refs[len(scalars) :]
        given, refs = refs[: len(args)], refs[len(args) :]
        wanted, refs = refs[: len(results)], refs[len(results) :]
        held, refs = refs[: len(args)], refs[len(args) :]
        made, (in_sems, out_sems) = refs[: len(results)], refs[len(results) :]
        copies = {}
        for i, (source, target) in enumerate(zip(given, held)):
            pieces = 4 if target.shape[0] % 4 == 0 else 1
            if len(target.shape) == 2 and target.shape[0] % 64:
                pieces = 1
            size = target.shape[0] // pieces
            for j in range(pieces):
                copy = pltpu.make_async_copy(
                    source.at[pl.ds(rows.get(i, 0) + j * size, size)],
                    target.at[pl.ds(j * size, size)],
                    in_sems.at[i, j],
                )
                if first is None or (i, j) in first:
                    copy.start()
                copies[i, j] = copy
        if first is None:
            for copy in copies.values():
                copy.wait()
            body(*small, *held, *made)
        else:
            for spot in first:
                copies[spot].wait()
            for spot, copy in copies.items():
                if spot not in first:
                    copy.start()

            def rest():
                for spot, copy in copies.items():
                    if spot not in first:
                        copy.wait()

            body(rest, *small, *held, *made)
        copies = []
        for i, (source, target) in enumerate(zip(made, wanted)):
            copies.append(pltpu.make_async_copy(source, target, out_sems.at[i]))
            copies[-1].start()
        for copy in copies:
            copy.wait()

    scratch = [pltpu.VMEM(size, x.dtype) for size, x in zip(sizes, args)]
    scratch += [pltpu.VMEM(x.shape, x.dtype) for x in results]
    scratch += [pltpu.SemaphoreType.DMA((len(args), 4)), pltpu.SemaphoreType.DMA((len(results),))]
    return call(
        kernel, name, outs, [SMEM] * len(scalars) + [HERE] * len(args), (*scalars, *args), flops,
        scratch=scratch, room=60, results=HERE,
    )


def shape(*dims, dtype=BF16):
    return jax.ShapeDtypeStruct(dims, dtype)


def swap(value, axes, bit):
    count = 1
    for axis in axes:
        count *= lax.axis_size(axis)
    return lax.ppermute(value, axes, [(i, i ^ 1 << bit) for i in range(count)])


PARTS = 4


def project_kernel(
    feat_h, wk_h, wv_h, wq_h, cot_h, wo_h, kv_h, kv_t_h, qa_t_h, all_h, own_h,
    feat, wk, wv, wq, cot, wo, kv, all_t, own, in_sems, out_sems,
):
    pairs = ((feat_h, feat), (wk_h, wk), (wv_h, wv), (wq_h, wq), (cot_h, cot), (wo_h, wo))
    copies = []
    for i, (source, target) in enumerate(pairs):
        size = target.shape[0] // PARTS
        copies.append([])
        for j in range(PARTS):
            rows = pl.ds(j * size, size)
            copy = pltpu.make_async_copy(source.at[rows, :], target.at[rows, :], in_sems.at[i, j])
            copies[i].append(copy)
    sends = []

    def start(i):
        for copy in copies[i]:
            copy.start()

    def wait(i):
        for copy in copies[i]:
            copy.wait()

    def send(source, target):
        copy = pltpu.make_async_copy(source, target, out_sems.at[len(sends)])
        copy.start()
        sends.append(copy)

    keys = pl.ds(0, WIDTH)
    values = pl.ds(WIDTH, WIDTH)
    top = pl.ds(0, MODEL)
    for i in range(3):
        start(i)
    wait(0)
    for part, span in enumerate((keys, values)):
        wait(1 + part)
        if part == 0:
            for i in range(3, 6):
                start(i)
        got = dot(feat[...], (wk, wv)[part][...]).astype(BF16)
        kv[:, span] = got
        all_t[span, :] = got.T
        send(all_t.at[span, :], kv_t_h.at[span, :])
        send(all_t.at[span, :], all_h.at[span, :])
    send(kv, kv_h)
    wait(3)
    span = pl.ds(MODEL, WIDTH)
    all_t[span, :] = dot(feat[...], wq[...]).astype(BF16).T
    send(all_t.at[span, :], qa_t_h.at[keys, :])
    send(all_t.at[span, :], all_h.at[span, :])
    own[top, :] = feat[...].T
    send(own.at[top, :], own_h.at[top, :])
    wait(4)
    rest = pl.ds(MODEL, MODEL)
    own[rest, :] = cot[...].T
    send(own.at[rest, :], own_h.at[rest, :])
    wait(5)
    span = pl.ds(MODEL + WIDTH, WIDTH)
    all_t[span, :] = dot_nt(cot[...], wo[...]).astype(BF16).T
    send(all_t.at[span, :], qa_t_h.at[values, :])
    send(all_t.at[span, :], all_h.at[span, :])
    for copy in sends:
        copy.wait()


def one_hot(row):
    spots = lax.broadcasted_iota(jnp.int32, (NODES, NODES), 0)
    return jnp.where(spots == row, 1.0, 0.0).astype(BF16)


def attend_kernel(
    core, mask, perms, kv_h, kv_t_h, qa_t_h, r0, r1, r2, r3,
    attn_h, query_h_t, mate_h, local_h, g0, g1, g2, g3,
    far, kv, kv_t, qa_t, far_in, attn_t, query_t, local_t, d0, d1, d2, d3, in_sems, out_sems,
):
    far_out = (d0, d1, d2, d3)
    fetched = []
    pairs = [(r, far_in.at[m]) for m, r in enumerate((r0, r1, r2, r3))]
    pairs += [(kv_h, kv), (qa_t_h, qa_t), (kv_t_h, kv_t)]
    for i, (source, target) in enumerate(pairs):
        size = target.shape[0] // 2
        fetched.append([])
        for j in range(2):
            rows = pl.ds(j * size, size)
            copy = pltpu.make_async_copy(source.at[rows, :], target.at[rows, :], in_sems.at[i, j])
            if i < 3:
                copy.start()
            fetched[i].append(copy)
    sends = []

    def send(source, target):
        copy = pltpu.make_async_copy(source, target, out_sems.at[len(sends)])
        copy.start()
        sends.append(copy)

    for m in range(EXPANDERS):
        for copy in fetched[m]:
            copy.wait()
        if m == 0:
            for group in fetched[3:]:
                for copy in group:
                    copy.start()
        far[m] = dot(far_in[m], one_hot(perms[m : m + 1, :])).astype(BF16)
        far_out[m][pl.ds(16, 8), :] = jnp.broadcast_to(perms[m : m + 1, :].astype(F32), (8, NODES))
    for group in fetched[EXPANDERS:]:
        for copy in group:
            copy.wait()
    half = NODES // 2
    row_head = lax.broadcasted_iota(jnp.int32, (2 * HEAD_DIM, NODES), 0) // HEAD_DIM
    for head in range(HEADS):
        pair = pl.ds(head // 2 * 128, 128)
        pair_v = pl.ds(WIDTH + head // 2 * 128, 128)
        here = pl.ds(head * HEAD_DIM, HEAD_DIM)
        here_v = pl.ds(WIDTH + head * HEAD_DIM, HEAD_DIM)
        mine = row_head == head % 2
        zero = jnp.zeros((), BF16)
        query_h = qa_t[here, :]
        grad_h = qa_t[here_v, :]
        query_f = query_h.astype(F32)
        grad_f = grad_h.astype(F32)
        scores = dot(kv[:, pair], jnp.where(mine, qa_t[pair, :], zero)) * SCALE
        parts = []
        for source in range(2):
            row = scores[source * half : (source + 1) * half]
            keep = [
                jnp.where(mask[to, source] > 0, row[:, to * half : (to + 1) * half], -1e30)
                for to in range(2)
            ]
            parts.append(jnp.concatenate(keep, axis=1))
        scores = jnp.concatenate(parts, axis=0)
        far_s, far_dp = [], []
        for m in range(EXPANDERS):
            far_k = far[m, here, :].astype(F32)
            far_v = far[m, here_v, :].astype(F32)
            far_s.append(jnp.sum(query_f * far_k, axis=0, keepdims=True) * SCALE)
            far_dp.append(jnp.sum(grad_f * far_v, axis=0, keepdims=True))
        top = jnp.max(scores, axis=0, keepdims=True)
        for s in far_s:
            top = jnp.maximum(top, s)
        weights = jnp.exp(scores - top)
        far_w = [jnp.exp(s - top) for s in far_s]
        total = jnp.sum(weights, axis=0, keepdims=True) + (far_w[0] + far_w[1] + far_w[2] + far_w[3])
        inverse = 1.0 / total
        probs = weights * inverse
        far_p = [w * inverse for w in far_w]
        probs_b = probs.astype(BF16)
        out = dot(kv_t[here_v, :], probs_b)
        for m in range(EXPANDERS):
            out = out + far_p[m] * far[m, here_v, :].astype(F32)
        delta = jnp.sum(grad_f * out, axis=0, keepdims=True)
        out_b = out.astype(BF16)
        attn_t[here, :] = out_b
        dprob = dot(kv[:, pair_v], jnp.where(mine, qa_t[pair_v, :], zero))
        dscore_b = (probs * (dprob - delta)).astype(BF16)
        query_g = dot(kv_t[here, :], dscore_b)
        for m in range(EXPANDERS):
            dfar = far_p[m] * (far_dp[m] - delta)
            query_g = query_g + dfar * far[m, here, :].astype(F32)
            far_out[m][head : head + 1, :] = dfar * SCALE
            far_out[m][8 + head : 9 + head, :] = far_p[m]
        query_t[here, :] = (query_g * SCALE).astype(BF16)
        local_t[here, :] = dot_nt(query_h, dscore_b) * SCALE
        local_t[here_v, :] = dot_nt(grad_h, probs_b)
        send(local_t.at[here, :], local_h.at[here, :])
        send(local_t.at[here_v, :], local_h.at[here_v, :])
        send(attn_t.at[here, :], attn_h.at[here, :])
        send(attn_t.at[here, :], mate_h.at[pl.ds(256 + head * HEAD_DIM, HEAD_DIM), :])
        send(query_t.at[here, :], query_h_t.at[here, :])
    other = pl.ds(pl.multiple_of((1 - core[0]) * 256, 256), 256)
    send(query_t.at[other, :], mate_h.at[pl.ds(0, 256), :])
    for source, target in zip(far_out, (g0, g1, g2, g3)):
        send(source, target)
    for copy in sends:
        copy.wait()


def owner_kernel(start, *refs):
    *pairs, grads_t = refs
    count = len(pairs) // 2
    total = start[...]
    for numbers, sent in zip(pairs[:count], pairs[count:]):
        place = one_hot(numbers[16:17, :].astype(jnp.int32))
        rows = []
        first = sent.shape[0] - MODEL
        for part in range(2 * HEADS):
            rows.append(
                (
                    sent[pl.ds(first + part * HEAD_DIM, HEAD_DIM), :].astype(F32)
                    * numbers[part : part + 1, :]
                ).astype(BF16)
            )
        total = total + dot_nt(jnp.concatenate(rows, axis=0), place)
    grads_t[...] = total.astype(grads_t.dtype)


def put_proj(out, prod, offset):
    nz, ny, nx, nl, _ = SIZES
    for y in range(ny):
        for x in range(nx):
            for z in range(nz):
                row = ((z * ny + y) * nx + x) * 16
                for low in range(nl):
                    out[(y * nx + x) * nl + low, pl.ds(z * 32 + offset, 16), :] = prod[
                        row : row + 16, low * 128 : low * 128 + 128
                    ].astype(BF16)


def early_terms_kernel(rest, core, own, theirs, query_t, attn_t, mate, out):
    nz, ny, nx, nl, _ = SIZES
    feat = pl.ds(0, MODEL)
    mine = pl.ds(pl.multiple_of(core[0] * 256, 256), 256)
    prod = dot_nt(own[feat, :], query_t[mine, :]) + dot_nt(theirs[feat, :], mate[pl.ds(0, 256), :])
    put_proj(out, prod, 0)
    rest()
    mine = pl.ds(pl.multiple_of(MODEL + core[0] * WIDTH, WIDTH), WIDTH)
    prod = dot_nt(attn_t[...], own[mine, :]) + dot_nt(mate[pl.ds(256, WIDTH), :], theirs[mine, :])
    for y in range(ny):
        for x in range(nx):
            for z in range(nz):
                row = ((z * ny + y) * nx + x) * 8
                for low in range(nl):
                    piece = prod[row : row + 8, low * 256 : low * 256 + 256]
                    both = jnp.concatenate([piece[:, :128], piece[:, 128:]], axis=0)
                    out[(y * nx + x) * nl + low, pl.ds(z * 32 + 16, 16), :] = both.astype(BF16)


def late_terms_kernel(core, own, theirs, grads_t, mate, out):
    feat = pl.ds(0, MODEL)
    for part in range(2):
        mine = pl.ds(pl.multiple_of(part * WIDTH + core[0] * 256, 256), 256)
        prod = dot_nt(own[feat, :], grads_t[mine, :])
        prod = prod + dot_nt(theirs[feat, :], mate[mine, :])
        put_proj(out, prod, part * 16)


def feature_grad_kernel(query_t, grads_t, wq, wk, wv, out):
    total = dot_nt(query_t[...].T, wq[...])
    total = total + dot_nt(grads_t[pl.ds(0, WIDTH), :].T, wk[...])
    total = total + dot_nt(grads_t[pl.ds(WIDTH, WIDTH), :].T, wv[...])
    out[...] = total.astype(BF16)


def plane_total(got):
    total = got[0].astype(F32)
    for i in range(1, got.shape[0]):
        total = total + got[i].astype(F32)
    return total.astype(BF16)


def early_sum_kernel(got, out):
    out[...] = plane_total(got)


def plane_sum_kernel(rest, early, got, out):
    half = got.shape[0] // 2
    late = got[0].astype(F32)
    for i in range(1, half):
        late = late + got[i].astype(F32)
    rest()
    for i in range(half, got.shape[0]):
        late = late + got[i].astype(F32)
    late = late.astype(BF16)
    for z in range(SIZES[0]):
        out[z, pl.ds(0, 32), :] = early[pl.ds(z * 32, 32), :]
        out[z, pl.ds(32, 32), :] = late[z * 32 : z * 32 + 32]


def line_sum_kernel(factor, got, out):
    total = got[0].astype(F32)
    for z in range(1, SIZES[0]):
        total = total + got[z].astype(F32)
    out[...] = (total * factor).astype(BF16)


def place_kernel(rep, own, g1, g2, g3, proj, outs):
    nc = SIZES[4]
    for k, got in enumerate((own, g1, g2, g3)):
        spot = rep[0] ^ k
        low, c = spot // nc, spot % nc
        share = got[...]
        cols = pl.ds(pl.multiple_of(c * 256 + low * 128, 128), 128)
        proj[0, :, cols] = share[:16]
        proj[1, :, cols] = share[32:48]
        proj[2, :, cols] = share[48:]
        for h in range(2):
            wide = pl.ds(pl.multiple_of(c * WIDTH + low * 256 + h * 128, 128), 128)
            outs[:, wide] = share[16 + 8 * h : 24 + 8 * h]


def after(value, *others):
    return lax.optimization_barrier((value, *others))[0]


def shards(features, block_mask, expander_perm, cotangent, w_query, w_key, w_value, w_out):
    feat = features[0]
    cot = cotangent[0]
    mask = block_mask[0, 0]
    perms = expander_perm[0, 0]
    core = lax.axis_index("core").astype(jnp.int32).reshape(1)
    domains = SIZES[0] * SIZES[1] * SIZES[2]
    levels = domains.bit_length() - 1
    bits = [m * levels // EXPANDERS for m in range(EXPANDERS)]
    proj_flops = 2 * 2 * NODES * MODEL * WIDTH
    kv, kv_t, qa_t, all_t, own = call(
        project_kernel, "project",
        (shape(NODES, MODEL), shape(MODEL, NODES), shape(MODEL, NODES))
        + (shape(2 * MODEL, NODES),) * 2,
        [HERE] * 6, (feat, w_key, w_value, w_query, cot, w_out), 2 * proj_flops,
        scratch=[pltpu.VMEM(x.shape, BF16) for x in (feat, w_key, w_value, w_query, cot, w_out)]
        + [pltpu.VMEM((NODES, MODEL), BF16), pltpu.VMEM((2 * MODEL, NODES), BF16)]
        + [pltpu.VMEM((2 * MODEL, NODES), BF16)]
        + [pltpu.SemaphoreType.DMA((6, PARTS)), pltpu.SemaphoreType.DMA((11,))],
        room=60, results=HERE,
    )
    far, sent = [None] * EXPANDERS, [None] * EXPANDERS
    for m in range(EXPANDERS):
        if bits[m] >= 3:
            far[m] = swap(kv_t, DOM, bits[m])
            sent[m] = swap(qa_t, DOM, bits[m])
        else:
            far[m] = sent[m] = swap(all_t, DOM, bits[m])
    theirs = swap(own, ("core",), 0)
    qa_here = after(qa_t, theirs)
    attn_t, query_t, mate, local_t, *numbers = call(
        attend_kernel, "attend",
        (shape(WIDTH, NODES), shape(WIDTH, NODES), shape(768, NODES), shape(MODEL, NODES, dtype=F32))
        + (shape(24, NODES, dtype=F32),) * 4,
        [SMEM, SMEM, VMEM] + [HERE] * 7,
        (core, mask, perms, kv, kv_t, qa_here, *far), 4 << 30,
        scratch=[pltpu.VMEM((EXPANDERS, MODEL, NODES), BF16), pltpu.VMEM((NODES, MODEL), BF16)]
        + [pltpu.VMEM((MODEL, NODES), BF16)] * 2
        + [pltpu.VMEM((EXPANDERS, MODEL, NODES), BF16)]
        + [pltpu.VMEM((WIDTH, NODES), BF16)] * 2
        + [pltpu.VMEM((MODEL, NODES), F32)]
        + [pltpu.VMEM((24, NODES), F32)] * 4
        + [pltpu.SemaphoreType.DMA((7, 2)), pltpu.SemaphoreType.DMA((5 * HEADS + 5,))],
        room=60, results=HERE,
    )
    for m in range(EXPANDERS):
        if bits[m] < 3:
            numbers[m] = swap(numbers[m], DOM, bits[m])
    mate = swap(mate, ("core",), 0)
    early = staged(
        early_terms_kernel, "early_terms", shape(16, 256, 128),
        (own, theirs, query_t, attn_t, mate), 2 * proj_flops, scalars=(core,),
        first=[(0, 0), (0, 1), (1, 0), (1, 1)] + [(2, j) for j in range(4)] + [(4, j) for j in range(4)],
    )
    local_t = after(local_t, early)
    late_m = [m for m in range(EXPANDERS) if bits[m] >= 3]
    early, *held = lax.optimization_barrier((early, *(numbers[m] for m in late_m)))
    for m, x in zip(late_m, held):
        numbers[m] = swap(x, DOM, bits[m])
    early = lax.all_to_all(early, PLANE, 0, 0, tiled=True)
    near = [m for m in range(EXPANDERS) if bits[m] < 3]
    line = [m for m in range(EXPANDERS) if bits[m] >= 3]
    far_rows = {1 + len(near) + i: sent[m].shape[0] - MODEL for i, m in enumerate(near)}
    local_t = staged(
        owner_kernel, "owner_near", shape(MODEL, NODES, dtype=F32),
        (local_t, *(numbers[m] for m in near), *(sent[m] for m in near)), 1 << 30, rows=far_rows,
    )
    grads_t = call(
        owner_kernel, "owner", shape(MODEL, NODES), [VMEM] * (1 + 2 * len(line)),
        (local_t, *(numbers[m] for m in line), *(sent[m] for m in line)), 30 << 30,
    )
    mate = swap(grads_t, ("core",), 0)
    late = call(
        late_terms_kernel, "late_terms", shape(16, 256, 128), [SMEM] + [VMEM] * 4,
        (core, own, theirs, grads_t, mate), 2 * proj_flops,
    )
    grads_here = after(grads_t, late)
    early = staged(early_sum_kernel, "early_sum", shape(256, 128), (early,), 1 << 20)
    late = lax.all_to_all(late, PLANE, 0, 0, tiled=True)
    feature_grad = call(
        feature_grad_kernel, "feature_grad", shape(NODES, MODEL), [VMEM] * 5,
        (query_t, grads_here, w_query, w_key, w_value), 2 * proj_flops,
    )
    graphs = SIZES[3] * SIZES[4]
    factor = (graphs * domains * NODES) ** (-0.5)
    part = staged(plane_sum_kernel, "plane_sum", shape(SIZES[0], 64, 128), (early, late), 1 << 20,
        first=[(1, 0), (1, 1)])
    part = lax.all_to_all(part, "z", 0, 0, tiled=True)
    part = call(
        functools.partial(line_sum_kernel, factor), "line_sum", shape(64, 128), [VMEM], (part,), 1 << 20
    )
    parts = [part]
    for k in range(1, graphs):
        parts.append(lax.ppermute(part, REP, [(i, i ^ k) for i in range(graphs)]))
    rep = lax.axis_index(REP).astype(jnp.int32).reshape(1)
    proj_grads, out_grad = call(
        place_kernel, "place", (shape(3, 16, WIDTH), shape(8, MODEL)), [SMEM] + [VMEM] * 4,
        (rep, *parts), 1 << 20,
    )
    return (feature_grad[None], proj_grads, out_grad)


def solution(mesh):
    fine = Mesh(mesh.devices.reshape(SIZES), DOM + REP)
    placed = (
        P(REP, DOM, None),
        P(REP, DOM, None, None),
        P(REP, DOM, None, None),
        P(REP, DOM, None),
        P(),
        P(),
        P(),
        P(),
    )
    return jax.shard_map(
        shards,
        mesh=fine,
        in_specs=placed,
        out_specs=(P(REP, DOM, None), P(None, DOM, None), P(DOM, None)),
        check_vma=False,
    )
```

```python
import functools

import jax
import jax.numpy as jnp
from jax import lax
from jax.experimental import pallas as pl
from jax.experimental.pallas import tpu as pltpu
from jax.sharding import Mesh, PartitionSpec as P

HEADS = 8
HEAD_DIM = 64
EXPANDERS = 4
NODES = 256
WIDTH = 512
MODEL = 1024
DOM = ("z", "y", "xh")
REP = ("xl", "core")
PLANE = ("y", "xh", "xl")
SIZES = (8, 4, 2, 2, 2)
F32 = jnp.float32
BF16 = jnp.bfloat16
SCALE = HEAD_DIM ** (-0.5)
VMEM = pl.BlockSpec(memory_space=pltpu.VMEM)
SMEM = pl.BlockSpec(memory_space=pltpu.SMEM)
HERE = pl.BlockSpec(memory_space=pl.ANY)


def dot(a, b):
    return jnp.dot(a, b, preferred_element_type=F32)


def dot_nt(a, b):
    return lax.dot_general(a, b, (((1,), (1,)), ((), ())), preferred_element_type=F32)


def call(body, name, outs, specs, args, flops, scratch=(), moved=2 << 20, room=16, results=VMEM):
    return pl.pallas_call(
        body,
        out_shape=outs,
        in_specs=specs,
        out_specs=jax.tree.map(lambda _: results, outs),
        scratch_shapes=scratch,
        compiler_params=pltpu.CompilerParams(vmem_limit_bytes=room << 20),
        cost_estimate=pl.CostEstimate(flops=flops if name in ("owner", "attend") else 1024, bytes_accessed=1024, transcendentals=0),
        name=name,
    )(*args)


def staged(body, name, outs, args, flops, rows=None, scalars=()):
    rows = rows or {}
    several = isinstance(outs, tuple)
    results = outs if several else (outs,)
    sizes = [(x.shape[0] - rows.get(i, 0),) + x.shape[1:] for i, x in enumerate(args)]

    def kernel(*refs):
        refs = list(refs)
        small, refs = refs[: len(scalars)], refs[len(scalars) :]
        given, refs = refs[: len(args)], refs[len(args) :]
        wanted, refs = refs[: len(results)], refs[len(results) :]
        held, refs = refs[: len(args)], refs[len(args) :]
        made, (in_sems, out_sems) = refs[: len(results)], refs[len(results) :]
        copies = []
        for i, (source, target) in enumerate(zip(given, held)):
            pieces = 4 if target.shape[0] % 4 == 0 else 1
            if len(target.shape) == 2 and target.shape[0] % 64:
                pieces = 1
            size = target.shape[0] // pieces
            for j in range(pieces):
                copy = pltpu.make_async_copy(
                    source.at[pl.ds(rows.get(i, 0) + j * size, size)],
                    target.at[pl.ds(j * size, size)],
                    in_sems.at[i, j],
                )
                copy.start()
                copies.append(copy)
        for copy in copies:
            copy.wait()
        body(*small, *held, *made)
        copies = []
        for i, (source, target) in enumerate(zip(made, wanted)):
            copies.append(pltpu.make_async_copy(source, target, out_sems.at[i]))
            copies[-1].start()
        for copy in copies:
            copy.wait()

    scratch = [pltpu.VMEM(size, x.dtype) for size, x in zip(sizes, args)]
    scratch += [pltpu.VMEM(x.shape, x.dtype) for x in results]
    scratch += [pltpu.SemaphoreType.DMA((len(args), 4)), pltpu.SemaphoreType.DMA((len(results),))]
    return call(
        kernel, name, outs, [SMEM] * len(scalars) + [HERE] * len(args), (*scalars, *args), flops,
        scratch=scratch, room=60, results=HERE,
    )


def shape(*dims, dtype=BF16):
    return jax.ShapeDtypeStruct(dims, dtype)


def swap(value, axes, bit):
    count = 1
    for axis in axes:
        count *= lax.axis_size(axis)
    return lax.ppermute(value, axes, [(i, i ^ 1 << bit) for i in range(count)])


PARTS = 4


def project_kernel(
    feat_h, wk_h, wv_h, wq_h, cot_h, wo_h, kv_h, kv_t_h, qa_t_h, all_h, own_h,
    feat, wk, wv, wq, cot, wo, kv, all_t, own, in_sems, out_sems,
):
    pairs = ((feat_h, feat), (wk_h, wk), (wv_h, wv), (wq_h, wq), (cot_h, cot), (wo_h, wo))
    copies = []
    for i, (source, target) in enumerate(pairs):
        size = target.shape[0] // PARTS
        copies.append([])
        for j in range(PARTS):
            rows = pl.ds(j * size, size)
            copy = pltpu.make_async_copy(source.at[rows, :], target.at[rows, :], in_sems.at[i, j])
            copy.start()
            copies[i].append(copy)
    sends = []

    def wait(i):
        for copy in copies[i]:
            copy.wait()

    def send(source, target):
        copy = pltpu.make_async_copy(source, target, out_sems.at[len(sends)])
        copy.start()
        sends.append(copy)

    keys = pl.ds(0, WIDTH)
    values = pl.ds(WIDTH, WIDTH)
    top = pl.ds(0, MODEL)
    wait(0)
    for part, span in enumerate((keys, values)):
        wait(1 + part)
        got = dot(feat[...], (wk, wv)[part][...]).astype(BF16)
        kv[:, span] = got
        all_t[span, :] = got.T
        send(all_t.at[span, :], kv_t_h.at[span, :])
        send(all_t.at[span, :], all_h.at[span, :])
    send(kv, kv_h)
    wait(3)
    span = pl.ds(MODEL, WIDTH)
    all_t[span, :] = dot(feat[...], wq[...]).astype(BF16).T
    send(all_t.at[span, :], qa_t_h.at[keys, :])
    send(all_t.at[span, :], all_h.at[span, :])
    own[top, :] = feat[...].T
    send(own.at[top, :], own_h.at[top, :])
    wait(4)
    wait(5)
    span = pl.ds(MODEL + WIDTH, WIDTH)
    all_t[span, :] = dot_nt(cot[...], wo[...]).astype(BF16).T
    send(all_t.at[span, :], qa_t_h.at[values, :])
    send(all_t.at[span, :], all_h.at[span, :])
    rest = pl.ds(MODEL, MODEL)
    own[rest, :] = cot[...].T
    send(own.at[rest, :], own_h.at[rest, :])
    for copy in sends:
        copy.wait()


def one_hot(row):
    spots = lax.broadcasted_iota(jnp.int32, (NODES, NODES), 0)
    return jnp.where(spots == row, 1.0, 0.0).astype(BF16)


def attend_kernel(
    core, mask, perms, kv_h, kv_t_h, qa_t_h, r0, r1, r2, r3,
    attn_h, query_h_t, mate_h, local_h, g0, g1, g2, g3,
    far, kv, kv_t, qa_t, far_in, attn_t, query_t, local_t, d0, d1, d2, d3, in_sems, out_sems,
):
    far_out = (d0, d1, d2, d3)
    fetched = []
    pairs = [(r, far_in.at[m]) for m, r in enumerate((r0, r1, r2, r3))]
    pairs += [(kv_h, kv), (qa_t_h, qa_t), (kv_t_h, kv_t)]
    for i, (source, target) in enumerate(pairs):
        size = target.shape[0] // 2
        fetched.append([])
        for j in range(2):
            rows = pl.ds(j * size, size)
            copy = pltpu.make_async_copy(source.at[rows, :], target.at[rows, :], in_sems.at[i, j])
            copy.start()
            fetched[i].append(copy)
    sends = []

    def send(source, target):
        copy = pltpu.make_async_copy(source, target, out_sems.at[len(sends)])
        copy.start()
        sends.append(copy)

    for m in range(EXPANDERS):
        for copy in fetched[m]:
            copy.wait()
        far[m] = dot(far_in[m], one_hot(perms[m : m + 1, :])).astype(BF16)
        far_out[m][pl.ds(16, 8), :] = jnp.broadcast_to(perms[m : m + 1, :].astype(F32), (8, NODES))
    for group in fetched[EXPANDERS:]:
        for copy in group:
            copy.wait()
    half = NODES // 2
    row_head = lax.broadcasted_iota(jnp.int32, (2 * HEAD_DIM, NODES), 0) // HEAD_DIM
    for head in range(HEADS):
        pair = pl.ds(head // 2 * 128, 128)
        pair_v = pl.ds(WIDTH + head // 2 * 128, 128)
        here = pl.ds(head * HEAD_DIM, HEAD_DIM)
        here_v = pl.ds(WIDTH + head * HEAD_DIM, HEAD_DIM)
        mine = row_head == head % 2
        zero = jnp.zeros((), BF16)
        query_h = qa_t[here, :]
        grad_h = qa_t[here_v, :]
        query_f = query_h.astype(F32)
        grad_f = grad_h.astype(F32)
        scores = dot(kv[:, pair], jnp.where(mine, qa_t[pair, :], zero)) * SCALE
        parts = []
        for source in range(2):
            row = scores[source * half : (source + 1) * half]
            keep = [
                jnp.where(mask[to, source] > 0, row[:, to * half : (to + 1) * half], -1e30)
                for to in range(2)
            ]
            parts.append(jnp.concatenate(keep, axis=1))
        scores = jnp.concatenate(parts, axis=0)
        far_s, far_dp = [], []
        for m in range(EXPANDERS):
            far_k = far[m, here, :].astype(F32)
            far_v = far[m, here_v, :].astype(F32)
            far_s.append(jnp.sum(query_f * far_k, axis=0, keepdims=True) * SCALE)
            far_dp.append(jnp.sum(grad_f * far_v, axis=0, keepdims=True))
        top = jnp.max(scores, axis=0, keepdims=True)
        for s in far_s:
            top = jnp.maximum(top, s)
        weights = jnp.exp(scores - top)
        far_w = [jnp.exp(s - top) for s in far_s]
        total = jnp.sum(weights, axis=0, keepdims=True) + (far_w[0] + far_w[1] + far_w[2] + far_w[3])
        inverse = 1.0 / total
        probs = weights * inverse
        far_p = [w * inverse for w in far_w]
        probs_b = probs.astype(BF16)
        out = dot(kv_t[here_v, :], probs_b)
        for m in range(EXPANDERS):
            out = out + far_p[m] * far[m, here_v, :].astype(F32)
        delta = jnp.sum(grad_f * out, axis=0, keepdims=True)
        out_b = out.astype(BF16)
        attn_t[here, :] = out_b
        dprob = dot(kv[:, pair_v], jnp.where(mine, qa_t[pair_v, :], zero))
        dscore_b = (probs * (dprob - delta)).astype(BF16)
        query_g = dot(kv_t[here, :], dscore_b)
        for m in range(EXPANDERS):
            dfar = far_p[m] * (far_dp[m] - delta)
            query_g = query_g + dfar * far[m, here, :].astype(F32)
            far_out[m][head : head + 1, :] = dfar * SCALE
            far_out[m][8 + head : 9 + head, :] = far_p[m]
        query_t[here, :] = (query_g * SCALE).astype(BF16)
        local_t[here, :] = dot_nt(query_h, dscore_b) * SCALE
        local_t[here_v, :] = dot_nt(grad_h, probs_b)
        send(local_t.at[here, :], local_h.at[here, :])
        send(local_t.at[here_v, :], local_h.at[here_v, :])
        send(attn_t.at[here, :], attn_h.at[here, :])
        send(attn_t.at[here, :], mate_h.at[pl.ds(256 + head * HEAD_DIM, HEAD_DIM), :])
        send(query_t.at[here, :], query_h_t.at[here, :])
    other = pl.ds(pl.multiple_of((1 - core[0]) * 256, 256), 256)
    send(query_t.at[other, :], mate_h.at[pl.ds(0, 256), :])
    for source, target in zip(far_out, (g0, g1, g2, g3)):
        send(source, target)
    for copy in sends:
        copy.wait()


def owner_kernel(start, *refs):
    *pairs, grads_t = refs
    count = len(pairs) // 2
    total = start[...]
    for numbers, sent in zip(pairs[:count], pairs[count:]):
        place = one_hot(numbers[16:17, :].astype(jnp.int32))
        rows = []
        first = sent.shape[0] - MODEL
        for part in range(2 * HEADS):
            rows.append(
                (
                    sent[pl.ds(first + part * HEAD_DIM, HEAD_DIM), :].astype(F32)
                    * numbers[part : part + 1, :]
                ).astype(BF16)
            )
        total = total + dot_nt(jnp.concatenate(rows, axis=0), place)
    grads_t[...] = total.astype(grads_t.dtype)


def put_proj(out, prod, offset):
    nz, ny, nx, nl, _ = SIZES
    for y in range(ny):
        for x in range(nx):
            for z in range(nz):
                row = ((z * ny + y) * nx + x) * 16
                for low in range(nl):
                    out[(y * nx + x) * nl + low, pl.ds(z * 32 + offset, 16), :] = prod[
                        row : row + 16, low * 128 : low * 128 + 128
                    ].astype(BF16)


def early_terms_kernel(core, own, theirs, query_t, attn_t, mate, out):
    nz, ny, nx, nl, _ = SIZES
    feat = pl.ds(0, MODEL)
    mine = pl.ds(pl.multiple_of(core[0] * 256, 256), 256)
    prod = dot_nt(own[feat, :], query_t[mine, :]) + dot_nt(theirs[feat, :], mate[pl.ds(0, 256), :])
    put_proj(out, prod, 0)
    mine = pl.ds(pl.multiple_of(MODEL + core[0] * WIDTH, WIDTH), WIDTH)
    prod = dot_nt(attn_t[...], own[mine, :]) + dot_nt(mate[pl.ds(256, WIDTH), :], theirs[mine, :])
    for y in range(ny):
        for x in range(nx):
            for z in range(nz):
                row = ((z * ny + y) * nx + x) * 8
                for low in range(nl):
                    piece = prod[row : row + 8, low * 256 : low * 256 + 256]
                    both = jnp.concatenate([piece[:, :128], piece[:, 128:]], axis=0)
                    out[(y * nx + x) * nl + low, pl.ds(z * 32 + 16, 16), :] = both.astype(BF16)


def late_terms_kernel(core, own, theirs, grads_t, mate, out):
    feat = pl.ds(0, MODEL)
    for part in range(2):
        mine = pl.ds(pl.multiple_of(part * WIDTH + core[0] * 256, 256), 256)
        prod = dot_nt(own[feat, :], grads_t[mine, :])
        prod = prod + dot_nt(theirs[feat, :], mate[mine, :])
        put_proj(out, prod, part * 16)


def feature_grad_kernel(query_t, grads_t, wq, wk, wv, out):
    total = dot_nt(query_t[...].T, wq[...])
    total = total + dot_nt(grads_t[pl.ds(0, WIDTH), :].T, wk[...])
    total = total + dot_nt(grads_t[pl.ds(WIDTH, WIDTH), :].T, wv[...])
    out[...] = total.astype(BF16)


def plane_total(got):
    total = got[0].astype(F32)
    for i in range(1, got.shape[0]):
        total = total + got[i].astype(F32)
    return total.astype(BF16)


def early_sum_kernel(got, out):
    out[...] = plane_total(got)


def plane_sum_kernel(early, got, out):
    late = plane_total(got)
    for z in range(SIZES[0]):
        out[z, pl.ds(0, 32), :] = early[pl.ds(z * 32, 32), :]
        out[z, pl.ds(32, 32), :] = late[z * 32 : z * 32 + 32]


def line_sum_kernel(factor, got, out):
    total = got[0].astype(F32)
    for z in range(1, SIZES[0]):
        total = total + got[z].astype(F32)
    out[...] = (total * factor).astype(BF16)


def place_kernel(rep, own, g1, g2, g3, proj, outs):
    nc = SIZES[4]
    for k, got in enumerate((own, g1, g2, g3)):
        spot = rep[0] ^ k
        low, c = spot // nc, spot % nc
        share = got[...]
        cols = pl.ds(pl.multiple_of(c * 256 + low * 128, 128), 128)
        proj[0, :, cols] = share[:16]
        proj[1, :, cols] = share[32:48]
        proj[2, :, cols] = share[48:]
        for h in range(2):
            wide = pl.ds(pl.multiple_of(c * WIDTH + low * 256 + h * 128, 128), 128)
            outs[:, wide] = share[16 + 8 * h : 24 + 8 * h]


def after(value, *others):
    return lax.optimization_barrier((value, *others))[0]


def shards(features, block_mask, expander_perm, cotangent, w_query, w_key, w_value, w_out):
    feat = features[0]
    cot = cotangent[0]
    mask = block_mask[0, 0]
    perms = expander_perm[0, 0]
    core = lax.axis_index("core").astype(jnp.int32).reshape(1)
    domains = SIZES[0] * SIZES[1] * SIZES[2]
    levels = domains.bit_length() - 1
    bits = [m * levels // EXPANDERS for m in range(EXPANDERS)]
    proj_flops = 2 * 2 * NODES * MODEL * WIDTH
    kv, kv_t, qa_t, all_t, own = call(
        project_kernel, "project",
        (shape(NODES, MODEL), shape(MODEL, NODES), shape(MODEL, NODES))
        + (shape(2 * MODEL, NODES),) * 2,
        [HERE] * 6, (feat, w_key, w_value, w_query, cot, w_out), 2 * proj_flops,
        scratch=[pltpu.VMEM(x.shape, BF16) for x in (feat, w_key, w_value, w_query, cot, w_out)]
        + [pltpu.VMEM((NODES, MODEL), BF16), pltpu.VMEM((2 * MODEL, NODES), BF16)]
        + [pltpu.VMEM((2 * MODEL, NODES), BF16)]
        + [pltpu.SemaphoreType.DMA((6, PARTS)), pltpu.SemaphoreType.DMA((11,))],
        room=60, results=HERE,
    )
    far, sent = [None] * EXPANDERS, [None] * EXPANDERS
    for m in range(EXPANDERS):
        if bits[m] >= 3:
            far[m] = swap(kv_t, DOM, bits[m])
            sent[m] = swap(qa_t, DOM, bits[m])
        else:
            far[m] = sent[m] = swap(all_t, DOM, bits[m])
    theirs = swap(own, ("core",), 0)
    qa_here = after(qa_t, theirs)
    attn_t, query_t, mate, local_t, *numbers = call(
        attend_kernel, "attend",
        (shape(WIDTH, NODES), shape(WIDTH, NODES), shape(768, NODES), shape(MODEL, NODES, dtype=F32))
        + (shape(24, NODES, dtype=F32),) * 4,
        [SMEM, SMEM, VMEM] + [HERE] * 7,
        (core, mask, perms, kv, kv_t, qa_here, *far), 4 << 30,
        scratch=[pltpu.VMEM((EXPANDERS, MODEL, NODES), BF16), pltpu.VMEM((NODES, MODEL), BF16)]
        + [pltpu.VMEM((MODEL, NODES), BF16)] * 2
        + [pltpu.VMEM((EXPANDERS, MODEL, NODES), BF16)]
        + [pltpu.VMEM((WIDTH, NODES), BF16)] * 2
        + [pltpu.VMEM((MODEL, NODES), F32)]
        + [pltpu.VMEM((24, NODES), F32)] * 4
        + [pltpu.SemaphoreType.DMA((7, 2)), pltpu.SemaphoreType.DMA((5 * HEADS + 5,))],
        room=60, results=HERE,
    )
    for m in range(EXPANDERS):
        if bits[m] < 3:
            numbers[m] = swap(numbers[m], DOM, bits[m])
    short_m = [m for m in range(EXPANDERS) if bits[m] < 3]
    mate, *held = lax.optimization_barrier((swap(mate, ("core",), 0), *(numbers[m] for m in short_m)))
    for m, x in zip(short_m, held):
        numbers[m] = x
    early = staged(
        early_terms_kernel, "early_terms", shape(16, 256, 128),
        (own, theirs, query_t, attn_t, mate), 2 * proj_flops, scalars=(core,),
    )
    local_t = after(local_t, early)
    late_m = [m for m in range(EXPANDERS) if bits[m] >= 3]
    early, *held = lax.optimization_barrier((early, *(numbers[m] for m in late_m)))
    for m, x in zip(late_m, held):
        numbers[m] = swap(x, DOM, bits[m])
    early = lax.all_to_all(early, PLANE, 0, 0, tiled=True)
    near = [m for m in range(EXPANDERS) if bits[m] < 3]
    line = [m for m in range(EXPANDERS) if bits[m] >= 3]
    far_rows = {1 + len(near) + i: sent[m].shape[0] - MODEL for i, m in enumerate(near)}
    local_t = staged(
        owner_kernel, "owner_near", shape(MODEL, NODES, dtype=F32),
        (local_t, *(numbers[m] for m in near), *(sent[m] for m in near)), 1 << 30, rows=far_rows,
    )
    grads_t = call(
        owner_kernel, "owner", shape(MODEL, NODES), [VMEM] * (1 + 2 * len(line)),
        (local_t, *(numbers[m] for m in line), *(sent[m] for m in line)), 4 << 30,
    )
    mate = swap(grads_t, ("core",), 0)
    late = call(
        late_terms_kernel, "late_terms", shape(16, 256, 128), [SMEM] + [VMEM] * 4,
        (core, own, theirs, grads_t, mate), 2 * proj_flops,
    )
    grads_here = after(grads_t, late)
    early = staged(early_sum_kernel, "early_sum", shape(256, 128), (early,), 1 << 20)
    late = lax.all_to_all(late, PLANE, 0, 0, tiled=True)
    feature_grad = call(
        feature_grad_kernel, "feature_grad", shape(NODES, MODEL), [VMEM] * 5,
        (query_t, grads_here, w_query, w_key, w_value), 2 * proj_flops,
    )
    graphs = SIZES[3] * SIZES[4]
    factor = (graphs * domains * NODES) ** (-0.5)
    part = staged(plane_sum_kernel, "plane_sum", shape(SIZES[0], 64, 128), (early, late), 1 << 20)
    part = after(lax.all_to_all(part, "z", 0, 0, tiled=True), feature_grad)
    part = call(
        functools.partial(line_sum_kernel, factor), "line_sum", shape(64, 128), [VMEM], (part,), 1 << 20
    )
    parts = [part]
    for k in range(1, graphs):
        parts.append(lax.ppermute(part, REP, [(i, i ^ k) for i in range(graphs)]))
    rep = lax.axis_index(REP).astype(jnp.int32).reshape(1)
    proj_grads, out_grad = call(
        place_kernel, "place", (shape(3, 16, WIDTH), shape(8, MODEL)), [SMEM] + [VMEM] * 4,
        (rep, *parts), 1 << 20,
    )
    return (feature_grad[None], proj_grads, out_grad)


def solution(mesh):
    fine = Mesh(mesh.devices.reshape(SIZES), DOM + REP)
    placed = (
        P(REP, DOM, None),
        P(REP, DOM, None, None),
        P(REP, DOM, None, None),
        P(REP, DOM, None),
        P(),
        P(),
        P(),
        P(),
    )
    return jax.shard_map(
        shards,
        mesh=fine,
        in_specs=placed,
        out_specs=(P(REP, DOM, None), P(None, DOM, None), P(DOM, None)),
        check_vma=False,
    )
```

```python
import functools

import jax
import jax.numpy as jnp
from jax import lax
from jax.experimental import pallas as pl
from jax.experimental.pallas import tpu as pltpu
from jax.sharding import Mesh, PartitionSpec as P

HEADS = 8
HEAD_DIM = 64
EXPANDERS = 4
NODES = 256
WIDTH = 512
MODEL = 1024
DOM = ("z", "y", "xh")
REP = ("xl", "core")
PLANE = ("y", "xh", "xl")
SIZES = (8, 4, 2, 2, 2)
F32 = jnp.float32
BF16 = jnp.bfloat16
SCALE = HEAD_DIM ** (-0.5)
VMEM = pl.BlockSpec(memory_space=pltpu.VMEM)
SMEM = pl.BlockSpec(memory_space=pltpu.SMEM)
HERE = pl.BlockSpec(memory_space=pl.ANY)


def dot(a, b):
    return jnp.dot(a, b, preferred_element_type=F32)


def dot_nt(a, b):
    return lax.dot_general(a, b, (((1,), (1,)), ((), ())), preferred_element_type=F32)


def call(body, name, outs, specs, args, flops, scratch=(), moved=2 << 20, room=16, results=VMEM):
    return pl.pallas_call(
        body,
        out_shape=outs,
        in_specs=specs,
        out_specs=jax.tree.map(lambda _: results, outs),
        scratch_shapes=scratch,
        compiler_params=pltpu.CompilerParams(vmem_limit_bytes=room << 20),
        cost_estimate=pl.CostEstimate(flops=flops if name in ("owner", "attend") else 1024, bytes_accessed=1024, transcendentals=0),
        name=name,
    )(*args)


def staged(body, name, outs, args, flops, rows=None, scalars=()):
    rows = rows or {}
    several = isinstance(outs, tuple)
    results = outs if several else (outs,)
    sizes = [(x.shape[0] - rows.get(i, 0),) + x.shape[1:] for i, x in enumerate(args)]

    def kernel(*refs):
        refs = list(refs)
        small, refs = refs[: len(scalars)], refs[len(scalars) :]
        given, refs = refs[: len(args)], refs[len(args) :]
        wanted, refs = refs[: len(results)], refs[len(results) :]
        held, refs = refs[: len(args)], refs[len(args) :]
        made, (in_sems, out_sems) = refs[: len(results)], refs[len(results) :]
        copies = []
        for i, (source, target) in enumerate(zip(given, held)):
            pieces = 4 if target.shape[0] % 4 == 0 else 1
            if len(target.shape) == 2 and target.shape[0] % 64:
                pieces = 1
            size = target.shape[0] // pieces
            for j in range(pieces):
                copy = pltpu.make_async_copy(
                    source.at[pl.ds(rows.get(i, 0) + j * size, size)],
                    target.at[pl.ds(j * size, size)],
                    in_sems.at[i, j],
                )
                copy.start()
                copies.append(copy)
        for copy in copies:
            copy.wait()
        body(*small, *held, *made)
        copies = []
        for i, (source, target) in enumerate(zip(made, wanted)):
            copies.append(pltpu.make_async_copy(source, target, out_sems.at[i]))
            copies[-1].start()
        for copy in copies:
            copy.wait()

    scratch = [pltpu.VMEM(size, x.dtype) for size, x in zip(sizes, args)]
    scratch += [pltpu.VMEM(x.shape, x.dtype) for x in results]
    scratch += [pltpu.SemaphoreType.DMA((len(args), 4)), pltpu.SemaphoreType.DMA((len(results),))]
    return call(
        kernel, name, outs, [SMEM] * len(scalars) + [HERE] * len(args), (*scalars, *args), flops,
        scratch=scratch, room=60, results=HERE,
    )


def shape(*dims, dtype=BF16):
    return jax.ShapeDtypeStruct(dims, dtype)


def swap(value, axes, bit):
    count = 1
    for axis in axes:
        count *= lax.axis_size(axis)
    return lax.ppermute(value, axes, [(i, i ^ 1 << bit) for i in range(count)])


PARTS = 4


def project_kernel(
    feat_h, wk_h, wv_h, wq_h, cot_h, wo_h, kv_h, kv_t_h, qa_t_h, all_h, own_h,
    feat, wk, wv, wq, cot, wo, kv, all_t, own, in_sems, out_sems,
):
    pairs = ((feat_h, feat), (wk_h, wk), (wv_h, wv), (wq_h, wq), (cot_h, cot), (wo_h, wo))
    copies = []
    for i, (source, target) in enumerate(pairs):
        size = target.shape[0] // PARTS
        copies.append([])
        for j in range(PARTS):
            rows = pl.ds(j * size, size)
            copy = pltpu.make_async_copy(source.at[rows, :], target.at[rows, :], in_sems.at[i, j])
            copy.start()
            copies[i].append(copy)
    sends = []

    def wait(i):
        for copy in copies[i]:
            copy.wait()

    def send(source, target):
        copy = pltpu.make_async_copy(source, target, out_sems.at[len(sends)])
        copy.start()
        sends.append(copy)

    keys = pl.ds(0, WIDTH)
    values = pl.ds(WIDTH, WIDTH)
    top = pl.ds(0, MODEL)
    wait(0)
    for part, span in enumerate((keys, values)):
        wait(1 + part)
        got = dot(feat[...], (wk, wv)[part][...]).astype(BF16)
        kv[:, span] = got
        all_t[span, :] = got.T
        send(all_t.at[span, :], kv_t_h.at[span, :])
        send(all_t.at[span, :], all_h.at[span, :])
    send(kv, kv_h)
    wait(3)
    span = pl.ds(MODEL, WIDTH)
    all_t[span, :] = dot(feat[...], wq[...]).astype(BF16).T
    send(all_t.at[span, :], qa_t_h.at[keys, :])
    send(all_t.at[span, :], all_h.at[span, :])
    own[top, :] = feat[...].T
    send(own.at[top, :], own_h.at[top, :])
    wait(4)
    wait(5)
    span = pl.ds(MODEL + WIDTH, WIDTH)
    all_t[span, :] = dot_nt(cot[...], wo[...]).astype(BF16).T
    send(all_t.at[span, :], qa_t_h.at[values, :])
    send(all_t.at[span, :], all_h.at[span, :])
    rest = pl.ds(MODEL, MODEL)
    own[rest, :] = cot[...].T
    send(own.at[rest, :], own_h.at[rest, :])
    for copy in sends:
        copy.wait()


def one_hot(row):
    spots = lax.broadcasted_iota(jnp.int32, (NODES, NODES), 0)
    return jnp.where(spots == row, 1.0, 0.0).astype(BF16)


def attend_kernel(
    core, mask, perms, kv_h, kv_t_h, qa_t_h, r0, r1, r2, r3,
    attn_h, query_h_t, mate_h, local_h, g0, g1, g2, g3,
    far, kv, kv_t, qa_t, far_in, attn_t, query_t, local_t, d0, d1, d2, d3, in_sems, out_sems,
):
    far_out = (d0, d1, d2, d3)
    fetched = []
    pairs = [(r, far_in.at[m]) for m, r in enumerate((r0, r1, r2, r3))]
    pairs += [(kv_h, kv), (qa_t_h, qa_t), (kv_t_h, kv_t)]
    for i, (source, target) in enumerate(pairs):
        size = target.shape[0] // 2
        fetched.append([])
        for j in range(2):
            rows = pl.ds(j * size, size)
            copy = pltpu.make_async_copy(source.at[rows, :], target.at[rows, :], in_sems.at[i, j])
            copy.start()
            fetched[i].append(copy)
    sends = []

    def send(source, target):
        copy = pltpu.make_async_copy(source, target, out_sems.at[len(sends)])
        copy.start()
        sends.append(copy)

    for m in range(EXPANDERS):
        for copy in fetched[m]:
            copy.wait()
        far[m] = dot(far_in[m], one_hot(perms[m : m + 1, :])).astype(BF16)
        far_out[m][pl.ds(16, 8), :] = jnp.broadcast_to(perms[m : m + 1, :].astype(F32), (8, NODES))
    for group in fetched[EXPANDERS:]:
        for copy in group:
            copy.wait()
    half = NODES // 2
    row_head = lax.broadcasted_iota(jnp.int32, (2 * HEAD_DIM, NODES), 0) // HEAD_DIM
    for head in range(HEADS):
        pair = pl.ds(head // 2 * 128, 128)
        pair_v = pl.ds(WIDTH + head // 2 * 128, 128)
        here = pl.ds(head * HEAD_DIM, HEAD_DIM)
        here_v = pl.ds(WIDTH + head * HEAD_DIM, HEAD_DIM)
        mine = row_head == head % 2
        zero = jnp.zeros((), BF16)
        query_h = qa_t[here, :]
        grad_h = qa_t[here_v, :]
        query_f = query_h.astype(F32)
        grad_f = grad_h.astype(F32)
        scores = dot(kv[:, pair], jnp.where(mine, qa_t[pair, :], zero)) * SCALE
        parts = []
        for source in range(2):
            row = scores[source * half : (source + 1) * half]
            keep = [
                jnp.where(mask[to, source] > 0, row[:, to * half : (to + 1) * half], -1e30)
                for to in range(2)
            ]
            parts.append(jnp.concatenate(keep, axis=1))
        scores = jnp.concatenate(parts, axis=0)
        far_s, far_dp = [], []
        for m in range(EXPANDERS):
            far_k = far[m, here, :].astype(F32)
            far_v = far[m, here_v, :].astype(F32)
            far_s.append(jnp.sum(query_f * far_k, axis=0, keepdims=True) * SCALE)
            far_dp.append(jnp.sum(grad_f * far_v, axis=0, keepdims=True))
        top = jnp.max(scores, axis=0, keepdims=True)
        for s in far_s:
            top = jnp.maximum(top, s)
        weights = jnp.exp(scores - top)
        far_w = [jnp.exp(s - top) for s in far_s]
        total = jnp.sum(weights, axis=0, keepdims=True) + (far_w[0] + far_w[1] + far_w[2] + far_w[3])
        inverse = 1.0 / total
        probs = weights * inverse
        far_p = [w * inverse for w in far_w]
        probs_b = probs.astype(BF16)
        out = dot(kv_t[here_v, :], probs_b)
        for m in range(EXPANDERS):
            out = out + far_p[m] * far[m, here_v, :].astype(F32)
        delta = jnp.sum(grad_f * out, axis=0, keepdims=True)
        out_b = out.astype(BF16)
        attn_t[here, :] = out_b
        dprob = dot(kv[:, pair_v], jnp.where(mine, qa_t[pair_v, :], zero))
        dscore_b = (probs * (dprob - delta)).astype(BF16)
        query_g = dot(kv_t[here, :], dscore_b)
        for m in range(EXPANDERS):
            dfar = far_p[m] * (far_dp[m] - delta)
            query_g = query_g + dfar * far[m, here, :].astype(F32)
            far_out[m][head : head + 1, :] = dfar * SCALE
            far_out[m][8 + head : 9 + head, :] = far_p[m]
        query_t[here, :] = (query_g * SCALE).astype(BF16)
        local_t[here, :] = dot_nt(query_h, dscore_b) * SCALE
        local_t[here_v, :] = dot_nt(grad_h, probs_b)
        send(local_t.at[here, :], local_h.at[here, :])
        send(local_t.at[here_v, :], local_h.at[here_v, :])
        send(attn_t.at[here, :], attn_h.at[here, :])
        send(attn_t.at[here, :], mate_h.at[pl.ds(256 + head * HEAD_DIM, HEAD_DIM), :])
        send(query_t.at[here, :], query_h_t.at[here, :])
    other = pl.ds(pl.multiple_of((1 - core[0]) * 256, 256), 256)
    send(query_t.at[other, :], mate_h.at[pl.ds(0, 256), :])
    for source, target in zip(far_out, (g0, g1, g2, g3)):
        send(source, target)
    for copy in sends:
        copy.wait()


def owner_kernel(start, *refs):
    *pairs, grads_t = refs
    count = len(pairs) // 2
    total = start[...]
    for numbers, sent in zip(pairs[:count], pairs[count:]):
        place = one_hot(numbers[16:17, :].astype(jnp.int32))
        rows = []
        first = sent.shape[0] - MODEL
        for part in range(2 * HEADS):
            rows.append(
                (
                    sent[pl.ds(first + part * HEAD_DIM, HEAD_DIM), :].astype(F32)
                    * numbers[part : part + 1, :]
                ).astype(BF16)
            )
        total = total + dot_nt(jnp.concatenate(rows, axis=0), place)
    grads_t[...] = total.astype(grads_t.dtype)


def put_proj(out, prod, offset):
    nz, ny, nx, nl, _ = SIZES
    for y in range(ny):
        for x in range(nx):
            for z in range(nz):
                row = ((z * ny + y) * nx + x) * 16
                for low in range(nl):
                    out[(y * nx + x) * nl + low, pl.ds(z * 32 + offset, 16), :] = prod[
                        row : row + 16, low * 128 : low * 128 + 128
                    ].astype(BF16)


def early_terms_kernel(core, own, theirs, query_t, attn_t, mate, out):
    nz, ny, nx, nl, _ = SIZES
    feat = pl.ds(0, MODEL)
    mine = pl.ds(pl.multiple_of(core[0] * 256, 256), 256)
    prod = dot_nt(own[feat, :], query_t[mine, :]) + dot_nt(theirs[feat, :], mate[pl.ds(0, 256), :])
    put_proj(out, prod, 0)
    mine = pl.ds(pl.multiple_of(MODEL + core[0] * WIDTH, WIDTH), WIDTH)
    prod = dot_nt(attn_t[...], own[mine, :]) + dot_nt(mate[pl.ds(256, WIDTH), :], theirs[mine, :])
    for y in range(ny):
        for x in range(nx):
            for z in range(nz):
                row = ((z * ny + y) * nx + x) * 8
                for low in range(nl):
                    piece = prod[row : row + 8, low * 256 : low * 256 + 256]
                    both = jnp.concatenate([piece[:, :128], piece[:, 128:]], axis=0)
                    out[(y * nx + x) * nl + low, pl.ds(z * 32 + 16, 16), :] = both.astype(BF16)


def late_terms_kernel(core, own, theirs, grads_t, mate, out):
    feat = pl.ds(0, MODEL)
    for part in range(2):
        mine = pl.ds(pl.multiple_of(part * WIDTH + core[0] * 256, 256), 256)
        prod = dot_nt(own[feat, :], grads_t[mine, :])
        prod = prod + dot_nt(theirs[feat, :], mate[mine, :])
        put_proj(out, prod, part * 16)


def feature_grad_kernel(query_t, grads_t, wq, wk, wv, out):
    total = dot_nt(query_t[...].T, wq[...])
    total = total + dot_nt(grads_t[pl.ds(0, WIDTH), :].T, wk[...])
    total = total + dot_nt(grads_t[pl.ds(WIDTH, WIDTH), :].T, wv[...])
    out[...] = total.astype(BF16)


def plane_total(got):
    total = got[0].astype(F32)
    for i in range(1, got.shape[0]):
        total = total + got[i].astype(F32)
    return total.astype(BF16)


def early_sum_kernel(got, out):
    out[...] = plane_total(got)


def plane_sum_kernel(early, got, out):
    late = plane_total(got)
    for z in range(SIZES[0]):
        out[z, pl.ds(0, 32), :] = early[pl.ds(z * 32, 32), :]
        out[z, pl.ds(32, 32), :] = late[z * 32 : z * 32 + 32]


def line_sum_kernel(factor, got, out):
    total = got[0].astype(F32)
    for z in range(1, SIZES[0]):
        total = total + got[z].astype(F32)
    out[...] = (total * factor).astype(BF16)


def place_kernel(rep, own, g1, g2, g3, proj, outs):
    nc = SIZES[4]
    for k, got in enumerate((own, g1, g2, g3)):
        spot = rep[0] ^ k
        low, c = spot // nc, spot % nc
        share = got[...]
        cols = pl.ds(pl.multiple_of(c * 256 + low * 128, 128), 128)
        proj[0, :, cols] = share[:16]
        proj[1, :, cols] = share[32:48]
        proj[2, :, cols] = share[48:]
        for h in range(2):
            wide = pl.ds(pl.multiple_of(c * WIDTH + low * 256 + h * 128, 128), 128)
            outs[:, wide] = share[16 + 8 * h : 24 + 8 * h]


def after(value, *others):
    return lax.optimization_barrier((value, *others))[0]


def shards(features, block_mask, expander_perm, cotangent, w_query, w_key, w_value, w_out):
    feat = features[0]
    cot = cotangent[0]
    mask = block_mask[0, 0]
    perms = expander_perm[0, 0]
    core = lax.axis_index("core").astype(jnp.int32).reshape(1)
    domains = SIZES[0] * SIZES[1] * SIZES[2]
    levels = domains.bit_length() - 1
    bits = [m * levels // EXPANDERS for m in range(EXPANDERS)]
    proj_flops = 2 * 2 * NODES * MODEL * WIDTH
    kv, kv_t, qa_t, all_t, own = call(
        project_kernel, "project",
        (shape(NODES, MODEL), shape(MODEL, NODES), shape(MODEL, NODES))
        + (shape(2 * MODEL, NODES),) * 2,
        [HERE] * 6, (feat, w_key, w_value, w_query, cot, w_out), 2 * proj_flops,
        scratch=[pltpu.VMEM(x.shape, BF16) for x in (feat, w_key, w_value, w_query, cot, w_out)]
        + [pltpu.VMEM((NODES, MODEL), BF16), pltpu.VMEM((2 * MODEL, NODES), BF16)]
        + [pltpu.VMEM((2 * MODEL, NODES), BF16)]
        + [pltpu.SemaphoreType.DMA((6, PARTS)), pltpu.SemaphoreType.DMA((11,))],
        room=60, results=HERE,
    )
    far, sent = [None] * EXPANDERS, [None] * EXPANDERS
    for m in range(EXPANDERS):
        if bits[m] >= 3:
            far[m] = swap(kv_t, DOM, bits[m])
            sent[m] = swap(qa_t, DOM, bits[m])
        else:
            far[m] = sent[m] = swap(all_t, DOM, bits[m])
    theirs = swap(own, ("core",), 0)
    qa_here = after(qa_t, theirs)
    attn_t, query_t, mate, local_t, *numbers = call(
        attend_kernel, "attend",
        (shape(WIDTH, NODES), shape(WIDTH, NODES), shape(768, NODES), shape(MODEL, NODES, dtype=F32))
        + (shape(24, NODES, dtype=F32),) * 4,
        [SMEM, SMEM, VMEM] + [HERE] * 7,
        (core, mask, perms, kv, kv_t, qa_here, *far), 4 << 30,
        scratch=[pltpu.VMEM((EXPANDERS, MODEL, NODES), BF16), pltpu.VMEM((NODES, MODEL), BF16)]
        + [pltpu.VMEM((MODEL, NODES), BF16)] * 2
        + [pltpu.VMEM((EXPANDERS, MODEL, NODES), BF16)]
        + [pltpu.VMEM((WIDTH, NODES), BF16)] * 2
        + [pltpu.VMEM((MODEL, NODES), F32)]
        + [pltpu.VMEM((24, NODES), F32)] * 4
        + [pltpu.SemaphoreType.DMA((7, 2)), pltpu.SemaphoreType.DMA((5 * HEADS + 5,))],
        room=60, results=HERE,
    )
    for m in range(EXPANDERS):
        if bits[m] < 3:
            numbers[m] = swap(numbers[m], DOM, bits[m])
    mate = swap(mate, ("core",), 0)
    early = staged(
        early_terms_kernel, "early_terms", shape(16, 256, 128),
        (own, theirs, query_t, attn_t, mate), 2 * proj_flops, scalars=(core,),
    )
    local_t = after(local_t, early)
    late_m = [m for m in range(EXPANDERS) if bits[m] >= 3]
    early, *held = lax.optimization_barrier((early, *(numbers[m] for m in late_m)))
    for m, x in zip(late_m, held):
        numbers[m] = swap(x, DOM, bits[m])
    early = lax.all_to_all(early, PLANE, 0, 0, tiled=True)
    near = [m for m in range(EXPANDERS) if bits[m] < 3]
    line = [m for m in range(EXPANDERS) if bits[m] >= 3]
    far_rows = {1 + len(near) + i: sent[m].shape[0] - MODEL for i, m in enumerate(near)}
    local_t = staged(
        owner_kernel, "owner_near", shape(MODEL, NODES, dtype=F32),
        (local_t, *(numbers[m] for m in near), *(sent[m] for m in near)), 1 << 30, rows=far_rows,
    )
    grads_t = call(
        owner_kernel, "owner", shape(MODEL, NODES), [VMEM] * (1 + 2 * len(line)),
        (local_t, *(numbers[m] for m in line), *(sent[m] for m in line)), 30 << 30,
    )
    mate = swap(grads_t, ("core",), 0)
    late = call(
        late_terms_kernel, "late_terms", shape(16, 256, 128), [SMEM] + [VMEM] * 4,
        (core, own, theirs, grads_t, mate), 2 * proj_flops,
    )
    grads_here = after(grads_t, late)
    early = staged(early_sum_kernel, "early_sum", shape(256, 128), (early,), 1 << 20)
    late = lax.all_to_all(late, PLANE, 0, 0, tiled=True)
    feature_grad = call(
        feature_grad_kernel, "feature_grad", shape(NODES, MODEL), [VMEM] * 5,
        (query_t, grads_here, w_query, w_key, w_value), 2 * proj_flops,
    )
    graphs = SIZES[3] * SIZES[4]
    factor = (graphs * domains * NODES) ** (-0.5)
    part = staged(plane_sum_kernel, "plane_sum", shape(SIZES[0], 64, 128), (early, late), 1 << 20)
    part = after(lax.all_to_all(part, "z", 0, 0, tiled=True), feature_grad)
    part = call(
        functools.partial(line_sum_kernel, factor), "line_sum", shape(64, 128), [VMEM], (part,), 1 << 20
    )
    parts = [part]
    for k in range(1, graphs):
        parts.append(lax.ppermute(part, REP, [(i, i ^ k) for i in range(graphs)]))
    rep = lax.axis_index(REP).astype(jnp.int32).reshape(1)
    proj_grads, out_grad = call(
        place_kernel, "place", (shape(3, 16, WIDTH), shape(8, MODEL)), [SMEM] + [VMEM] * 4,
        (rep, *parts), 1 << 20,
    )
    return (feature_grad[None], proj_grads, out_grad)


def solution(mesh):
    fine = Mesh(mesh.devices.reshape(SIZES), DOM + REP)
    placed = (
        P(REP, DOM, None),
        P(REP, DOM, None, None),
        P(REP, DOM, None, None),
        P(REP, DOM, None),
        P(),
        P(),
        P(),
        P(),
    )
    return jax.shard_map(
        shards,
        mesh=fine,
        in_specs=placed,
        out_specs=(P(REP, DOM, None), P(None, DOM, None), P(DOM, None)),
        check_vma=False,
    )
```

```python
import functools

import jax
import jax.numpy as jnp
from jax import lax
from jax.experimental import pallas as pl
from jax.experimental.pallas import tpu as pltpu
from jax.sharding import Mesh, PartitionSpec as P

HEADS = 8
HEAD_DIM = 64
EXPANDERS = 4
NODES = 256
WIDTH = 512
MODEL = 1024
DOM = ("z", "y", "xh")
REP = ("xl", "core")
PLANE = ("y", "xh", "xl")
SIZES = (8, 4, 2, 2, 2)
F32 = jnp.float32
BF16 = jnp.bfloat16
SCALE = HEAD_DIM ** (-0.5)
VMEM = pl.BlockSpec(memory_space=pltpu.VMEM)
SMEM = pl.BlockSpec(memory_space=pltpu.SMEM)
HERE = pl.BlockSpec(memory_space=pl.ANY)


def dot(a, b):
    return jnp.dot(a, b, preferred_element_type=F32)


def dot_nt(a, b):
    return lax.dot_general(a, b, (((1,), (1,)), ((), ())), preferred_element_type=F32)


def call(body, name, outs, specs, args, flops, scratch=(), moved=2 << 20, room=16, results=VMEM):
    return pl.pallas_call(
        body,
        out_shape=outs,
        in_specs=specs,
        out_specs=jax.tree.map(lambda _: results, outs),
        scratch_shapes=scratch,
        compiler_params=pltpu.CompilerParams(vmem_limit_bytes=room << 20),
        cost_estimate=pl.CostEstimate(flops=flops if name == "owner" else 1024, bytes_accessed=1024, transcendentals=0),
        name=name,
    )(*args)


def staged(body, name, outs, args, flops, rows=None, scalars=()):
    rows = rows or {}
    several = isinstance(outs, tuple)
    results = outs if several else (outs,)
    sizes = [(x.shape[0] - rows.get(i, 0),) + x.shape[1:] for i, x in enumerate(args)]

    def kernel(*refs):
        refs = list(refs)
        small, refs = refs[: len(scalars)], refs[len(scalars) :]
        given, refs = refs[: len(args)], refs[len(args) :]
        wanted, refs = refs[: len(results)], refs[len(results) :]
        held, refs = refs[: len(args)], refs[len(args) :]
        made, (in_sems, out_sems) = refs[: len(results)], refs[len(results) :]
        copies = []
        for i, (source, target) in enumerate(zip(given, held)):
            pieces = 4 if target.shape[0] % 4 == 0 else 1
            if len(target.shape) == 2 and target.shape[0] % 64:
                pieces = 1
            size = target.shape[0] // pieces
            for j in range(pieces):
                copy = pltpu.make_async_copy(
                    source.at[pl.ds(rows.get(i, 0) + j * size, size)],
                    target.at[pl.ds(j * size, size)],
                    in_sems.at[i, j],
                )
                copy.start()
                copies.append(copy)
        for copy in copies:
            copy.wait()
        body(*small, *held, *made)
        copies = []
        for i, (source, target) in enumerate(zip(made, wanted)):
            copies.append(pltpu.make_async_copy(source, target, out_sems.at[i]))
            copies[-1].start()
        for copy in copies:
            copy.wait()

    scratch = [pltpu.VMEM(size, x.dtype) for size, x in zip(sizes, args)]
    scratch += [pltpu.VMEM(x.shape, x.dtype) for x in results]
    scratch += [pltpu.SemaphoreType.DMA((len(args), 4)), pltpu.SemaphoreType.DMA((len(results),))]
    return call(
        kernel, name, outs, [SMEM] * len(scalars) + [HERE] * len(args), (*scalars, *args), flops,
        scratch=scratch, room=60, results=HERE,
    )


def shape(*dims, dtype=BF16):
    return jax.ShapeDtypeStruct(dims, dtype)


def swap(value, axes, bit):
    count = 1
    for axis in axes:
        count *= lax.axis_size(axis)
    return lax.ppermute(value, axes, [(i, i ^ 1 << bit) for i in range(count)])


PARTS = 4


def project_kernel(
    feat_h, wk_h, wv_h, wq_h, cot_h, wo_h, kv_h, kv_t_h, qa_t_h, all_h, own_h,
    feat, wk, wv, wq, cot, wo, kv, all_t, own, in_sems, out_sems,
):
    pairs = ((feat_h, feat), (wk_h, wk), (wv_h, wv), (wq_h, wq), (cot_h, cot), (wo_h, wo))
    copies = []
    for i, (source, target) in enumerate(pairs):
        size = target.shape[0] // PARTS
        copies.append([])
        for j in range(PARTS):
            rows = pl.ds(j * size, size)
            copy = pltpu.make_async_copy(source.at[rows, :], target.at[rows, :], in_sems.at[i, j])
            copy.start()
            copies[i].append(copy)
    sends = []

    def wait(i):
        for copy in copies[i]:
            copy.wait()

    def send(source, target):
        copy = pltpu.make_async_copy(source, target, out_sems.at[len(sends)])
        copy.start()
        sends.append(copy)

    keys = pl.ds(0, WIDTH)
    values = pl.ds(WIDTH, WIDTH)
    top = pl.ds(0, MODEL)
    wait(0)
    for part, span in enumerate((keys, values)):
        wait(1 + part)
        got = dot(feat[...], (wk, wv)[part][...]).astype(BF16)
        kv[:, span] = got
        all_t[span, :] = got.T
        send(all_t.at[span, :], kv_t_h.at[span, :])
        send(all_t.at[span, :], all_h.at[span, :])
    send(kv, kv_h)
    wait(3)
    span = pl.ds(MODEL, WIDTH)
    all_t[span, :] = dot(feat[...], wq[...]).astype(BF16).T
    send(all_t.at[span, :], qa_t_h.at[keys, :])
    send(all_t.at[span, :], all_h.at[span, :])
    own[top, :] = feat[...].T
    send(own.at[top, :], own_h.at[top, :])
    wait(4)
    wait(5)
    span = pl.ds(MODEL + WIDTH, WIDTH)
    all_t[span, :] = dot_nt(cot[...], wo[...]).astype(BF16).T
    send(all_t.at[span, :], qa_t_h.at[values, :])
    send(all_t.at[span, :], all_h.at[span, :])
    rest = pl.ds(MODEL, MODEL)
    own[rest, :] = cot[...].T
    send(own.at[rest, :], own_h.at[rest, :])
    for copy in sends:
        copy.wait()


def one_hot(row):
    spots = lax.broadcasted_iota(jnp.int32, (NODES, NODES), 0)
    return jnp.where(spots == row, 1.0, 0.0).astype(BF16)


def attend_kernel(
    core, mask, perms, kv_h, kv_t_h, qa_t_h, r0, r1, r2, r3,
    attn_h, query_h_t, mate_h, local_h, g0, g1, g2, g3,
    far, kv, kv_t, qa_t, far_in, attn_t, query_t, local_t, d0, d1, d2, d3, in_sems, out_sems,
):
    far_out = (d0, d1, d2, d3)
    fetched = []
    pairs = [(r, far_in.at[m]) for m, r in enumerate((r0, r1, r2, r3))]
    pairs += [(kv_h, kv), (qa_t_h, qa_t), (kv_t_h, kv_t)]
    for i, (source, target) in enumerate(pairs):
        size = target.shape[0] // 2
        fetched.append([])
        for j in range(2):
            rows = pl.ds(j * size, size)
            copy = pltpu.make_async_copy(source.at[rows, :], target.at[rows, :], in_sems.at[i, j])
            copy.start()
            fetched[i].append(copy)
    sends = []

    def send(source, target):
        copy = pltpu.make_async_copy(source, target, out_sems.at[len(sends)])
        copy.start()
        sends.append(copy)

    for m in range(EXPANDERS):
        for copy in fetched[m]:
            copy.wait()
        far[m] = dot(far_in[m], one_hot(perms[m : m + 1, :])).astype(BF16)
        far_out[m][pl.ds(16, 8), :] = jnp.broadcast_to(perms[m : m + 1, :].astype(F32), (8, NODES))
    for group in fetched[EXPANDERS:]:
        for copy in group:
            copy.wait()
    half = NODES // 2
    row_head = lax.broadcasted_iota(jnp.int32, (2 * HEAD_DIM, NODES), 0) // HEAD_DIM
    for head in range(HEADS):
        pair = pl.ds(head // 2 * 128, 128)
        pair_v = pl.ds(WIDTH + head // 2 * 128, 128)
        here = pl.ds(head * HEAD_DIM, HEAD_DIM)
        here_v = pl.ds(WIDTH + head * HEAD_DIM, HEAD_DIM)
        mine = row_head == head % 2
        zero = jnp.zeros((), BF16)
        query_h = qa_t[here, :]
        grad_h = qa_t[here_v, :]
        query_f = query_h.astype(F32)
        grad_f = grad_h.astype(F32)
        scores = dot(kv[:, pair], jnp.where(mine, qa_t[pair, :], zero)) * SCALE
        parts = []
        for source in range(2):
            row = scores[source * half : (source + 1) * half]
            keep = [
                jnp.where(mask[to, source] > 0, row[:, to * half : (to + 1) * half], -1e30)
                for to in range(2)
            ]
            parts.append(jnp.concatenate(keep, axis=1))
        scores = jnp.concatenate(parts, axis=0)
        far_s, far_dp = [], []
        for m in range(EXPANDERS):
            far_k = far[m, here, :].astype(F32)
            far_v = far[m, here_v, :].astype(F32)
            far_s.append(jnp.sum(query_f * far_k, axis=0, keepdims=True) * SCALE)
            far_dp.append(jnp.sum(grad_f * far_v, axis=0, keepdims=True))
        top = jnp.max(scores, axis=0, keepdims=True)
        for s in far_s:
            top = jnp.maximum(top, s)
        weights = jnp.exp(scores - top)
        far_w = [jnp.exp(s - top) for s in far_s]
        total = jnp.sum(weights, axis=0, keepdims=True) + (far_w[0] + far_w[1] + far_w[2] + far_w[3])
        inverse = 1.0 / total
        probs = weights * inverse
        far_p = [w * inverse for w in far_w]
        probs_b = probs.astype(BF16)
        out = dot(kv_t[here_v, :], probs_b)
        for m in range(EXPANDERS):
            out = out + far_p[m] * far[m, here_v, :].astype(F32)
        delta = jnp.sum(grad_f * out, axis=0, keepdims=True)
        out_b = out.astype(BF16)
        attn_t[here, :] = out_b
        dprob = dot(kv[:, pair_v], jnp.where(mine, qa_t[pair_v, :], zero))
        dscore_b = (probs * (dprob - delta)).astype(BF16)
        query_g = dot(kv_t[here, :], dscore_b)
        for m in range(EXPANDERS):
            dfar = far_p[m] * (far_dp[m] - delta)
            query_g = query_g + dfar * far[m, here, :].astype(F32)
            far_out[m][head : head + 1, :] = dfar * SCALE
            far_out[m][8 + head : 9 + head, :] = far_p[m]
        query_t[here, :] = (query_g * SCALE).astype(BF16)
        local_t[here, :] = dot_nt(query_h, dscore_b) * SCALE
        local_t[here_v, :] = dot_nt(grad_h, probs_b)
        send(local_t.at[here, :], local_h.at[here, :])
        send(local_t.at[here_v, :], local_h.at[here_v, :])
        send(attn_t.at[here, :], attn_h.at[here, :])
        send(attn_t.at[here, :], mate_h.at[pl.ds(256 + head * HEAD_DIM, HEAD_DIM), :])
        send(query_t.at[here, :], query_h_t.at[here, :])
    other = pl.ds(pl.multiple_of((1 - core[0]) * 256, 256), 256)
    send(query_t.at[other, :], mate_h.at[pl.ds(0, 256), :])
    for source, target in zip(far_out, (g0, g1, g2, g3)):
        send(source, target)
    for copy in sends:
        copy.wait()


def owner_kernel(start, *refs):
    *pairs, grads_t = refs
    count = len(pairs) // 2
    total = start[...]
    for numbers, sent in zip(pairs[:count], pairs[count:]):
        place = one_hot(numbers[16:17, :].astype(jnp.int32))
        rows = []
        first = sent.shape[0] - MODEL
        for part in range(2 * HEADS):
            rows.append(
                (
                    sent[pl.ds(first + part * HEAD_DIM, HEAD_DIM), :].astype(F32)
                    * numbers[part : part + 1, :]
                ).astype(BF16)
            )
        total = total + dot_nt(jnp.concatenate(rows, axis=0), place)
    grads_t[...] = total.astype(grads_t.dtype)


def put_proj(out, prod, offset):
    nz, ny, nx, nl, _ = SIZES
    for y in range(ny):
        for x in range(nx):
            for z in range(nz):
                row = ((z * ny + y) * nx + x) * 16
                for low in range(nl):
                    out[(y * nx + x) * nl + low, pl.ds(z * 32 + offset, 16), :] = prod[
                        row : row + 16, low * 128 : low * 128 + 128
                    ].astype(BF16)


def early_terms_kernel(core, own, theirs, query_t, attn_t, mate, out):
    nz, ny, nx, nl, _ = SIZES
    feat = pl.ds(0, MODEL)
    mine = pl.ds(pl.multiple_of(core[0] * 256, 256), 256)
    prod = dot_nt(own[feat, :], query_t[mine, :]) + dot_nt(theirs[feat, :], mate[pl.ds(0, 256), :])
    put_proj(out, prod, 0)
    mine = pl.ds(pl.multiple_of(MODEL + core[0] * WIDTH, WIDTH), WIDTH)
    prod = dot_nt(attn_t[...], own[mine, :]) + dot_nt(mate[pl.ds(256, WIDTH), :], theirs[mine, :])
    for y in range(ny):
        for x in range(nx):
            for z in range(nz):
                row = ((z * ny + y) * nx + x) * 8
                for low in range(nl):
                    piece = prod[row : row + 8, low * 256 : low * 256 + 256]
                    both = jnp.concatenate([piece[:, :128], piece[:, 128:]], axis=0)
                    out[(y * nx + x) * nl + low, pl.ds(z * 32 + 16, 16), :] = both.astype(BF16)


def late_terms_kernel(core, own, theirs, grads_t, mate, out):
    feat = pl.ds(0, MODEL)
    for part in range(2):
        mine = pl.ds(pl.multiple_of(part * WIDTH + core[0] * 256, 256), 256)
        prod = dot_nt(own[feat, :], grads_t[mine, :])
        prod = prod + dot_nt(theirs[feat, :], mate[mine, :])
        put_proj(out, prod, part * 16)


def feature_grad_kernel(query_t, grads_t, wq, wk, wv, out):
    total = dot_nt(query_t[...].T, wq[...])
    total = total + dot_nt(grads_t[pl.ds(0, WIDTH), :].T, wk[...])
    total = total + dot_nt(grads_t[pl.ds(WIDTH, WIDTH), :].T, wv[...])
    out[...] = total.astype(BF16)


def plane_total(got):
    total = got[0].astype(F32)
    for i in range(1, got.shape[0]):
        total = total + got[i].astype(F32)
    return total.astype(BF16)


def early_sum_kernel(got, out):
    out[...] = plane_total(got)


def plane_sum_kernel(early, got, out):
    late = plane_total(got)
    for z in range(SIZES[0]):
        out[z, pl.ds(0, 32), :] = early[pl.ds(z * 32, 32), :]
        out[z, pl.ds(32, 32), :] = late[z * 32 : z * 32 + 32]


def line_sum_kernel(factor, got, out):
    total = got[0].astype(F32)
    for z in range(1, SIZES[0]):
        total = total + got[z].astype(F32)
    out[...] = (total * factor).astype(BF16)


def place_kernel(rep, own, g1, g2, g3, proj, outs):
    nc = SIZES[4]
    for k, got in enumerate((own, g1, g2, g3)):
        spot = rep[0] ^ k
        low, c = spot // nc, spot % nc
        share = got[...]
        cols = pl.ds(pl.multiple_of(c * 256 + low * 128, 128), 128)
        proj[0, :, cols] = share[:16]
        proj[1, :, cols] = share[32:48]
        proj[2, :, cols] = share[48:]
        for h in range(2):
            wide = pl.ds(pl.multiple_of(c * WIDTH + low * 256 + h * 128, 128), 128)
            outs[:, wide] = share[16 + 8 * h : 24 + 8 * h]


def after(value, *others):
    return lax.optimization_barrier((value, *others))[0]


def shards(features, block_mask, expander_perm, cotangent, w_query, w_key, w_value, w_out):
    feat = features[0]
    cot = cotangent[0]
    mask = block_mask[0, 0]
    perms = expander_perm[0, 0]
    core = lax.axis_index("core").astype(jnp.int32).reshape(1)
    domains = SIZES[0] * SIZES[1] * SIZES[2]
    levels = domains.bit_length() - 1
    bits = [m * levels // EXPANDERS for m in range(EXPANDERS)]
    proj_flops = 2 * 2 * NODES * MODEL * WIDTH
    kv, kv_t, qa_t, all_t, own = call(
        project_kernel, "project",
        (shape(NODES, MODEL), shape(MODEL, NODES), shape(MODEL, NODES))
        + (shape(2 * MODEL, NODES),) * 2,
        [HERE] * 6, (feat, w_key, w_value, w_query, cot, w_out), 2 * proj_flops,
        scratch=[pltpu.VMEM(x.shape, BF16) for x in (feat, w_key, w_value, w_query, cot, w_out)]
        + [pltpu.VMEM((NODES, MODEL), BF16), pltpu.VMEM((2 * MODEL, NODES), BF16)]
        + [pltpu.VMEM((2 * MODEL, NODES), BF16)]
        + [pltpu.SemaphoreType.DMA((6, PARTS)), pltpu.SemaphoreType.DMA((11,))],
        room=60, results=HERE,
    )
    far, sent = [None] * EXPANDERS, [None] * EXPANDERS
    for m in range(EXPANDERS):
        if bits[m] >= 3:
            far[m] = swap(kv_t, DOM, bits[m])
            sent[m] = swap(qa_t, DOM, bits[m])
        else:
            far[m] = sent[m] = swap(all_t, DOM, bits[m])
    theirs = swap(own, ("core",), 0)
    qa_here = after(qa_t, theirs)
    attn_t, query_t, mate, local_t, *numbers = call(
        attend_kernel, "attend",
        (shape(WIDTH, NODES), shape(WIDTH, NODES), shape(768, NODES), shape(MODEL, NODES, dtype=F32))
        + (shape(24, NODES, dtype=F32),) * 4,
        [SMEM, SMEM, VMEM] + [HERE] * 7,
        (core, mask, perms, kv, kv_t, qa_here, *far), 4 << 30,
        scratch=[pltpu.VMEM((EXPANDERS, MODEL, NODES), BF16), pltpu.VMEM((NODES, MODEL), BF16)]
        + [pltpu.VMEM((MODEL, NODES), BF16)] * 2
        + [pltpu.VMEM((EXPANDERS, MODEL, NODES), BF16)]
        + [pltpu.VMEM((WIDTH, NODES), BF16)] * 2
        + [pltpu.VMEM((MODEL, NODES), F32)]
        + [pltpu.VMEM((24, NODES), F32)] * 4
        + [pltpu.SemaphoreType.DMA((7, 2)), pltpu.SemaphoreType.DMA((5 * HEADS + 5,))],
        room=60, results=HERE,
    )
    for m in range(EXPANDERS):
        if bits[m] < 3:
            numbers[m] = swap(numbers[m], DOM, bits[m])
    mate = swap(mate, ("core",), 0)
    early = staged(
        early_terms_kernel, "early_terms", shape(16, 256, 128),
        (own, theirs, query_t, attn_t, mate), 2 * proj_flops, scalars=(core,),
    )
    local_t = after(local_t, early)
    late_m = [m for m in range(EXPANDERS) if bits[m] >= 3]
    early, *held = lax.optimization_barrier((early, *(numbers[m] for m in late_m)))
    for m, x in zip(late_m, held):
        numbers[m] = swap(x, DOM, bits[m])
    early = lax.all_to_all(early, PLANE, 0, 0, tiled=True)
    near = [m for m in range(EXPANDERS) if bits[m] < 3]
    line = [m for m in range(EXPANDERS) if bits[m] >= 3]
    far_rows = {1 + len(near) + i: sent[m].shape[0] - MODEL for i, m in enumerate(near)}
    local_t = staged(
        owner_kernel, "owner_near", shape(MODEL, NODES, dtype=F32),
        (local_t, *(numbers[m] for m in near), *(sent[m] for m in near)), 1 << 30, rows=far_rows,
    )
    grads_t = call(
        owner_kernel, "owner", shape(MODEL, NODES), [VMEM] * (1 + 2 * len(line)),
        (local_t, *(numbers[m] for m in line), *(sent[m] for m in line)), 30 << 30,
    )
    mate = swap(grads_t, ("core",), 0)
    late = call(
        late_terms_kernel, "late_terms", shape(16, 256, 128), [SMEM] + [VMEM] * 4,
        (core, own, theirs, grads_t, mate), 2 * proj_flops,
    )
    grads_here = after(grads_t, late)
    early = staged(early_sum_kernel, "early_sum", shape(256, 128), (early,), 1 << 20)
    late = lax.all_to_all(late, PLANE, 0, 0, tiled=True)
    feature_grad = call(
        feature_grad_kernel, "feature_grad", shape(NODES, MODEL), [VMEM] * 5,
        (query_t, grads_here, w_query, w_key, w_value), 2 * proj_flops,
    )
    graphs = SIZES[3] * SIZES[4]
    factor = (graphs * domains * NODES) ** (-0.5)
    part = staged(plane_sum_kernel, "plane_sum", shape(SIZES[0], 64, 128), (early, late), 1 << 20)
    part = after(lax.all_to_all(part, "z", 0, 0, tiled=True), feature_grad)
    part = call(
        functools.partial(line_sum_kernel, factor), "line_sum", shape(64, 128), [VMEM], (part,), 1 << 20
    )
    parts = [part]
    for k in range(1, graphs):
        parts.append(lax.ppermute(part, REP, [(i, i ^ k) for i in range(graphs)]))
    rep = lax.axis_index(REP).astype(jnp.int32).reshape(1)
    proj_grads, out_grad = call(
        place_kernel, "place", (shape(3, 16, WIDTH), shape(8, MODEL)), [SMEM] + [VMEM] * 4,
        (rep, *parts), 1 << 20,
    )
    return (feature_grad[None], proj_grads, out_grad)


def solution(mesh):
    fine = Mesh(mesh.devices.reshape(SIZES), DOM + REP)
    placed = (
        P(REP, DOM, None),
        P(REP, DOM, None, None),
        P(REP, DOM, None, None),
        P(REP, DOM, None),
        P(),
        P(),
        P(),
        P(),
    )
    return jax.shard_map(
        shards,
        mesh=fine,
        in_specs=placed,
        out_specs=(P(REP, DOM, None), P(None, DOM, None), P(DOM, None)),
        check_vma=False,
    )
```
